32 devices in a mesh: dp: 2 (over core), expert: 16 (over z, y, x).
Axes of the slice: x: 2, y: 2, z: 4, core: 2. Of those that a mesh axis runs over, the one named last changes fastest.
Arguments:
- tokens: bfloat16 [2048, 2048], P('expert'), may hold values from -6 to 6
- out_grad: bfloat16 [2048, 2048], P('expert'), may hold values from -6 to 6
- route_ids: int32 [2048, 8], P('expert'), may hold values from 0 to 15, all different within a row; in each aligned block of 128 rows (0 to 127, 128 to 255, ...) at most 72 rows name the same one
- route_probs: float32 [2048, 8], P('expert'), may hold values from 0.05 to 1
- gate_store: bfloat16 [16, 2048, 768], P(None, 'expert', 'dp'), may hold values from -0.125 to 0.125
- up_store: bfloat16 [16, 2048, 768], P(None, 'expert', 'dp'), may hold values from -0.125 to 0.125
- down_store: bfloat16 [16, 2048, 768], P(None, 'expert', 'dp'), may hold values from -0.21875 to 0.21875
Outputs:
- grad_gate: bfloat16 [16, 2048, 768], P('expert', None, 'dp')
- grad_up: bfloat16 [16, 2048, 768], P('expert', None, 'dp')
- grad_down: bfloat16 [16, 2048, 768], P('expert', None, 'dp')
- grad_tokens: bfloat16 [2048, 2048], P('expert')
The draws below stay inside these ranges and needn't reach their ends.
Inputs may be any that keep to these rules, and one draw needn't show every extreme that they name: `route_ids`: among the 128 tokens of one device no expert is named more than 72 times, and in every draw some expert is named exactly 72 times by some device's tokens.
All inputs are finite; a program needn't handle non-finite values.
Results may differ from the reference program's by a relative error of at most 0.0065.
Values may be sent and summed in bfloat16 or wider, within the bound.
A program may use at most 128 MiB of HBM per device.

```python
import math
import jax
import jax.numpy as jnp
import numpy as np
from jax import lax

D = 2048
HID = 768
TOPK = 8
TOK_DEV = 128
EXPERTS = 16
TOKENS = 2048
CAP = 72
N_EXPERT = 16


def levels(rng, shape, cuts, least, top_value):
    def one(dim, blocks):
        steps = jax.random.uniform(jax.random.fold_in(jax.random.fold_in(rng, 6), dim), (blocks,), jnp.float32, least / len(cuts), top_value / len(cuts))
        return jnp.repeat(jnp.exp(steps), shape[dim] // blocks).reshape((-1,) + (1,) * (len(shape) - dim - 1))

    gain = one(*cuts[0])
    for cut in cuts[1:]:
        gain = gain * one(*cut)
    return gain


def shared_out(rng, own, number, rows, amount, top, reach, lean):
    sequence = jax.random.permutation(rng, amount)
    heavy_load, usual = shares(amount, rows * top, reach, lean, True), shares(amount, rows * top, reach, lean, False)
    places = jnp.arange(amount)

    def named(sizes, offset_by):
        used = int((sizes > 0).sum())
        fixed = max(1, used // 4)
        shifted = fixed + (places - fixed + offset_by * (used - fixed)) % max(1, amount - fixed)
        return jnp.zeros((amount,), jnp.int32).at[sequence[jnp.where(places < fixed, places, shifted)]].set(jnp.asarray(sizes, jnp.int32))

    sizes = jnp.where(number % 4 == 0, named(heavy_load, number // 4), named(usual, number - number // 4 - 1))
    mixed = jax.random.permutation(jax.random.fold_in(own, 3), amount)
    donor, receiver = mixed[0:amount // 2 * 2:2], mixed[1:amount // 2 * 2:2]
    margin = jnp.minimum(sizes[donor] - 1, reach - sizes[receiver]) // 2
    margin = jnp.where((donor == sequence[0]) | (receiver == sequence[0]) | (sizes[receiver] == 0), 0, jnp.maximum(margin, 0))
    shifted = jax.random.randint(jax.random.fold_in(own, 4), (amount // 2,), 0, 1 << 20) % (margin + 1)
    sizes = sizes.at[donor].add(-shifted).at[receiver].add(shifted)
    items = jnp.searchsorted(jnp.cumsum(sizes), jnp.arange(rows * top), side="right").astype(jnp.int32)
    listing = items.reshape(top, rows).T
    listing = listing[jax.random.permutation(jax.random.fold_in(own, 1), rows)]
    offset_by = jax.random.randint(jax.random.fold_in(own, 2), (rows, 1), 0, top)
    return jnp.take_along_axis(listing, (jnp.arange(top)[None, :] + offset_by) % top, axis=1)


def shares(count, total, bound, skew, full):
    weights = [(1 << 20) // math.isqrt(standing ** skew) + 1 for standing in range(1, count + 1)]
    largest = bound if full else min(bound, max(-(-total // count), total * weights[0] // sum(weights)))
    least = 1 if total - largest >= count - 1 else 0
    given, spare = [largest] + [least] * (count - 1), total - largest - least * (count - 1)
    while spare > 0:
        free = [i for i in range(1, count) if given[i] < largest] or [i for i in range(1, count) if given[i] < bound]
        whole, budget = sum([weights[i] for i in free]), spare
        for i in free:
            extra = min(bound - given[i], max(1, budget * weights[i] // whole), spare)
            given[i] = given[i] + extra
            spare = spare - extra
    return np.array(given)


def centred(stream_key, shape, scale, bound, split=(), kind=jnp.bfloat16):
    drawn = scale * jax.random.normal(stream_key, shape, jnp.float32)
    if split:
        drawn = drawn * levels(stream_key, shape, split, -0.22, 0.18)
    return jnp.clip(drawn, -bound, bound).astype(kind)


def setup_inputs(seed: int = 0) -> dict:
    splits = jax.random.split(jax.random.key(seed), 8)
    tokens = centred(splits[0], (TOKENS, D), 1.0, 6.0, ((0, 16),))
    out_grad = centred(splits[1], (TOKENS, D), 1.0, 6.0, ((0, 16),))
    route_ids_keys = jax.random.split(jax.random.fold_in(splits[2], 1), TOKENS // TOK_DEV)
    route_ids_turns = jax.random.permutation(jax.random.fold_in(splits[2], 3), TOKENS // TOK_DEV)
    route_ids = jax.vmap(lambda own, number: shared_out(jax.random.fold_in(splits[2], 2), own, number, TOK_DEV, EXPERTS, TOPK, CAP, 2))(route_ids_keys, route_ids_turns).reshape((TOKENS, TOPK))
    route_probs = jnp.clip(jnp.exp(math.log(1.0) - 2.9957323 * jax.random.uniform(splits[3], (TOKENS, TOPK), jnp.float32) ** levels(splits[3], (TOKENS, TOPK), ((0, 16),), -0.2, 0.2)), 0.05, 1.0)
    gate_store = centred(splits[4], (EXPERTS, D, HID), D ** -0.5, 0.125, ((1, 16), (2, 2)))
    up_store = centred(splits[5], (EXPERTS, D, HID), D ** -0.5, 0.125, ((1, 16), (2, 2)))
    down_store = centred(splits[6], (EXPERTS, D, HID), HID ** -0.5, 0.21875, ((1, 16), (2, 2)))
    return {"tokens": tokens, "out_grad": out_grad, "route_ids": route_ids, "route_probs": route_probs, "gate_store": gate_store, "up_store": up_store, "down_store": down_store}


def reference(tokens, out_grad, route_ids, route_probs, gate_store, up_store, down_store):
    top_count = route_ids.shape[1]
    flat_ids = route_ids.reshape(-1)
    flat_probs = route_probs.reshape(-1)
    slot_total = flat_ids.shape[0]
    most_rows = N_EXPERT * CAP

    def per_expert(token_sum, expert):
        slot_list = jnp.nonzero(flat_ids == expert, size=most_rows, fill_value=slot_total)[0].astype(jnp.int32)
        is_valid = slot_list < slot_total
        safe_index = jnp.where(is_valid, slot_list, 0).astype(jnp.int32)
        owner_row = (safe_index // top_count).astype(jnp.int32)
        rows_in = jnp.where(is_valid[:, None], tokens[owner_row], jnp.zeros((), jnp.bfloat16)).astype(jnp.bfloat16)
        slot_scale = jnp.where(is_valid, flat_probs[safe_index], jnp.zeros((), jnp.float32))
        slot_grad = (slot_scale[:, None] * out_grad[owner_row].astype(jnp.float32)).astype(jnp.bfloat16)
        gate_panel = gate_store[expert]
        up_panel = up_store[expert]
        down_panel = down_store[expert]
        gate_pre = jnp.dot(rows_in, gate_panel, preferred_element_type=jnp.float32)
        up_pre = jnp.dot(rows_in, up_panel, preferred_element_type=jnp.float32)
        sigmoid_gate = jax.nn.sigmoid(gate_pre)
        activation = (gate_pre * sigmoid_gate * up_pre).astype(jnp.bfloat16)
        act_grad = jnp.dot(slot_grad, down_panel, preferred_element_type=jnp.float32)
        up_grad = (act_grad * gate_pre * sigmoid_gate).astype(jnp.bfloat16)
        gate_grad = (act_grad * up_pre * sigmoid_gate * (1.0 + gate_pre * (1.0 - sigmoid_gate))).astype(jnp.bfloat16)
        contract = (((0,), (0,)), ((), ()))
        down_part = lax.dot_general(slot_grad, activation, contract, preferred_element_type=jnp.float32)
        gate_part = lax.dot_general(rows_in, gate_grad, contract, preferred_element_type=jnp.float32)
        up_part = lax.dot_general(rows_in, up_grad, contract, preferred_element_type=jnp.float32)
        back_contract = (((1,), (1,)), ((), ()))
        slot_input = (lax.dot_general(gate_grad, gate_panel, back_contract, preferred_element_type=jnp.float32)
                      + lax.dot_general(up_grad, up_panel, back_contract, preferred_element_type=jnp.float32)).astype(jnp.bfloat16)
        added = jnp.where(is_valid[:, None], slot_input.astype(jnp.float32), jnp.zeros((), jnp.float32))
        token_sum = token_sum.at[owner_row].add(added)
        return token_sum, (gate_part.astype(jnp.bfloat16), up_part.astype(jnp.bfloat16), down_part.astype(jnp.bfloat16))

    start_sum = jnp.zeros(tokens.shape, jnp.float32)
    token_sum, grads = lax.scan(per_expert, start_sum, jnp.arange(EXPERTS, dtype=jnp.int32))
    return grads[0], grads[1], grads[2], token_sum.astype(jnp.bfloat16)
```

```python
import jax
import jax.numpy as jnp
from jax import lax
from jax.sharding import PartitionSpec as P


def joined(own, other):
    first = lax.axis_index("dp") == 0
    return jnp.where(first, jnp.concatenate([own, other], -1), jnp.concatenate([other, own], -1))


def swapped(part):
    return lax.ppermute(part, "dp", [(0, 1), (1, 0)])


def placed_sparse(tokens, out_grad, route_ids, route_probs, gate_store, up_store, down_store):
    tok_rows, model_width = tokens.shape
    top_count = route_ids.shape[1]
    experts = lax.axis_size("expert")
    capacity = max(2, 9 * tok_rows * top_count // (8 * experts))
    slots = experts * capacity
    width = model_width // 2
    here = lax.axis_index("dp") * width
    there = width - here
    f32, bf16 = jnp.float32, jnp.bfloat16

    chosen = route_ids[:, :, None] == jnp.arange(experts, dtype=jnp.int32)[None, None, :]
    weight = jnp.sum(jnp.where(chosen, route_probs[:, :, None], 0.0), axis=1)
    named = jnp.any(chosen, axis=1)
    earlier = jnp.arange(tok_rows)[:, None] > jnp.arange(tok_rows)[None, :]
    rank = jnp.dot(earlier.astype(bf16), named.astype(bf16), preferred_element_type=f32)
    rank = jnp.where(named, rank, -1.0)
    hit = rank.T[:, None, :] == jnp.arange(capacity, dtype=f32)[None, :, None]
    slot_prob = jnp.sum(jnp.where(hit, weight.T[:, None, :], 0.0), axis=2)
    place = hit.astype(bf16).reshape(slots, tok_rows)

    x_part = jnp.dot(
        place, lax.dynamic_slice_in_dim(tokens, here, width, 1), preferred_element_type=f32
    ).astype(bf16)
    dy_part = (
        jnp.dot(place, lax.dynamic_slice_in_dim(out_grad, here, width, 1), preferred_element_type=f32)
        * slot_prob.reshape(slots, 1)
    ).astype(bf16)

    def exchange(a):
        return lax.all_to_all(a, "expert", split_axis=0, concat_axis=0, tiled=True)

    def panel(store):
        return lax.all_to_all(store, "expert", split_axis=0, concat_axis=1, tiled=True)[0]

    x_own = exchange(x_part.reshape(experts, capacity, width)).reshape(slots, width)
    gate_panel = panel(gate_store)
    up_panel = panel(up_store)
    dy_own = exchange(dy_part.reshape(experts, capacity, width)).reshape(slots, width)
    down_panel = panel(down_store)
    rows_in = joined(x_own, swapped(x_own))
    dy_rows = joined(dy_own, swapped(dy_own))
    gate_pre = jnp.dot(rows_in, gate_panel, preferred_element_type=f32)
    up_pre = jnp.dot(rows_in, up_panel, preferred_element_type=f32)
    sig = jax.nn.sigmoid(gate_pre)
    activation = (gate_pre * sig * up_pre).astype(bf16)
    act_grad = jnp.dot(dy_rows, down_panel, preferred_element_type=f32)
    up_grad = (act_grad * gate_pre * sig).astype(bf16)
    gate_grad = (act_grad * up_pre * sig * (1.0 + gate_pre * (1.0 - sig))).astype(bf16)
    back = (((1,), (1,)), ((), ()))

    def slot_part(start):
        rows = [lax.dynamic_slice_in_dim(w, start, width, 0) for w in (gate_panel, up_panel)]
        return lax.dot_general(gate_grad, rows[0], back, preferred_element_type=f32) + lax.dot_general(
            up_grad, rows[1], back, preferred_element_type=f32
        )

    arrived = swapped(slot_part(there).astype(bf16))
    summed = (slot_part(here) + arrived.astype(f32)).astype(bf16)
    returned = exchange(summed.reshape(experts, capacity, width)).reshape(slots, width)
    share = lax.dot_general(place, returned, (((0,), (0,)), ((), ())), preferred_element_type=f32).astype(bf16)
    grad_tokens = joined(share, swapped(share))
    outer = (((0,), (0,)), ((), ()))
    grad_down = lax.dot_general(dy_rows, activation, outer, preferred_element_type=f32).astype(bf16)
    grad_gate = lax.dot_general(rows_in, gate_grad, outer, preferred_element_type=f32).astype(bf16)
    grad_up = lax.dot_general(rows_in, up_grad, outer, preferred_element_type=f32).astype(bf16)
    return (grad_gate[None], grad_up[None], grad_down[None], grad_tokens)


def placed_dense(tokens, out_grad, route_ids, route_probs, gate_store, up_store, down_store):
    tok_rows, model_width = tokens.shape
    top_count = route_ids.shape[1]
    experts = lax.axis_size("expert")
    capacity = max(2, 9 * tok_rows * top_count // (8 * experts))
    slots = experts * capacity
    width = model_width // 2
    here = lax.axis_index("dp") * width
    there = width - here
    me = lax.axis_index("expert")
    f32, bf16 = jnp.float32, jnp.bfloat16

    def panel(store):
        return lax.all_to_all(store, "expert", split_axis=0, concat_axis=1, tiled=True)[0]

    route = jnp.concatenate([route_ids.astype(f32), route_probs], axis=1)
    route = lax.all_gather(route, "expert", axis=0, tiled=False)
    x_all = lax.all_gather(lax.dynamic_slice_in_dim(tokens, here, width, 1), "expert", axis=0, tiled=False)
    dy_all = lax.all_gather(lax.dynamic_slice_in_dim(out_grad, here, width, 1), "expert", axis=0, tiled=False)
    chosen = route[:, :, :top_count] == me.astype(f32)
    weight = jnp.sum(jnp.where(chosen, route[:, :, top_count:], 0.0), axis=2)
    named = jnp.any(chosen, axis=2)
    earlier = jnp.arange(tok_rows)[:, None] < jnp.arange(tok_rows)[None, :]
    rank = jnp.dot(named.astype(bf16), earlier.astype(bf16), preferred_element_type=f32)
    rank = jnp.where(named, rank, -1.0)
    hit = rank[:, None, :] == jnp.arange(capacity, dtype=f32)[None, :, None]
    slot_prob = jnp.sum(jnp.where(hit, weight[:, None, :], 0.0), axis=2)
    place = hit.astype(bf16)
    batch = (((2,), (1,)), ((0,), (0,)))
    x_own = lax.dot_general(place, x_all, batch, preferred_element_type=f32).astype(bf16).reshape(slots, width)
    dy_own = (
        lax.dot_general(place, dy_all, batch, preferred_element_type=f32) * slot_prob[:, :, None]
    ).astype(bf16).reshape(slots, width)
    gate_panel = panel(gate_store)
    up_panel = panel(up_store)
    down_panel = panel(down_store)
    rows_in = joined(x_own, swapped(x_own))
    dy_rows = joined(dy_own, swapped(dy_own))
    gate_pre = jnp.dot(rows_in, gate_panel, preferred_element_type=f32)
    up_pre = jnp.dot(rows_in, up_panel, preferred_element_type=f32)
    sig = jax.nn.sigmoid(gate_pre)
    activation = (gate_pre * sig * up_pre).astype(bf16)
    act_grad = jnp.dot(dy_rows, down_panel, preferred_element_type=f32)
    up_grad = (act_grad * gate_pre * sig).astype(bf16)
    gate_grad = (act_grad * up_pre * sig * (1.0 + gate_pre * (1.0 - sig))).astype(bf16)
    back = (((1,), (1,)), ((), ()))

    def slot_part(start):
        rows = [lax.dynamic_slice_in_dim(w, start, width, 0) for w in (gate_panel, up_panel)]
        return lax.dot_general(gate_grad, rows[0], back, preferred_element_type=f32) + lax.dot_general(
            up_grad, rows[1], back, preferred_element_type=f32
        )

    arrived = swapped(slot_part(there).astype(bf16))
    summed = (slot_part(here) + arrived.astype(f32)).astype(bf16)
    sums = lax.dot_general(
        place, summed.reshape(experts, capacity, width), (((1,), (1,)), ((0,), (0,))), preferred_element_type=f32
    ).astype(bf16)
    share = lax.psum_scatter(sums, "expert", scatter_dimension=0, tiled=False)
    grad_tokens = joined(share, swapped(share))
    outer = (((0,), (0,)), ((), ()))
    grad_down = lax.dot_general(dy_rows, activation, outer, preferred_element_type=f32).astype(bf16)
    grad_gate = lax.dot_general(rows_in, gate_grad, outer, preferred_element_type=f32).astype(bf16)
    grad_up = lax.dot_general(rows_in, up_grad, outer, preferred_element_type=f32).astype(bf16)
    return (grad_gate[None], grad_up[None], grad_down[None], grad_tokens)


def placed(tokens, out_grad, route_ids, route_probs, gate_store, up_store, down_store):
    dense = 4 * route_ids.shape[1] >= lax.axis_size("expert")
    body = placed_dense if dense else placed_sparse
    return body(tokens, out_grad, route_ids, route_probs, gate_store, up_store, down_store)


def solution(mesh):
    return jax.shard_map(
        placed,
        mesh=mesh,
        in_specs=(
            P("expert", None),
            P("expert", None),
            P("expert", None),
            P("expert", None),
            P(None, "expert", "dp"),
            P(None, "expert", "dp"),
            P(None, "expert", "dp"),
        ),
        out_specs=(
            P("expert", None, "dp"),
            P("expert", None, "dp"),
            P("expert", None, "dp"),
            P("expert", None),
        ),
        check_vma=False,
    )
```

```python
import functools

import jax
import jax.numpy as jnp
from jax import lax
from jax.experimental import pallas as pl
from jax.experimental.pallas import tpu as pltpu
from jax.sharding import PartitionSpec as P


def joined(own, other):
    first = lax.axis_index("dp") == 0
    return jnp.where(first, jnp.concatenate([own, other], -1), jnp.concatenate([other, own], -1))


def swapped(part):
    return lax.ppermute(part, "dp", [(0, 1), (1, 0)])


def placed_sparse(tokens, out_grad, route_ids, route_probs, gate_store, up_store, down_store):
    tok_rows, model_width = tokens.shape
    top_count = route_ids.shape[1]
    experts = lax.axis_size("expert")
    capacity = max(2, 9 * tok_rows * top_count // (8 * experts))
    slots = experts * capacity
    width = model_width // 2
    here = lax.axis_index("dp") * width
    there = width - here
    f32, bf16 = jnp.float32, jnp.bfloat16

    chosen = route_ids[:, :, None] == jnp.arange(experts, dtype=jnp.int32)[None, None, :]
    weight = jnp.sum(jnp.where(chosen, route_probs[:, :, None], 0.0), axis=1)
    named = jnp.any(chosen, axis=1)
    earlier = jnp.arange(tok_rows)[:, None] > jnp.arange(tok_rows)[None, :]
    rank = jnp.dot(earlier.astype(bf16), named.astype(bf16), preferred_element_type=f32)
    rank = jnp.where(named, rank, -1.0)
    hit = rank.T[:, None, :] == jnp.arange(capacity, dtype=f32)[None, :, None]
    slot_prob = jnp.sum(jnp.where(hit, weight.T[:, None, :], 0.0), axis=2)
    place = hit.astype(bf16).reshape(slots, tok_rows)

    x_part = jnp.dot(
        place, lax.dynamic_slice_in_dim(tokens, here, width, 1), preferred_element_type=f32
    ).astype(bf16)
    dy_part = (
        jnp.dot(place, lax.dynamic_slice_in_dim(out_grad, here, width, 1), preferred_element_type=f32)
        * slot_prob.reshape(slots, 1)
    ).astype(bf16)

    def exchange(a):
        return lax.all_to_all(a, "expert", split_axis=0, concat_axis=0, tiled=True)

    def panel(store):
        return lax.all_to_all(store, "expert", split_axis=0, concat_axis=1, tiled=True)[0]

    x_own = exchange(x_part.reshape(experts, capacity, width)).reshape(slots, width)
    gate_panel = panel(gate_store)
    up_panel = panel(up_store)
    dy_own = exchange(dy_part.reshape(experts, capacity, width)).reshape(slots, width)
    down_panel = panel(down_store)
    rows_in = joined(x_own, swapped(x_own))
    dy_rows = joined(dy_own, swapped(dy_own))
    gate_pre = jnp.dot(rows_in, gate_panel, preferred_element_type=f32)
    up_pre = jnp.dot(rows_in, up_panel, preferred_element_type=f32)
    sig = jax.nn.sigmoid(gate_pre)
    activation = (gate_pre * sig * up_pre).astype(bf16)
    act_grad = jnp.dot(dy_rows, down_panel, preferred_element_type=f32)
    up_grad = (act_grad * gate_pre * sig).astype(bf16)
    gate_grad = (act_grad * up_pre * sig * (1.0 + gate_pre * (1.0 - sig))).astype(bf16)
    back = (((1,), (1,)), ((), ()))

    def slot_part(start):
        rows = [lax.dynamic_slice_in_dim(w, start, width, 0) for w in (gate_panel, up_panel)]
        return lax.dot_general(gate_grad, rows[0], back, preferred_element_type=f32) + lax.dot_general(
            up_grad, rows[1], back, preferred_element_type=f32
        )

    arrived = swapped(slot_part(there).astype(bf16))
    summed = (slot_part(here) + arrived.astype(f32)).astype(bf16)
    returned = exchange(summed.reshape(experts, capacity, width)).reshape(slots, width)
    share = lax.dot_general(place, returned, (((0,), (0,)), ((), ())), preferred_element_type=f32).astype(bf16)
    grad_tokens = joined(share, swapped(share))
    outer = (((0,), (0,)), ((), ()))
    grad_down = lax.dot_general(dy_rows, activation, outer, preferred_element_type=f32).astype(bf16)
    grad_gate = lax.dot_general(rows_in, gate_grad, outer, preferred_element_type=f32).astype(bf16)
    grad_up = lax.dot_general(rows_in, up_grad, outer, preferred_element_type=f32).astype(bf16)
    return (grad_gate[None], grad_up[None], grad_down[None], grad_tokens)


f32, bf16 = jnp.float32, jnp.bfloat16
MESH = pl.DeviceIdType.MESH


def dense_kernel(
    experts, capacity,
    ids_ref, probs_ref, x_ref, dy_ref, gate_ref, up_ref, down_ref,
    grad_gate_ref, grad_up_ref, grad_down_ref, grad_tokens_ref,
    info, info_all, gu, dn, tok, nbr_out, rows, pls, pre, act, activ, gg,
    mine, cs_out, cs_in, comb, s_out, t_own, t_out, xr, z_out, z_in, stage, fin,
    local_sem, info_send, info_recv, w_send, w_recv, w_own,
    ag_up, ag_down, ag_zr, ag_xs, ag_xr, y_send, y_recv, c_send, c_recv,
    cs_send, cs_recv, ys_send, ys_recv, xs_send, xs_recv, zs_send, zs_recv, out_sem, fin_sem,
):
    me, core = lax.axis_index("expert"), lax.axis_index("dp")
    planes = experts // 4
    z, y, x = me // 4, (me // 2) % 2, me % 2
    x_peer, y_peer = me + 1 - 2 * x, me + 2 - 4 * y
    tok_rows, model_width = x_ref.shape
    width = model_width // 2
    hid = gate_ref.shape[2]
    pair = 2 * capacity
    quad = 4 * capacity
    slots = experts * capacity
    slab = model_width // planes
    here = pl.multiple_of(core * width, width)
    batch0 = (((0,), (0,)), ((), ()))

    def remote(src, dst, send, recv, expert=None):
        target = {"dp": 1 - core} if expert is None else {"expert": expert}
        return pltpu.make_async_remote_copy(
            src_ref=src, dst_ref=dst, send_sem=send, recv_sem=recv, device_id=target, device_id_type=MESH
        )

    def at(start, size):
        return pl.ds(pl.multiple_of(start, size), size)

    def peer_of(k):
        return lax.rem(me + k, experts)

    barrier = pltpu.get_barrier_semaphore()

    def greet(k, carry):
        pl.semaphore_signal(barrier, inc=1, device_id={"expert": peer_of(k)}, device_id_type=MESH)
        return carry

    lax.fori_loop(1, experts, greet, 0)
    pl.semaphore_signal(barrier, inc=1, device_id={"dp": 1 - core}, device_id_type=MESH)

    own_copies = []
    for a, ref in enumerate((x_ref, dy_ref)):
        own_copies.append(
            pltpu.make_async_copy(ref.at[:, pl.ds(here, width)], tok.at[a, z, at(x * tok_rows, tok_rows), :], local_sem.at[a])
        )
    own_rows = at((me % 4) * tok_rows, tok_rows)
    own_panels = [
        pltpu.make_async_copy(gate_ref.at[me], gu.at[z, own_rows, pl.ds(0, hid)], w_own.at[0]),
        pltpu.make_async_copy(up_ref.at[me], gu.at[z, own_rows, pl.ds(hid, hid)], w_own.at[1]),
        pltpu.make_async_copy(down_ref.at[me], dn.at[z, own_rows, :], w_own.at[2]),
    ]
    for copy in own_copies:
        copy.start()
    for copy in own_panels:
        copy.start()
    pl.semaphore_wait(barrier, experts)

    def w_copy(w, target, owner):
        spot = at((owner % 4) * tok_rows, tok_rows)
        if w == 0:
            src, dst = gate_ref, gu.at[owner // 4, spot, pl.ds(0, hid)]
        elif w == 1:
            src, dst = up_ref, gu.at[owner // 4, spot, pl.ds(hid, hid)]
        else:
            src, dst = down_ref, dn.at[owner // 4, spot, :]
        return remote(src.at[target], dst, w_send.at[w, target], w_recv.at[w, owner], target)

    def start_panel(w, first, last):
        def body(k, carry):
            w_copy(w, peer_of(k), me).start()
            return carry

        lax.fori_loop(first, last, body, 0)

    def wait_panel(w, source):
        w_copy(w, source, source).wait_recv()

    def tok_block(a, zs, xs):
        return tok.at[a, zs, at(xs * tok_rows, tok_rows), :]

    def ag_copy(a, zs, direction):
        block = tok_block(a, zs, x)
        if direction == 0:
            return remote(block, block, ag_up.at[a, zs], ag_zr.at[a, zs], me + 4)
        if direction == 1:
            return remote(block, block, ag_down.at[a, zs], ag_zr.at[a, zs], me - 4)
        return remote(block, block, ag_xs.at[a, zs], ag_xr.at[a, zs], x_peer)

    def walk(t):
        return z + ((t + 1) // 2) * (1 - 2 * (t % 2))

    def inside(zs):
        return jnp.logical_and(zs >= 0, zs < planes)

    def forwards(zs):
        return (
            jnp.logical_and(zs <= z, z < planes - 1),
            jnp.logical_and(zs >= z, z > 0),
        )

    def send_block(a, zs):
        go_up, go_down = forwards(zs)

        @pl.when(go_up)
        def _():
            ag_copy(a, zs, 0).start()

        @pl.when(go_down)
        def _():
            ag_copy(a, zs, 1).start()

        ag_copy(a, zs, 2).start()

    for a in range(2):
        own_copies[a].wait()
        send_block(a, z)
    start_panel(0, 1, experts)

    ids, probs = ids_ref[...], probs_ref[...]
    named_by = lax.broadcasted_iota(jnp.int32, (experts,) + ids.shape, 0) == ids[None, :, :]
    weight = jnp.sum(jnp.where(named_by, probs[None, :, :], 0.0), axis=1)
    named = jnp.sum(jnp.where(named_by, 1.0, 0.0), axis=1)
    before = lax.broadcasted_iota(jnp.int32, (tok_rows, tok_rows), 0) < lax.broadcasted_iota(
        jnp.int32, (tok_rows, tok_rows), 1
    )
    rank = jnp.dot(named.astype(bf16), jnp.where(before, 1.0, 0.0).astype(bf16), preferred_element_type=f32)
    rank = jnp.where(named > 0.5, rank + (x * capacity).astype(f32), -1.0)
    line = lax.broadcasted_iota(jnp.int32, (experts, 8, tok_rows), 1)
    info[...] = jnp.where(line == 0, rank[:, None, :], weight[:, None, :])
    info_all[me] = info[at(z * 4, 4)]

    def info_copy(target, owner):
        return remote(
            info.at[at((target // 4) * 4, 4)], info_all.at[owner], info_send.at[target], info_recv.at[owner], target
        )

    def send_info(k, carry):
        info_copy(peer_of(k), me).start()
        return carry

    lax.fori_loop(1, experts, send_info, 0)

    hops = 2 * planes - 2
    for t in range(1, hops + 1):
        zs = walk(t)

        @pl.when(inside(zs))
        def _():
            for a in range(2):
                remote(tok_block(a, zs, x), tok_block(a, zs, x), ag_up.at[a, zs], ag_zr.at[a, zs], x_peer).wait_recv()
                send_block(a, zs)

        start_panel(1, 1 + (t - 1) * (experts - 1) // hops, 1 + t * (experts - 1) // hops)

    def wait_info(k, carry):
        source = peer_of(k)
        info_copy(source, source).wait_recv()
        return carry

    lax.fori_loop(1, experts, wait_info, 0)

    def pair_rows(zs, ys):
        return at((2 * zs + ys) * pair, pair)

    def places(zs, expert_index):
        first = 4 * zs + 2 * y
        both = jnp.concatenate(
            [info_all[first, expert_index, :, :], info_all[first + 1, expert_index, :, :]], axis=1
        )
        hit = both[0:1, :] == lax.broadcasted_iota(jnp.int32, (pair, 2 * tok_rows), 0).astype(f32)
        prob = jnp.sum(jnp.where(hit, both[1:2, :], 0.0), axis=1, keepdims=True)
        return jnp.where(hit, 1.0, 0.0).astype(bf16), prob

    def y_copy(a, zs, ys):
        return remote(
            nbr_out.at[a, zs], rows.at[a, core, pair_rows(zs, ys), :], y_send.at[a, zs], y_recv.at[a, zs], y_peer
        )

    def core_copy(a, half, zs, ys):
        block = rows.at[a, half, pair_rows(zs, ys), :]
        return remote(block, block, c_send.at[a, 2 * zs + ys], c_recv.at[a, 2 * zs + ys])

    mine_q = me % 4
    peer_q = y_peer % 4

    def gather(t, carry):
        zs = walk(t)

        @pl.when(inside(zs))
        def _():
            own_place, own_prob = places(zs, mine_q)
            nbr_place, nbr_prob = places(zs, peer_q)
            pls[zs, pl.ds(0, pair), :] = own_place
            pls[zs, pl.ds(pair, pair), :] = nbr_place
            for a in range(2):
                ag_copy(a, zs, 2).wait_recv()
                got = jnp.dot(own_place, tok[a, zs], preferred_element_type=f32)
                lent = jnp.dot(nbr_place, tok[a, zs], preferred_element_type=f32)
                if a == 1:
                    got, lent = got * own_prob, lent * nbr_prob
                nbr_out[a, zs] = lent.astype(bf16)
                y_copy(a, zs, y).start()
                rows[a, core, pair_rows(zs, y), :] = got.astype(bf16)
                core_copy(a, core, zs, y).start()

        def more(k, inner):
            @pl.when(k < experts)
            def _():
                w_copy(2, peer_of(k), me).start()

            return inner

        lax.fori_loop(1 + 3 * t, 4 + 3 * t, more, 0)
        return carry

    lax.fori_loop(0, hops + 1, gather, 0)

    def pass_on(t, carry):
        zs = walk(t)

        @pl.when(inside(zs))
        def _():
            for a in range(2):
                y_copy(a, zs, 1 - y).wait_recv()
                core_copy(a, core, zs, 1 - y).start()

        return carry

    lax.fori_loop(0, hops + 1, pass_on, 0)

    def wait_core(p, carry):
        for a in range(2):
            core_copy(a, 1 - core, p // 2, p % 2).wait_recv()
        return carry

    lax.fori_loop(0, 2 * planes, wait_core, 0)
    for w in range(2):
        own_panels[w].wait()

        def wait_gu(k, carry):
            wait_panel(w, peer_of(k))
            return carry

        lax.fori_loop(1, experts, wait_gu, 0)

    def slab_of(a, g, spot):
        half, off = (g * slab) // width, (g * slab) % width
        return rows[a, half, spot, pl.ds(off, slab)]

    def forward(m, carry):
        spot = at(m * quad, quad)
        total = jnp.dot(slab_of(0, 0, spot), gu[0], preferred_element_type=f32)
        for g in range(1, planes):
            total += jnp.dot(slab_of(0, g, spot), gu[g], preferred_element_type=f32)
        pre[spot, :] = total
        return carry

    lax.fori_loop(0, planes, forward, 0)
    own_panels[2].wait()
    for g in range(planes):
        for q in range(4):
            source = 4 * g + q

            @pl.when(source != me)
            def _():
                wait_panel(2, source)

        def backward(m, carry):
            spot = at(m * quad, quad)
            part = jnp.dot(slab_of(1, g, spot), dn[g], preferred_element_type=f32)
            if g == 0:
                act[spot, :] = part
            else:
                act[spot, :] += part
            return carry

        lax.fori_loop(0, planes, backward, 0)

    def pointwise(m, carry):
        spot = at(m * 16, 16)
        gate_pre, up_pre, act_grad = pre[spot, pl.ds(0, hid)], pre[spot, pl.ds(hid, hid)], act[spot, :]
        sig = jax.nn.sigmoid(gate_pre)
        activ[spot, :] = (gate_pre * sig * up_pre).astype(bf16)
        gg[spot, pl.ds(0, hid)] = (act_grad * up_pre * sig * (1.0 + gate_pre * (1.0 - sig))).astype(bf16)
        gg[spot, pl.ds(hid, hid)] = (act_grad * gate_pre * sig).astype(bf16)
        return carry

    back = (((1,), (1,)), ((), ()))
    half_planes = planes // 2

    def cs_copy(d):
        return remote(cs_out.at[d], cs_in.at[d], cs_send.at[d], cs_recv.at[d])

    def ys_copy(d):
        return remote(s_out.at[d], comb.at[d, pl.ds(pair, pair), :], ys_send.at[d], ys_recv.at[d], y_peer)

    def xs_copy(d):
        return remote(t_out.at[d], xr.at[d], xs_send.at[d], xs_recv.at[d], x_peer)

    def slot_step(d):
        lax.fori_loop(d * (quad // 16), (d + 1) * (quad // 16), pointwise, 0)
        spot = pl.ds(d * quad, quad)
        for i in range(half_planes):
            there = (1 - core) * half_planes + i
            cs_out[d, :, pl.ds(i * slab, slab)] = lax.dot_general(
                gg[spot, :], gu[there], back, preferred_element_type=f32
            ).astype(bf16)
        cs_copy(d).start()
        for i in range(half_planes):
            mine[d, :, pl.ds(i * slab, slab)] = lax.dot_general(
                gg[spot, :], gu[core * half_planes + i], back, preferred_element_type=f32
            )

    def slot_sum(d):
        cs_copy(d).wait_recv()
        away, home = at((1 - y) * pair, pair), at(y * pair, pair)
        s_out[d] = (mine[d, away, :] + cs_in[d, away, :].astype(f32)).astype(bf16)
        ys_copy(d).start()
        comb[d, pl.ds(0, pair), :] = (mine[d, home, :] + cs_in[d, home, :].astype(f32)).astype(bf16)

    def token_step(d):
        ys_copy(d).wait_recv()
        t_out[d] = lax.dot_general(
            pls[d, :, at((1 - x) * tok_rows, tok_rows)], comb[d], batch0, preferred_element_type=f32
        ).astype(bf16)
        xs_copy(d).start()
        t_own[d] = lax.dot_general(
            pls[d, :, at(x * tok_rows, tok_rows)], comb[d], batch0, preferred_element_type=f32
        )

    def z_copy(d, up):
        if up:
            return remote(z_out.at[d], z_in.at[0, d], zs_send.at[d], zs_recv.at[0, d], me + 4)
        return remote(z_out.at[d], z_in.at[1, d], zs_send.at[d], zs_recv.at[1, d], me - 4)

    def z_take(d, side):
        remote(z_out.at[d], z_in.at[side, d], zs_send.at[d], zs_recv.at[side, d], x_peer).wait_recv()
        t_own[d] += z_in[side, d].astype(f32)

    def z_step(d):
        xs_copy(d).wait_recv()
        t_own[d] += xr[d].astype(f32)

        @pl.when(jnp.logical_and(d > z, z > 0))
        def _():
            z_take(d, 0)

        @pl.when(jnp.logical_and(d < z, z < planes - 1))
        def _():
            z_take(d, 1)

        @pl.when(d > z)
        def _():
            z_out[d] = t_own[d].astype(bf16)
            z_copy(d, True).start()

        @pl.when(d < z)
        def _():
            z_out[d] = t_own[d].astype(bf16)
            z_copy(d, False).start()

    tile = width // 4

    def out_copy(w, i):
        span = at(i * tile, tile)
        return pltpu.make_async_copy(
            stage.at[w, span, :], (grad_gate_ref, grad_up_ref, grad_down_ref)[w].at[span, :], out_sem.at[w, i]
        )

    def weight_grads(first, last):
        def body(i, carry):
            half, off, span = i // 4, at((i % 4) * tile, tile), at(i * tile, tile)
            both = lax.dot_general(rows[0, half, :, off], gg[...], batch0, preferred_element_type=f32)
            stage[0, span, :] = both[:, :hid].astype(bf16)
            stage[1, span, :] = both[:, hid:].astype(bf16)
            stage[2, span, :] = lax.dot_general(
                rows[1, half, :, off], activ[...], batch0, preferred_element_type=f32
            ).astype(bf16)
            for w in range(3):
                out_copy(w, i).start()
            return carry

        lax.fori_loop(first, last, body, 0)

    order = []
    for i in range(half_planes):
        order += [i, planes - 1 - i]
    for i, d in enumerate(order):
        slot_step(d)
        if i > 0:
            slot_sum(order[i - 1])
    slot_sum(order[-1])
    weight_grads(0, 3)
    token_step(order[0])
    weight_grads(3, 6)
    for i in range(1, planes):
        token_step(order[i])
        d = order[i - 1]

        @pl.when(d != z)
        def _():
            z_step(d)

        if i == 1:
            weight_grads(6, 8)

    @pl.when(order[-1] != z)
    def _():
        z_step(order[-1])

    xs_copy(z).wait_recv()
    t_own[z] += xr[z].astype(f32)

    @pl.when(z > 0)
    def _():
        z_take(z, 0)

    @pl.when(z < planes - 1)
    def _():
        z_take(z, 1)

    fin[...] = t_own[z].astype(bf16)
    home_spot = grad_tokens_ref.at[:, pl.ds(here, width)]
    last = remote(fin, home_spot, fin_sem.at[0], fin_sem.at[1])
    last.start()
    keep = pltpu.make_async_copy(fin, home_spot, fin_sem.at[2])
    keep.start()

    def drain_peers(k, carry):
        target = peer_of(k)
        for w in range(3):
            w_copy(w, target, me).wait_send()
        info_copy(target, me).wait_send()
        return carry

    lax.fori_loop(1, experts, drain_peers, 0)

    def drain_tokens(zs, carry):
        go_up, go_down = forwards(zs)
        for a in range(2):

            @pl.when(go_up)
            def _():
                ag_copy(a, zs, 0).wait_send()

            @pl.when(go_down)
            def _():
                ag_copy(a, zs, 1).wait_send()

            ag_copy(a, zs, 2).wait_send()
            y_copy(a, zs, y).wait_send()
            for ys in range(2):
                core_copy(a, core, zs, ys).wait_send()
        cs_copy(zs).wait_send()
        ys_copy(zs).wait_send()
        xs_copy(zs).wait_send()

        @pl.when(zs > z)
        def _():
            z_copy(zs, True).wait_send()

        @pl.when(zs < z)
        def _():
            z_copy(zs, False).wait_send()

        return carry

    lax.fori_loop(0, planes, drain_tokens, 0)

    def drain_out(i, carry):
        for w in range(3):
            out_copy(w, i).wait()
        return carry

    lax.fori_loop(0, 8, drain_out, 0)
    keep.wait()
    last.wait()


def placed_dense(tokens, out_grad, route_ids, route_probs, gate_store, up_store, down_store):
    tok_rows, model_width = tokens.shape
    top_count = route_ids.shape[1]
    experts, _, hid = gate_store.shape
    capacity = 9 * tok_rows * top_count // (8 * experts)
    slots, width, planes = experts * capacity, model_width // 2, experts // 4
    pair, quad, slab = 2 * capacity, 4 * capacity, model_width // planes
    vmem, dma = pltpu.VMEM, pltpu.SemaphoreType.DMA
    anywhere, on_chip = pl.BlockSpec(memory_space=pl.ANY), pl.BlockSpec(memory_space=pltpu.VMEM)
    scratch = [
        vmem((experts, 8, tok_rows), f32),
        vmem((experts, 4, 8, tok_rows), f32),
        vmem((planes, slab, 2 * hid), bf16),
        vmem((planes, slab, hid), bf16),
        vmem((2, planes, 2 * tok_rows, width), bf16),
        vmem((2, planes, pair, width), bf16),
        vmem((2, 2, slots, width), bf16),
        vmem((planes, quad, 2 * tok_rows), bf16),
        vmem((slots, 2 * hid), f32),
        vmem((slots, hid), f32),
        vmem((slots, hid), bf16),
        vmem((slots, 2 * hid), bf16),
        vmem((planes, quad, width), f32),
        vmem((planes, quad, width), bf16),
        vmem((planes, quad, width), bf16),
        vmem((planes, quad, width), bf16),
        vmem((planes, pair, width), bf16),
        vmem((planes, tok_rows, width), f32),
        vmem((planes, tok_rows, width), bf16),
        vmem((planes, tok_rows, width), bf16),
        vmem((planes, tok_rows, width), bf16),
        vmem((2, planes, tok_rows, width), bf16),
        vmem((3, model_width, hid), bf16),
        vmem((tok_rows, width), bf16),
        dma((2,)), dma((experts,)), dma((experts,)), dma((3, experts)), dma((3, experts)), dma((3,)),
        dma((2, planes)), dma((2, planes)), dma((2, planes)), dma((2, planes)), dma((2, planes)),
        dma((2, planes)), dma((2, planes)), dma((2, 2 * planes)), dma((2, 2 * planes)),
        dma((planes,)), dma((planes,)), dma((planes,)), dma((planes,)),
        dma((planes,)), dma((planes,)), dma((planes,)), dma((2, planes)), dma((3, 8)), dma((3,)),
    ]
    grad = jax.ShapeDtypeStruct((model_width, hid), bf16)
    outs = pl.pallas_call(
        functools.partial(dense_kernel, experts, capacity),
        out_shape=(grad, grad, grad, jax.ShapeDtypeStruct((tok_rows, model_width), bf16)),
        in_specs=[on_chip, on_chip] + [anywhere] * 5,
        out_specs=(anywhere,) * 4,
        scratch_shapes=scratch,
        compiler_params=pltpu.CompilerParams(
            collective_id=0, has_side_effects=True, vmem_limit_bytes=60 * 1024 * 1024
        ),
    )(route_ids.T, route_probs.T, tokens, out_grad, gate_store, up_store, down_store)
    return (outs[0][None], outs[1][None], outs[2][None], outs[3])


def placed(tokens, out_grad, route_ids, route_probs, gate_store, up_store, down_store):
    experts, top_count = lax.axis_size("expert"), route_ids.shape[1]
    capacity = 9 * tokens.shape[0] * top_count // (8 * experts)
    dense = 4 * top_count >= experts and experts % 8 == 0 and capacity % 8 == 0
    body = placed_dense if dense else placed_sparse
    return body(tokens, out_grad, route_ids, route_probs, gate_store, up_store, down_store)


def solution(mesh):
    return jax.shard_map(
        placed,
        mesh=mesh,
        in_specs=(
            P("expert", None),
            P("expert", None),
            P("expert", None),
            P("expert", None),
            P(None, "expert", "dp"),
            P(None, "expert", "dp"),
            P(None, "expert", "dp"),
        ),
        out_specs=(
            P("expert", None, "dp"),
            P("expert", None, "dp"),
            P("expert", None, "dp"),
            P("expert", None),
        ),
        check_vma=False,
    )
```

```python
import functools

import jax
import jax.numpy as jnp
from jax import lax
from jax.experimental import pallas as pl
from jax.experimental.pallas import tpu as pltpu
from jax.sharding import PartitionSpec as P


def joined(own, other):
    first = lax.axis_index("dp") == 0
    return jnp.where(first, jnp.concatenate([own, other], -1), jnp.concatenate([other, own], -1))


def swapped(part):
    return lax.ppermute(part, "dp", [(0, 1), (1, 0)])


def placed_sparse(tokens, out_grad, route_ids, route_probs, gate_store, up_store, down_store):
    tok_rows, model_width = tokens.shape
    top_count = route_ids.shape[1]
    experts = lax.axis_size("expert")
    capacity = max(2, 9 * tok_rows * top_count // (8 * experts))
    slots = experts * capacity
    width = model_width // 2
    here = lax.axis_index("dp") * width
    there = width - here
    f32, bf16 = jnp.float32, jnp.bfloat16

    chosen = route_ids[:, :, None] == jnp.arange(experts, dtype=jnp.int32)[None, None, :]
    weight = jnp.sum(jnp.where(chosen, route_probs[:, :, None], 0.0), axis=1)
    named = jnp.any(chosen, axis=1)
    earlier = jnp.arange(tok_rows)[:, None] > jnp.arange(tok_rows)[None, :]
    rank = jnp.dot(earlier.astype(bf16), named.astype(bf16), preferred_element_type=f32)
    rank = jnp.where(named, rank, -1.0)
    hit = rank.T[:, None, :] == jnp.arange(capacity, dtype=f32)[None, :, None]
    slot_prob = jnp.sum(jnp.where(hit, weight.T[:, None, :], 0.0), axis=2)
    place = hit.astype(bf16).reshape(slots, tok_rows)

    x_part = jnp.dot(
        place, lax.dynamic_slice_in_dim(tokens, here, width, 1), preferred_element_type=f32
    ).astype(bf16)
    dy_part = (
        jnp.dot(place, lax.dynamic_slice_in_dim(out_grad, here, width, 1), preferred_element_type=f32)
        * slot_prob.reshape(slots, 1)
    ).astype(bf16)

    def exchange(a):
        return lax.all_to_all(a, "expert", split_axis=0, concat_axis=0, tiled=True)

    def panel(store):
        return lax.all_to_all(store, "expert", split_axis=0, concat_axis=1, tiled=True)[0]

    x_own = exchange(x_part.reshape(experts, capacity, width)).reshape(slots, width)
    gate_panel = panel(gate_store)
    up_panel = panel(up_store)
    dy_own = exchange(dy_part.reshape(experts, capacity, width)).reshape(slots, width)
    down_panel = panel(down_store)
    rows_in = joined(x_own, swapped(x_own))
    dy_rows = joined(dy_own, swapped(dy_own))
    gate_pre = jnp.dot(rows_in, gate_panel, preferred_element_type=f32)
    up_pre = jnp.dot(rows_in, up_panel, preferred_element_type=f32)
    sig = jax.nn.sigmoid(gate_pre)
    activation = (gate_pre * sig * up_pre).astype(bf16)
    act_grad = jnp.dot(dy_rows, down_panel, preferred_element_type=f32)
    up_grad = (act_grad * gate_pre * sig).astype(bf16)
    gate_grad = (act_grad * up_pre * sig * (1.0 + gate_pre * (1.0 - sig))).astype(bf16)
    back = (((1,), (1,)), ((), ()))

    def slot_part(start):
        rows = [lax.dynamic_slice_in_dim(w, start, width, 0) for w in (gate_panel, up_panel)]
        return lax.dot_general(gate_grad, rows[0], back, preferred_element_type=f32) + lax.dot_general(
            up_grad, rows[1], back, preferred_element_type=f32
        )

    arrived = swapped(slot_part(there).astype(bf16))
    summed = (slot_part(here) + arrived.astype(f32)).astype(bf16)
    returned = exchange(summed.reshape(experts, capacity, width)).reshape(slots, width)
    share = lax.dot_general(place, returned, (((0,), (0,)), ((), ())), preferred_element_type=f32).astype(bf16)
    grad_tokens = joined(share, swapped(share))
    outer = (((0,), (0,)), ((), ()))
    grad_down = lax.dot_general(dy_rows, activation, outer, preferred_element_type=f32).astype(bf16)
    grad_gate = lax.dot_general(rows_in, gate_grad, outer, preferred_element_type=f32).astype(bf16)
    grad_up = lax.dot_general(rows_in, up_grad, outer, preferred_element_type=f32).astype(bf16)
    return (grad_gate[None], grad_up[None], grad_down[None], grad_tokens)


f32, bf16 = jnp.float32, jnp.bfloat16
MESH = pl.DeviceIdType.MESH


def dense_kernel(
    experts, capacity,
    ids_ref, probs_ref, x_ref, dy_ref, gate_ref, up_ref, down_ref,
    grad_gate_ref, grad_up_ref, grad_down_ref, grad_tokens_ref,
    info, info_all, gu, dn, tok, nbr_out, rows, pls, pre, act, activ, gg,
    mine, cs_out, cs_in, comb, s_out, t_own, t_out, xr, z_out, z_in, stage, fin,
    local_sem, info_send, info_recv, w_send, w_recv, w_own,
    ag_up, ag_down, ag_zr, ag_xs, ag_xr, y_send, y_recv, c_send, c_recv,
    cs_send, cs_recv, ys_send, ys_recv, xs_send, xs_recv, zs_send, zs_recv, out_sem, fin_sem,
):
    me, core = lax.axis_index("expert"), lax.axis_index("dp")
    planes = experts // 4
    z, y, x = me // 4, (me // 2) % 2, me % 2
    x_peer, y_peer = me + 1 - 2 * x, me + 2 - 4 * y
    tok_rows, model_width = x_ref.shape
    width = model_width // 2
    hid = gate_ref.shape[2]
    pair = 2 * capacity
    quad = 4 * capacity
    slots = experts * capacity
    slab = model_width // planes
    here = pl.multiple_of(core * width, width)
    batch0 = (((0,), (0,)), ((), ()))

    def remote(src, dst, send, recv, expert=None):
        target = {"dp": 1 - core} if expert is None else {"expert": expert}
        return pltpu.make_async_remote_copy(
            src_ref=src, dst_ref=dst, send_sem=send, recv_sem=recv, device_id=target, device_id_type=MESH
        )

    def at(start, size):
        return pl.ds(pl.multiple_of(start, size), size)

    def peer_of(k):
        return lax.rem(me + k, experts)

    barrier = pltpu.get_barrier_semaphore()

    def greet(k, carry):
        pl.semaphore_signal(barrier, inc=1, device_id={"expert": peer_of(k)}, device_id_type=MESH)
        return carry

    lax.fori_loop(1, experts, greet, 0)
    pl.semaphore_signal(barrier, inc=1, device_id={"dp": 1 - core}, device_id_type=MESH)

    own_copies = []
    for a, ref in enumerate((x_ref, dy_ref)):
        own_copies.append(
            pltpu.make_async_copy(ref.at[:, pl.ds(here, width)], tok.at[a, z, at(x * tok_rows, tok_rows), :], local_sem.at[a])
        )
    own_rows = at((me % 4) * tok_rows, tok_rows)
    own_panels = [
        pltpu.make_async_copy(gate_ref.at[me], gu.at[z, own_rows, pl.ds(0, hid)], w_own.at[0]),
        pltpu.make_async_copy(up_ref.at[me], gu.at[z, own_rows, pl.ds(hid, hid)], w_own.at[1]),
        pltpu.make_async_copy(down_ref.at[me], dn.at[z, own_rows, :], w_own.at[2]),
    ]
    for copy in own_copies:
        copy.start()
    for copy in own_panels:
        copy.start()
    pl.semaphore_wait(barrier, experts)

    def w_copy(w, target, owner):
        spot = at((owner % 4) * tok_rows, tok_rows)
        if w == 0:
            src, dst = gate_ref, gu.at[owner // 4, spot, pl.ds(0, hid)]
        elif w == 1:
            src, dst = up_ref, gu.at[owner // 4, spot, pl.ds(hid, hid)]
        else:
            src, dst = down_ref, dn.at[owner // 4, spot, :]
        return remote(src.at[target], dst, w_send.at[w, target], w_recv.at[w, owner], target)

    def start_panel(w, first, last):
        def body(k, carry):
            w_copy(w, peer_of(k), me).start()
            return carry

        lax.fori_loop(first, last, body, 0)

    def wait_panel(w, source):
        w_copy(w, source, source).wait_recv()

    def tok_block(a, zs, xs):
        return tok.at[a, zs, at(xs * tok_rows, tok_rows), :]

    def ag_copy(a, zs, direction):
        block = tok_block(a, zs, x)
        if direction == 0:
            return remote(block, block, ag_up.at[a, zs], ag_zr.at[a, zs], me + 4)
        if direction == 1:
            return remote(block, block, ag_down.at[a, zs], ag_zr.at[a, zs], me - 4)
        return remote(block, block, ag_xs.at[a, zs], ag_xr.at[a, zs], x_peer)

    def walk(t):
        return z + ((t + 1) // 2) * (1 - 2 * (t % 2))

    def inside(zs):
        return jnp.logical_and(zs >= 0, zs < planes)

    def forwards(zs):
        return (
            jnp.logical_and(zs <= z, z < planes - 1),
            jnp.logical_and(zs >= z, z > 0),
        )

    def send_block(a, zs):
        go_up, go_down = forwards(zs)

        @pl.when(go_up)
        def _():
            ag_copy(a, zs, 0).start()

        @pl.when(go_down)
        def _():
            ag_copy(a, zs, 1).start()

        ag_copy(a, zs, 2).start()

    for a in range(2):
        own_copies[a].wait()
        send_block(a, z)

    ids, probs = ids_ref[...], probs_ref[...]
    named_by = lax.broadcasted_iota(jnp.int32, (experts,) + ids.shape, 0) == ids[None, :, :]
    weight = jnp.sum(jnp.where(named_by, probs[None, :, :], 0.0), axis=1)
    named = jnp.sum(jnp.where(named_by, 1.0, 0.0), axis=1)
    before = lax.broadcasted_iota(jnp.int32, (tok_rows, tok_rows), 0) < lax.broadcasted_iota(
        jnp.int32, (tok_rows, tok_rows), 1
    )
    rank = jnp.dot(named.astype(bf16), jnp.where(before, 1.0, 0.0).astype(bf16), preferred_element_type=f32)
    rank = jnp.where(named > 0.5, rank + (x * capacity).astype(f32), -1.0)
    line = lax.broadcasted_iota(jnp.int32, (experts, 8, tok_rows), 1)
    info[...] = jnp.where(line == 0, rank[:, None, :], weight[:, None, :])
    info_all[me] = info[at(z * 4, 4)]

    def info_copy(target, owner):
        return remote(
            info.at[at((target // 4) * 4, 4)], info_all.at[owner], info_send.at[target], info_recv.at[owner], target
        )

    def send_info(k, carry):
        info_copy(peer_of(k), me).start()
        return carry

    lax.fori_loop(1, experts, send_info, 0)
    start_panel(0, 1, experts)

    def wait_info(k, carry):
        source = peer_of(k)
        info_copy(source, source).wait_recv()
        return carry

    lax.fori_loop(1, experts, wait_info, 0)

    def pair_rows(zs, ys):
        return at((2 * zs + ys) * pair, pair)

    def places(zs, expert_index):
        first = 4 * zs + 2 * y
        both = jnp.concatenate(
            [info_all[first, expert_index, :, :], info_all[first + 1, expert_index, :, :]], axis=1
        )
        hit = both[0:1, :] == lax.broadcasted_iota(jnp.int32, (pair, 2 * tok_rows), 0).astype(f32)
        prob = jnp.sum(jnp.where(hit, both[1:2, :], 0.0), axis=1, keepdims=True)
        return jnp.where(hit, 1.0, 0.0).astype(bf16), prob

    def y_copy(a, zs, ys):
        return remote(
            nbr_out.at[a, zs], rows.at[a, core, pair_rows(zs, ys), :], y_send.at[a, zs], y_recv.at[a, zs], y_peer
        )

    def core_copy(a, half, zs, ys):
        block = rows.at[a, half, pair_rows(zs, ys), :]
        return remote(block, block, c_send.at[a, 2 * zs + ys], c_recv.at[a, 2 * zs + ys])

    mine_q = me % 4
    peer_q = y_peer % 4

    def gather(zs):
        own_place, own_prob = places(zs, mine_q)
        nbr_place, nbr_prob = places(zs, peer_q)
        pls[zs, pl.ds(0, pair), :] = own_place
        pls[zs, pl.ds(pair, pair), :] = nbr_place
        for a in range(2):
            ag_copy(a, zs, 2).wait_recv()
            got = jnp.dot(own_place, tok[a, zs], preferred_element_type=f32)
            lent = jnp.dot(nbr_place, tok[a, zs], preferred_element_type=f32)
            if a == 1:
                got, lent = got * own_prob, lent * nbr_prob
            nbr_out[a, zs] = lent.astype(bf16)
            y_copy(a, zs, y).start()
            rows[a, core, pair_rows(zs, y), :] = got.astype(bf16)
            core_copy(a, core, zs, y).start()

    hops = 2 * planes - 2
    others = experts - 1

    def spread(t, carry):
        zs, ready = walk(t), walk(t - 1)

        @pl.when(jnp.logical_and(t <= hops, inside(zs)))
        def _():
            for a in range(2):
                remote(tok_block(a, zs, x), tok_block(a, zs, x), ag_up.at[a, zs], ag_zr.at[a, zs], x_peer).wait_recv()
                send_block(a, zs)

        @pl.when(t < planes)
        def _():
            start_panel(1, 1 + (t - 1) * others // (planes - 1), 1 + t * others // (planes - 1))

        @pl.when(t >= planes)
        def _():
            start_panel(2, 1 + (t - planes) * others // planes, 1 + (t - planes + 1) * others // planes)

        @pl.when(inside(ready))
        def _():
            gather(ready)

        return carry

    lax.fori_loop(1, hops + 2, spread, 0)

    def pass_on(t, carry):
        zs = walk(t)

        @pl.when(inside(zs))
        def _():
            for a in range(2):
                y_copy(a, zs, 1 - y).wait_recv()
                core_copy(a, core, zs, 1 - y).start()

        return carry

    lax.fori_loop(0, hops + 1, pass_on, 0)

    def wait_core(p, carry):
        for a in range(2):
            core_copy(a, 1 - core, p // 2, p % 2).wait_recv()
        return carry

    lax.fori_loop(0, 2 * planes, wait_core, 0)
    for w in range(2):
        own_panels[w].wait()

        def wait_gu(k, carry):
            wait_panel(w, peer_of(k))
            return carry

        lax.fori_loop(1, experts, wait_gu, 0)

    def slab_of(a, g, spot):
        half, off = (g * slab) // width, (g * slab) % width
        return rows[a, half, spot, pl.ds(off, slab)]

    def forward(m, carry):
        spot = at(m * quad, quad)
        total = jnp.dot(slab_of(0, 0, spot), gu[0], preferred_element_type=f32)
        for g in range(1, planes):
            total += jnp.dot(slab_of(0, g, spot), gu[g], preferred_element_type=f32)
        pre[spot, :] = total
        return carry

    lax.fori_loop(0, planes, forward, 0)
    own_panels[2].wait()
    for g in range(planes):
        for q in range(4):
            source = 4 * g + q

            @pl.when(source != me)
            def _():
                wait_panel(2, source)

        def backward(m, carry):
            spot = at(m * quad, quad)
            part = jnp.dot(slab_of(1, g, spot), dn[g], preferred_element_type=f32)
            if g == 0:
                act[spot, :] = part
            else:
                act[spot, :] += part
            return carry

        lax.fori_loop(0, planes, backward, 0)

    def pointwise(m, carry):
        spot = at(m * 16, 16)
        gate_pre, up_pre, act_grad = pre[spot, pl.ds(0, hid)], pre[spot, pl.ds(hid, hid)], act[spot, :]
        sig = jax.nn.sigmoid(gate_pre)
        activ[spot, :] = (gate_pre * sig * up_pre).astype(bf16)
        gg[spot, pl.ds(0, hid)] = (act_grad * up_pre * sig * (1.0 + gate_pre * (1.0 - sig))).astype(bf16)
        gg[spot, pl.ds(hid, hid)] = (act_grad * gate_pre * sig).astype(bf16)
        return carry

    back = (((1,), (1,)), ((), ()))
    half_planes = planes // 2

    def cs_copy(d):
        return remote(cs_out.at[d], cs_in.at[d], cs_send.at[d], cs_recv.at[d])

    def ys_copy(d):
        return remote(s_out.at[d], comb.at[d, pl.ds(pair, pair), :], ys_send.at[d], ys_recv.at[d], y_peer)

    def xs_copy(d):
        return remote(t_out.at[d], xr.at[d], xs_send.at[d], xs_recv.at[d], x_peer)

    def slot_step(d):
        lax.fori_loop(d * (quad // 16), (d + 1) * (quad // 16), pointwise, 0)
        spot = pl.ds(d * quad, quad)
        for i in range(half_planes):
            there = (1 - core) * half_planes + i
            cs_out[d, :, pl.ds(i * slab, slab)] = lax.dot_general(
                gg[spot, :], gu[there], back, preferred_element_type=f32
            ).astype(bf16)
        cs_copy(d).start()
        for i in range(half_planes):
            mine[d, :, pl.ds(i * slab, slab)] = lax.dot_general(
                gg[spot, :], gu[core * half_planes + i], back, preferred_element_type=f32
            )

    def slot_sum(d):
        cs_copy(d).wait_recv()
        away, home = at((1 - y) * pair, pair), at(y * pair, pair)
        s_out[d] = (mine[d, away, :] + cs_in[d, away, :].astype(f32)).astype(bf16)
        ys_copy(d).start()
        comb[d, pl.ds(0, pair), :] = (mine[d, home, :] + cs_in[d, home, :].astype(f32)).astype(bf16)

    def token_step(d):
        ys_copy(d).wait_recv()
        t_out[d] = lax.dot_general(
            pls[d, :, at((1 - x) * tok_rows, tok_rows)], comb[d], batch0, preferred_element_type=f32
        ).astype(bf16)
        xs_copy(d).start()
        t_own[d] = lax.dot_general(
            pls[d, :, at(x * tok_rows, tok_rows)], comb[d], batch0, preferred_element_type=f32
        )

    def z_copy(d, up):
        if up:
            return remote(z_out.at[d], z_in.at[0, d], zs_send.at[d], zs_recv.at[0, d], me + 4)
        return remote(z_out.at[d], z_in.at[1, d], zs_send.at[d], zs_recv.at[1, d], me - 4)

    def z_take(d, side):
        remote(z_out.at[d], z_in.at[side, d], zs_send.at[d], zs_recv.at[side, d], x_peer).wait_recv()
        t_own[d] += z_in[side, d].astype(f32)

    def z_step(d):
        xs_copy(d).wait_recv()
        t_own[d] += xr[d].astype(f32)

        @pl.when(jnp.logical_and(d > z, z > 0))
        def _():
            z_take(d, 0)

        @pl.when(jnp.logical_and(d < z, z < planes - 1))
        def _():
            z_take(d, 1)

        @pl.when(d > z)
        def _():
            z_out[d] = t_own[d].astype(bf16)
            z_copy(d, True).start()

        @pl.when(d < z)
        def _():
            z_out[d] = t_own[d].astype(bf16)
            z_copy(d, False).start()

    tile = width // 4

    def out_copy(w, i):
        span = at(i * tile, tile)
        return pltpu.make_async_copy(
            stage.at[w, span, :], (grad_gate_ref, grad_up_ref, grad_down_ref)[w].at[span, :], out_sem.at[w, i]
        )

    def weight_grads(first, last):
        def body(i, carry):
            half, off, span = i // 4, at((i % 4) * tile, tile), at(i * tile, tile)
            both = lax.dot_general(rows[0, half, :, off], gg[...], batch0, preferred_element_type=f32)
            stage[0, span, :] = both[:, :hid].astype(bf16)
            stage[1, span, :] = both[:, hid:].astype(bf16)
            stage[2, span, :] = lax.dot_general(
                rows[1, half, :, off], activ[...], batch0, preferred_element_type=f32
            ).astype(bf16)
            for w in range(3):
                out_copy(w, i).start()
            return carry

        lax.fori_loop(first, last, body, 0)

    order = []
    for i in range(half_planes):
        order += [i, planes - 1 - i]
    for i, d in enumerate(order):
        slot_step(d)
        if i > 0:
            slot_sum(order[i - 1])
    slot_sum(order[-1])
    weight_grads(0, 3)
    token_step(order[0])
    weight_grads(3, 6)
    for i in range(1, planes):
        token_step(order[i])
        d = order[i - 1]

        @pl.when(d != z)
        def _():
            z_step(d)

        if i == 1:
            weight_grads(6, 8)

    @pl.when(order[-1] != z)
    def _():
        z_step(order[-1])

    xs_copy(z).wait_recv()
    t_own[z] += xr[z].astype(f32)

    @pl.when(z > 0)
    def _():
        z_take(z, 0)

    @pl.when(z < planes - 1)
    def _():
        z_take(z, 1)

    fin[...] = t_own[z].astype(bf16)
    home_spot = grad_tokens_ref.at[:, pl.ds(here, width)]
    last = remote(fin, home_spot, fin_sem.at[0], fin_sem.at[1])
    last.start()
    keep = pltpu.make_async_copy(fin, home_spot, fin_sem.at[2])
    keep.start()

    def drain_peers(k, carry):
        target = peer_of(k)
        for w in range(3):
            w_copy(w, target, me).wait_send()
        info_copy(target, me).wait_send()
        return carry

    lax.fori_loop(1, experts, drain_peers, 0)

    def drain_tokens(zs, carry):
        go_up, go_down = forwards(zs)
        for a in range(2):

            @pl.when(go_up)
            def _():
                ag_copy(a, zs, 0).wait_send()

            @pl.when(go_down)
            def _():
                ag_copy(a, zs, 1).wait_send()

            ag_copy(a, zs, 2).wait_send()
            y_copy(a, zs, y).wait_send()
            for ys in range(2):
                core_copy(a, core, zs, ys).wait_send()
        cs_copy(zs).wait_send()
        ys_copy(zs).wait_send()
        xs_copy(zs).wait_send()

        @pl.when(zs > z)
        def _():
            z_copy(zs, True).wait_send()

        @pl.when(zs < z)
        def _():
            z_copy(zs, False).wait_send()

        return carry

    lax.fori_loop(0, planes, drain_tokens, 0)

    def drain_out(i, carry):
        for w in range(3):
            out_copy(w, i).wait()
        return carry

    lax.fori_loop(0, 8, drain_out, 0)
    keep.wait()
    last.wait()


def placed_dense(tokens, out_grad, route_ids, route_probs, gate_store, up_store, down_store):
    tok_rows, model_width = tokens.shape
    top_count = route_ids.shape[1]
    experts, _, hid = gate_store.shape
    capacity = 9 * tok_rows * top_count // (8 * experts)
    slots, width, planes = experts * capacity, model_width // 2, experts // 4
    pair, quad, slab = 2 * capacity, 4 * capacity, model_width // planes
    vmem, dma = pltpu.VMEM, pltpu.SemaphoreType.DMA
    anywhere, on_chip = pl.BlockSpec(memory_space=pl.ANY), pl.BlockSpec(memory_space=pltpu.VMEM)
    scratch = [
        vmem((experts, 8, tok_rows), f32),
        vmem((experts, 4, 8, tok_rows), f32),
        vmem((planes, slab, 2 * hid), bf16),
        vmem((planes, slab, hid), bf16),
        vmem((2, planes, 2 * tok_rows, width), bf16),
        vmem((2, planes, pair, width), bf16),
        vmem((2, 2, slots, width), bf16),
        vmem((planes, quad, 2 * tok_rows), bf16),
        vmem((slots, 2 * hid), f32),
        vmem((slots, hid), f32),
        vmem((slots, hid), bf16),
        vmem((slots, 2 * hid), bf16),
        vmem((planes, quad, width), f32),
        vmem((planes, quad, width), bf16),
        vmem((planes, quad, width), bf16),
        vmem((planes, quad, width), bf16),
        vmem((planes, pair, width), bf16),
        vmem((planes, tok_rows, width), f32),
        vmem((planes, tok_rows, width), bf16),
        vmem((planes, tok_rows, width), bf16),
        vmem((planes, tok_rows, width), bf16),
        vmem((2, planes, tok_rows, width), bf16),
        vmem((3, model_width, hid), bf16),
        vmem((tok_rows, width), bf16),
        dma((2,)), dma((experts,)), dma((experts,)), dma((3, experts)), dma((3, experts)), dma((3,)),
        dma((2, planes)), dma((2, planes)), dma((2, planes)), dma((2, planes)), dma((2, planes)),
        dma((2, planes)), dma((2, planes)), dma((2, 2 * planes)), dma((2, 2 * planes)),
        dma((planes,)), dma((planes,)), dma((planes,)), dma((planes,)),
        dma((planes,)), dma((planes,)), dma((planes,)), dma((2, planes)), dma((3, 8)), dma((3,)),
    ]
    grad = jax.ShapeDtypeStruct((model_width, hid), bf16)
    outs = pl.pallas_call(
        functools.partial(dense_kernel, experts, capacity),
        out_shape=(grad, grad, grad, jax.ShapeDtypeStruct((tok_rows, model_width), bf16)),
        in_specs=[on_chip, on_chip] + [anywhere] * 5,
        out_specs=(anywhere,) * 4,
        scratch_shapes=scratch,
        compiler_params=pltpu.CompilerParams(
            collective_id=0, has_side_effects=True, vmem_limit_bytes=60 * 1024 * 1024
        ),
    )(route_ids.T, route_probs.T, tokens, out_grad, gate_store, up_store, down_store)
    return (outs[0][None], outs[1][None], outs[2][None], outs[3])


def placed(tokens, out_grad, route_ids, route_probs, gate_store, up_store, down_store):
    experts, top_count = lax.axis_size("expert"), route_ids.shape[1]
    capacity = 9 * tokens.shape[0] * top_count // (8 * experts)
    dense = 4 * top_count >= experts and experts % 8 == 0 and capacity % 8 == 0
    body = placed_dense if dense else placed_sparse
    return body(tokens, out_grad, route_ids, route_probs, gate_store, up_store, down_store)


def solution(mesh):
    return jax.shard_map(
        placed,
        mesh=mesh,
        in_specs=(
            P("expert", None),
            P("expert", None),
            P("expert", None),
            P("expert", None),
            P(None, "expert", "dp"),
            P(None, "expert", "dp"),
            P(None, "expert", "dp"),
        ),
        out_specs=(
            P("expert", None, "dp"),
            P("expert", None, "dp"),
            P("expert", None, "dp"),
            P("expert", None),
        ),
        check_vma=False,
    )
```

```python
import functools

import jax
import jax.numpy as jnp
from jax import lax
from jax.experimental import pallas as pl
from jax.experimental.pallas import tpu as pltpu
from jax.sharding import PartitionSpec as P


def joined(own, other):
    first = lax.axis_index("dp") == 0
    return jnp.where(first, jnp.concatenate([own, other], -1), jnp.concatenate([other, own], -1))


def swapped(part):
    return lax.ppermute(part, "dp", [(0, 1), (1, 0)])


def placed_sparse(tokens, out_grad, route_ids, route_probs, gate_store, up_store, down_store):
    tok_rows, model_width = tokens.shape
    top_count = route_ids.shape[1]
    experts = lax.axis_size("expert")
    capacity = max(2, 9 * tok_rows * top_count // (8 * experts))
    slots = experts * capacity
    width = model_width // 2
    here = lax.axis_index("dp") * width
    there = width - here
    f32, bf16 = jnp.float32, jnp.bfloat16

    chosen = route_ids[:, :, None] == jnp.arange(experts, dtype=jnp.int32)[None, None, :]
    weight = jnp.sum(jnp.where(chosen, route_probs[:, :, None], 0.0), axis=1)
    named = jnp.any(chosen, axis=1)
    earlier = jnp.arange(tok_rows)[:, None] > jnp.arange(tok_rows)[None, :]
    rank = jnp.dot(earlier.astype(bf16), named.astype(bf16), preferred_element_type=f32)
    rank = jnp.where(named, rank, -1.0)
    hit = rank.T[:, None, :] == jnp.arange(capacity, dtype=f32)[None, :, None]
    slot_prob = jnp.sum(jnp.where(hit, weight.T[:, None, :], 0.0), axis=2)
    place = hit.astype(bf16).reshape(slots, tok_rows)

    x_part = jnp.dot(
        place, lax.dynamic_slice_in_dim(tokens, here, width, 1), preferred_element_type=f32
    ).astype(bf16)
    dy_part = (
        jnp.dot(place, lax.dynamic_slice_in_dim(out_grad, here, width, 1), preferred_element_type=f32)
        * slot_prob.reshape(slots, 1)
    ).astype(bf16)

    def exchange(a):
        return lax.all_to_all(a, "expert", split_axis=0, concat_axis=0, tiled=True)

    def panel(store):
        return lax.all_to_all(store, "expert", split_axis=0, concat_axis=1, tiled=True)[0]

    x_own = exchange(x_part.reshape(experts, capacity, width)).reshape(slots, width)
    gate_panel = panel(gate_store)
    up_panel = panel(up_store)
    dy_own = exchange(dy_part.reshape(experts, capacity, width)).reshape(slots, width)
    down_panel = panel(down_store)
    rows_in = joined(x_own, swapped(x_own))
    dy_rows = joined(dy_own, swapped(dy_own))
    gate_pre = jnp.dot(rows_in, gate_panel, preferred_element_type=f32)
    up_pre = jnp.dot(rows_in, up_panel, preferred_element_type=f32)
    sig = jax.nn.sigmoid(gate_pre)
    activation = (gate_pre * sig * up_pre).astype(bf16)
    act_grad = jnp.dot(dy_rows, down_panel, preferred_element_type=f32)
    up_grad = (act_grad * gate_pre * sig).astype(bf16)
    gate_grad = (act_grad * up_pre * sig * (1.0 + gate_pre * (1.0 - sig))).astype(bf16)
    back = (((1,), (1,)), ((), ()))

    def slot_part(start):
        rows = [lax.dynamic_slice_in_dim(w, start, width, 0) for w in (gate_panel, up_panel)]
        return lax.dot_general(gate_grad, rows[0], back, preferred_element_type=f32) + lax.dot_general(
            up_grad, rows[1], back, preferred_element_type=f32
        )

    arrived = swapped(slot_part(there).astype(bf16))
    summed = (slot_part(here) + arrived.astype(f32)).astype(bf16)
    returned = exchange(summed.reshape(experts, capacity, width)).reshape(slots, width)
    share = lax.dot_general(place, returned, (((0,), (0,)), ((), ())), preferred_element_type=f32).astype(bf16)
    grad_tokens = joined(share, swapped(share))
    outer = (((0,), (0,)), ((), ()))
    grad_down = lax.dot_general(dy_rows, activation, outer, preferred_element_type=f32).astype(bf16)
    grad_gate = lax.dot_general(rows_in, gate_grad, outer, preferred_element_type=f32).astype(bf16)
    grad_up = lax.dot_general(rows_in, up_grad, outer, preferred_element_type=f32).astype(bf16)
    return (grad_gate[None], grad_up[None], grad_down[None], grad_tokens)


f32, bf16 = jnp.float32, jnp.bfloat16
MESH = pl.DeviceIdType.MESH
CUTS = 2
Y_LAG, X_LAG, HOP_LAG = 6, 2, 2


def dense_kernel(
    experts, capacity,
    ids_ref, probs_ref, x_ref, dy_ref, gate_ref, up_ref, down_ref,
    grad_gate_ref, grad_up_ref, grad_down_ref, grad_tokens_ref,
    info, info_all, gu, dn, tok, nbr_out, rows, pls, pre, act, activ, gg,
    mine, cs_out, cs_in, comb, s_out, t_own, t_out, xr, z_out, z_in, stage, fin,
    local_sem, info_send, info_recv, w_send, w_recv, w_own,
    ag_up, ag_down, ag_zr, ag_xs, ag_xr, y_send, y_recv, c_send, c_recv,
    cs_send, cs_recv, ys_send, ys_recv, xs_send, xs_recv, zs_send, zs_recv, out_sem, fin_send, fin_recv, fin_keep,
):
    me, core = lax.axis_index("expert"), lax.axis_index("dp")
    planes = experts // 4
    z, y, x = me // 4, (me // 2) % 2, me % 2
    x_peer, y_peer = me + 1 - 2 * x, me + 2 - 4 * y
    tok_rows, model_width = x_ref.shape
    width = model_width // 2
    hid = gate_ref.shape[2]
    pair = 2 * capacity
    quad = 4 * capacity
    slots = experts * capacity
    slab = model_width // planes
    here = pl.multiple_of(core * width, width)
    batch0 = (((0,), (0,)), ((), ()))

    def remote(src, dst, send, recv, expert=None):
        target = {"dp": 1 - core} if expert is None else {"expert": expert}
        return pltpu.make_async_remote_copy(
            src_ref=src, dst_ref=dst, send_sem=send, recv_sem=recv, device_id=target, device_id_type=MESH
        )

    def at(start, size):
        return pl.ds(pl.multiple_of(start, size), size)

    def peer_of(k):
        return lax.rem(me + k, experts)

    barrier = pltpu.get_barrier_semaphore()

    def greet(k, carry):
        pl.semaphore_signal(barrier, inc=1, device_id={"expert": peer_of(k)}, device_id_type=MESH)
        return carry

    lax.fori_loop(1, experts, greet, 0)
    pl.semaphore_signal(barrier, inc=1, device_id={"dp": 1 - core}, device_id_type=MESH)

    own_copies = []
    for a, ref in enumerate((x_ref, dy_ref)):
        own_copies.append(
            pltpu.make_async_copy(ref.at[:, pl.ds(here, width)], tok.at[a, z, at(x * tok_rows, tok_rows), :], local_sem.at[a])
        )
    own_rows = at((me % 4) * tok_rows, tok_rows)
    own_panels = [
        pltpu.make_async_copy(gate_ref.at[me], gu.at[z, own_rows, pl.ds(0, hid)], w_own.at[0]),
        pltpu.make_async_copy(up_ref.at[me], gu.at[z, own_rows, pl.ds(hid, hid)], w_own.at[1]),
        pltpu.make_async_copy(down_ref.at[me], dn.at[z, own_rows, :], w_own.at[2]),
    ]
    for copy in own_copies:
        copy.start()
    for copy in own_panels:
        copy.start()
    pl.semaphore_wait(barrier, experts)

    def w_copy(w, target, owner):
        spot = at((owner % 4) * tok_rows, tok_rows)
        if w == 0:
            src, dst = gate_ref, gu.at[owner // 4, spot, pl.ds(0, hid)]
        elif w == 1:
            src, dst = up_ref, gu.at[owner // 4, spot, pl.ds(hid, hid)]
        else:
            src, dst = down_ref, dn.at[owner // 4, spot, :]
        return remote(src.at[target], dst, w_send.at[w, target], w_recv.at[w, owner], target)

    def start_panel(w, first, last):
        def body(k, carry):
            w_copy(w, peer_of(k), me).start()
            return carry

        lax.fori_loop(first, last, body, 0)

    def wait_panel(w, source):
        w_copy(w, source, source).wait_recv()

    def tok_block(a, zs, xs):
        return tok.at[a, zs, at(xs * tok_rows, tok_rows), :]

    def ag_copy(a, zs, direction):
        block = tok_block(a, zs, x)
        if direction == 0:
            return remote(block, block, ag_up.at[a, zs], ag_zr.at[a, zs], me + 4)
        if direction == 1:
            return remote(block, block, ag_down.at[a, zs], ag_zr.at[a, zs], me - 4)
        return remote(block, block, ag_xs.at[a, zs], ag_xr.at[a, zs], x_peer)

    def walk(t):
        return z + ((t + 1) // 2) * (1 - 2 * (t % 2))

    def inside(zs):
        return jnp.logical_and(zs >= 0, zs < planes)

    def forwards(zs):
        return (
            jnp.logical_and(zs <= z, z < planes - 1),
            jnp.logical_and(zs >= z, z > 0),
        )

    def send_block(a, zs):
        go_up, go_down = forwards(zs)

        @pl.when(go_up)
        def _():
            ag_copy(a, zs, 0).start()

        @pl.when(go_down)
        def _():
            ag_copy(a, zs, 1).start()

        ag_copy(a, zs, 2).start()

    for a in range(2):
        own_copies[a].wait()
        send_block(a, z)

    ids, probs = ids_ref[...], probs_ref[...]
    named_by = lax.broadcasted_iota(jnp.int32, (experts,) + ids.shape, 0) == ids[None, :, :]
    weight = jnp.sum(jnp.where(named_by, probs[None, :, :], 0.0), axis=1)
    named = jnp.sum(jnp.where(named_by, 1.0, 0.0), axis=1)
    before = lax.broadcasted_iota(jnp.int32, (tok_rows, tok_rows), 0) < lax.broadcasted_iota(
        jnp.int32, (tok_rows, tok_rows), 1
    )
    rank = jnp.dot(named.astype(bf16), jnp.where(before, 1.0, 0.0).astype(bf16), preferred_element_type=f32)
    rank = jnp.where(named > 0.5, rank + (x * capacity).astype(f32), -1.0)
    line = lax.broadcasted_iota(jnp.int32, (experts, 8, tok_rows), 1)
    info[...] = jnp.where(line == 0, rank[:, None, :], weight[:, None, :])
    info_all[me] = info[at(z * 4, 4)]

    def info_copy(target, owner):
        return remote(
            info.at[at((target // 4) * 4, 4)], info_all.at[owner], info_send.at[target], info_recv.at[owner], target
        )

    def send_info(k, carry):
        info_copy(peer_of(k), me).start()
        return carry

    lax.fori_loop(1, experts, send_info, 0)
    start_panel(0, 1, experts)

    def wait_info(k, carry):
        source = peer_of(k)
        info_copy(source, source).wait_recv()
        return carry

    lax.fori_loop(1, experts, wait_info, 0)

    def pair_rows(zs, ys):
        return at((2 * zs + ys) * pair, pair)

    def places(zs, expert_index):
        first = 4 * zs + 2 * y
        both = jnp.concatenate(
            [info_all[first, expert_index, :, :], info_all[first + 1, expert_index, :, :]], axis=1
        )
        hit = both[0:1, :] == lax.broadcasted_iota(jnp.int32, (pair, 2 * tok_rows), 0).astype(f32)
        prob = jnp.sum(jnp.where(hit, both[1:2, :], 0.0), axis=1, keepdims=True)
        return jnp.where(hit, 1.0, 0.0).astype(bf16), prob

    def y_copy(a, zs, ys):
        return remote(
            nbr_out.at[a, zs], rows.at[a, core, pair_rows(zs, ys), :], y_send.at[a, zs], y_recv.at[a, zs], y_peer
        )

    def core_copy(a, half, zs, ys):
        block = rows.at[a, half, pair_rows(zs, ys), :]
        return remote(block, block, c_send.at[a, 2 * zs + ys], c_recv.at[a, 2 * zs + ys])

    mine_q = me % 4
    peer_q = y_peer % 4

    def gather(a, zs):
        own_place, own_prob = places(zs, mine_q)
        nbr_place, nbr_prob = places(zs, peer_q)
        if a == 0:
            pls[zs, pl.ds(0, pair), :] = own_place
            pls[zs, pl.ds(pair, pair), :] = nbr_place
        ag_copy(a, zs, 2).wait_recv()
        lent = jnp.dot(nbr_place, tok[a, zs], preferred_element_type=f32)
        if a == 1:
            lent = lent * nbr_prob
        nbr_out[a, zs] = lent.astype(bf16)
        y_copy(a, zs, y).start()
        got = jnp.dot(own_place, tok[a, zs], preferred_element_type=f32)
        if a == 1:
            got = got * own_prob
        rows[a, core, pair_rows(zs, y), :] = got.astype(bf16)
        core_copy(a, core, zs, y).start()

    hops = 2 * planes - 2
    others = experts - 1

    def spread(t, carry):
        zs, ready = walk(t), walk(t - 1)

        @pl.when(jnp.logical_and(t <= hops, inside(zs)))
        def _():
            for a in range(2):
                block = tok_block(a, zs, x)
                remote(block, block, ag_up.at[a, zs], ag_zr.at[a, zs], x_peer).wait_recv()
                send_block(a, zs)

        @pl.when(t < planes)
        def _():
            start_panel(1, 1 + (t - 1) * others // (planes - 1), 1 + t * others // (planes - 1))

        @pl.when(t >= planes)
        def _():
            start_panel(2, 1 + (t - planes) * others // planes, 1 + (t - planes + 1) * others // planes)

        @pl.when(inside(ready))
        def _():
            for a in range(2):
                gather(a, ready)

        return carry

    def collect(a):
        def pass_on(t, carry):
            zs = walk(t)

            @pl.when(inside(zs))
            def _():
                y_copy(a, zs, 1 - y).wait_recv()
                core_copy(a, core, zs, 1 - y).start()

            return carry

        lax.fori_loop(0, hops + 1, pass_on, 0)

        def wait_core(p, carry):
            core_copy(a, 1 - core, p // 2, p % 2).wait_recv()
            return carry

        lax.fori_loop(0, 2 * planes, wait_core, 0)

    lax.fori_loop(1, hops + 2, spread, 0)
    collect(0)
    for w in range(2):
        own_panels[w].wait()

        def wait_gu(k, carry):
            wait_panel(w, peer_of(k))
            return carry

        lax.fori_loop(1, experts, wait_gu, 0)

    def slab_of(a, g, spot):
        half, off = (g * slab) // width, (g * slab) % width
        return rows[a, half, spot, pl.ds(off, slab)]

    def forward(m, carry):
        spot = at(m * quad, quad)
        total = jnp.dot(slab_of(0, 0, spot), gu[0], preferred_element_type=f32)
        for g in range(1, planes):
            total += jnp.dot(slab_of(0, g, spot), gu[g], preferred_element_type=f32)
        pre[spot, :] = total
        return carry

    lax.fori_loop(0, planes, forward, 0)
    collect(1)
    own_panels[2].wait()
    for g in range(planes):
        for q in range(4):
            source = 4 * g + q

            @pl.when(source != me)
            def _():
                wait_panel(2, source)

        def backward(m, carry):
            spot = at(m * quad, quad)
            part = jnp.dot(slab_of(1, g, spot), dn[g], preferred_element_type=f32)
            if g == 0:
                act[spot, :] = part
            else:
                act[spot, :] += part
            return carry

        lax.fori_loop(0, planes, backward, 0)

    def pointwise(m, carry):
        spot = at(m * 16, 16)
        gate_pre, up_pre, act_grad = pre[spot, pl.ds(0, hid)], pre[spot, pl.ds(hid, hid)], act[spot, :]
        sig = jax.nn.sigmoid(gate_pre)
        activ[spot, :] = (gate_pre * sig * up_pre).astype(bf16)
        gg[spot, pl.ds(0, hid)] = (act_grad * up_pre * sig * (1.0 + gate_pre * (1.0 - sig))).astype(bf16)
        gg[spot, pl.ds(hid, hid)] = (act_grad * gate_pre * sig).astype(bf16)
        return carry

    back = (((1,), (1,)), ((), ()))
    chunk = width // CUTS
    pieces = planes * CUTS

    upper = (2 * z) // planes
    near = z + upper * (planes - 1 - 2 * z)
    far_count = planes - 1 - 2 * near

    def plane_of(c):
        i = c // CUTS
        j = i - far_count
        close = (j + planes) // planes
        swing = (2 * near - j // 2) * (1 - j % 2) + (j // 2) * (j % 2)
        d = close * swing + (1 - close) * (planes - 1 - i)
        return d + upper * (planes - 1 - 2 * d)

    def cs_copy(d, i):
        return remote(cs_out.at[d, i], cs_in.at[d, i], cs_send.at[d, i], cs_recv.at[d, i])

    def ys_copy(d, i):
        return remote(s_out.at[d, i], comb.at[d, i, pl.ds(pair, pair), :], ys_send.at[d, i], ys_recv.at[d, i], y_peer)

    def xs_copy(d, i):
        return remote(t_out.at[d, i], xr.at[d, i], xs_send.at[d, i], xs_recv.at[d, i], x_peer)

    def weight_rows(half, i):
        start = half * width + i * chunk
        return gu[start // slab, at(start % slab, chunk), :]

    def slot_step(d, i):
        @pl.when(i == 0)
        def _():
            lax.fori_loop(d * (quad // 16), (d + 1) * (quad // 16), pointwise, 0)

        spot = at(d * quad, quad)
        cs_out[d, i] = lax.dot_general(
            gg[spot, :], weight_rows(1 - core, i), back, preferred_element_type=f32
        ).astype(bf16)
        cs_copy(d, i).start()
        mine[d, i] = lax.dot_general(gg[spot, :], weight_rows(core, i), back, preferred_element_type=f32)

    def slot_sum(d, i):
        cs_copy(d, i).wait_recv()
        away, home = at((1 - y) * pair, pair), at(y * pair, pair)
        s_out[d, i] = (mine[d, i, away, :] + cs_in[d, i, away, :].astype(f32)).astype(bf16)
        ys_copy(d, i).start()
        comb[d, i, pl.ds(0, pair), :] = (mine[d, i, home, :] + cs_in[d, i, home, :].astype(f32)).astype(bf16)

    def token_step(d, i):
        ys_copy(d, i).wait_recv()
        t_out[d, i] = lax.dot_general(
            pls[d, :, at((1 - x) * tok_rows, tok_rows)], comb[d, i], batch0, preferred_element_type=f32
        ).astype(bf16)
        xs_copy(d, i).start()
        t_own[d, i] = lax.dot_general(
            pls[d, :, at(x * tok_rows, tok_rows)], comb[d, i], batch0, preferred_element_type=f32
        )

    def z_copy(d, i, up):
        if up:
            return remote(z_out.at[d, i], z_in.at[0, d, i], zs_send.at[d, i], zs_recv.at[0, d, i], me + 4)
        return remote(z_out.at[d, i], z_in.at[1, d, i], zs_send.at[d, i], zs_recv.at[1, d, i], me - 4)

    def z_take(d, i, side):
        remote(
            z_out.at[d, i], z_in.at[side, d, i], zs_send.at[d, i], zs_recv.at[side, d, i], x_peer
        ).wait_recv()
        t_own[d, i] += z_in[side, d, i].astype(f32)

    def fin_copy(i):
        spot = grad_tokens_ref.at[:, pl.ds(pl.multiple_of(here + i * chunk, chunk), chunk)]
        return remote(fin.at[i], spot, fin_send.at[i], fin_recv.at[i]), pltpu.make_async_copy(
            fin.at[i], spot, fin_keep.at[i]
        )

    def z_step(d, i):
        xs_copy(d, i).wait_recv()
        t_own[d, i] += xr[d, i].astype(f32)

        @pl.when(jnp.logical_and(d >= z, z > 0))
        def _():
            z_take(d, i, 0)

        @pl.when(jnp.logical_and(d <= z, z < planes - 1))
        def _():
            z_take(d, i, 1)

        @pl.when(d != z)
        def _():
            z_out[d, i] = t_own[d, i].astype(bf16)

        @pl.when(d > z)
        def _():
            z_copy(d, i, True).start()

        @pl.when(d < z)
        def _():
            z_copy(d, i, False).start()

        @pl.when(d == z)
        def _():
            fin[i] = t_own[d, i].astype(bf16)
            out, keep = fin_copy(i)
            out.start()
            keep.start()

    tile = width // 4

    def out_copy(w, i):
        span = at(i * tile, tile)
        return pltpu.make_async_copy(
            stage.at[w, span, :], (grad_gate_ref, grad_up_ref, grad_down_ref)[w].at[span, :], out_sem.at[w, i]
        )

    def weight_grad(i):
        half, off, span = i // 4, at((i % 4) * tile, tile), at(i * tile, tile)
        both = lax.dot_general(rows[0, half, :, off], gg[...], batch0, preferred_element_type=f32)
        stage[0, span, :] = both[:, :hid].astype(bf16)
        stage[1, span, :] = both[:, hid:].astype(bf16)
        stage[2, span, :] = lax.dot_general(
            rows[1, half, :, off], activ[...], batch0, preferred_element_type=f32
        ).astype(bf16)
        for w in range(3):
            out_copy(w, i).start()

    def hop_lag(d):
        waits = jnp.logical_or(jnp.logical_and(d > z, upper == 0), jnp.logical_and(d < z, upper == 1))
        return X_LAG + jnp.where(waits, HOP_LAG * near, 0)

    steps = pieces + max(8, Y_LAG + X_LAG + max(0, HOP_LAG * (planes // 2 - 1) - CUTS))

    def ladder(s, carry):
        @pl.when(s < pieces)
        def _():
            slot_step(plane_of(s), s % CUTS)

        @pl.when(jnp.logical_and(s >= 1, s <= pieces))
        def _():
            slot_sum(plane_of(s - 1), (s - 1) % CUTS)

        @pl.when(jnp.logical_and(s >= Y_LAG, s < pieces + Y_LAG))
        def _():
            token_step(plane_of(s - Y_LAG), (s - Y_LAG) % CUTS)

        lag = Y_LAG + X_LAG

        def z_try(c, inner):
            d = plane_of(c)

            @pl.when(c + Y_LAG + hop_lag(d) == s)
            def _():
                z_step(d, c % CUTS)

            return inner

        @pl.when(s >= lag)
        def _():
            lax.fori_loop(0, pieces, z_try, 0)

        @pl.when(jnp.logical_and(s >= pieces, s < pieces + 8))
        def _():
            weight_grad(s - pieces)

        return carry

    lax.fori_loop(0, steps, ladder, 0)

    def drain_peers(k, carry):
        target = peer_of(k)
        for w in range(3):
            w_copy(w, target, me).wait_send()
        info_copy(target, me).wait_send()
        return carry

    lax.fori_loop(1, experts, drain_peers, 0)

    def drain_tokens(zs, carry):
        go_up, go_down = forwards(zs)
        for a in range(2):

            @pl.when(go_up)
            def _():
                ag_copy(a, zs, 0).wait_send()

            @pl.when(go_down)
            def _():
                ag_copy(a, zs, 1).wait_send()

            ag_copy(a, zs, 2).wait_send()
            y_copy(a, zs, y).wait_send()
            for ys in range(2):
                core_copy(a, core, zs, ys).wait_send()
        for i in range(CUTS):
            cs_copy(zs, i).wait_send()
            ys_copy(zs, i).wait_send()
            xs_copy(zs, i).wait_send()

            @pl.when(zs > z)
            def _():
                z_copy(zs, i, True).wait_send()

            @pl.when(zs < z)
            def _():
                z_copy(zs, i, False).wait_send()

        return carry

    lax.fori_loop(0, planes, drain_tokens, 0)

    def drain_out(i, carry):
        for w in range(3):
            out_copy(w, i).wait()
        return carry

    lax.fori_loop(0, 8, drain_out, 0)
    for i in range(CUTS):
        out, keep = fin_copy(i)
        keep.wait()
        out.wait()


def placed_dense(tokens, out_grad, route_ids, route_probs, gate_store, up_store, down_store):
    tok_rows, model_width = tokens.shape
    top_count = route_ids.shape[1]
    experts, _, hid = gate_store.shape
    capacity = 9 * tok_rows * top_count // (8 * experts)
    slots, width, planes = experts * capacity, model_width // 2, experts // 4
    pair, quad, slab = 2 * capacity, 4 * capacity, model_width // planes
    chunk = width // CUTS
    vmem, dma = pltpu.VMEM, pltpu.SemaphoreType.DMA
    anywhere, on_chip = pl.BlockSpec(memory_space=pl.ANY), pl.BlockSpec(memory_space=pltpu.VMEM)
    scratch = [
        vmem((experts, 8, tok_rows), f32),
        vmem((experts, 4, 8, tok_rows), f32),
        vmem((planes, slab, 2 * hid), bf16),
        vmem((planes, slab, hid), bf16),
        vmem((2, planes, 2 * tok_rows, width), bf16),
        vmem((2, planes, pair, width), bf16),
        vmem((2, 2, slots, width), bf16),
        vmem((planes, quad, 2 * tok_rows), bf16),
        vmem((slots, 2 * hid), f32),
        vmem((slots, hid), f32),
        vmem((slots, hid), bf16),
        vmem((slots, 2 * hid), bf16),
        vmem((planes, CUTS, quad, chunk), f32),
        vmem((planes, CUTS, quad, chunk), bf16),
        vmem((planes, CUTS, quad, chunk), bf16),
        vmem((planes, CUTS, quad, chunk), bf16),
        vmem((planes, CUTS, pair, chunk), bf16),
        vmem((planes, CUTS, tok_rows, chunk), f32),
        vmem((planes, CUTS, tok_rows, chunk), bf16),
        vmem((planes, CUTS, tok_rows, chunk), bf16),
        vmem((planes, CUTS, tok_rows, chunk), bf16),
        vmem((2, planes, CUTS, tok_rows, chunk), bf16),
        vmem((3, model_width, hid), bf16),
        vmem((CUTS, tok_rows, chunk), bf16),
        dma((2,)), dma((experts,)), dma((experts,)), dma((3, experts)), dma((3, experts)), dma((3,)),
        dma((2, planes)), dma((2, planes)), dma((2, planes)), dma((2, planes)), dma((2, planes)),
        dma((2, planes)), dma((2, planes)), dma((2, 2 * planes)), dma((2, 2 * planes)),
        dma((planes, CUTS)), dma((planes, CUTS)), dma((planes, CUTS)), dma((planes, CUTS)),
        dma((planes, CUTS)), dma((planes, CUTS)), dma((planes, CUTS)), dma((2, planes, CUTS)),
        dma((3, 8)), dma((CUTS,)), dma((CUTS,)), dma((CUTS,)),
    ]
    grad = jax.ShapeDtypeStruct((model_width, hid), bf16)
    outs = pl.pallas_call(
        functools.partial(dense_kernel, experts, capacity),
        out_shape=(grad, grad, grad, jax.ShapeDtypeStruct((tok_rows, model_width), bf16)),
        in_specs=[on_chip, on_chip] + [anywhere] * 5,
        out_specs=(anywhere,) * 4,
        scratch_shapes=scratch,
        compiler_params=pltpu.CompilerParams(
            collective_id=0, has_side_effects=True, vmem_limit_bytes=60 * 1024 * 1024
        ),
    )(route_ids.T, route_probs.T, tokens, out_grad, gate_store, up_store, down_store)
    return (outs[0][None], outs[1][None], outs[2][None], outs[3])


def placed(tokens, out_grad, route_ids, route_probs, gate_store, up_store, down_store):
    experts, top_count = lax.axis_size("expert"), route_ids.shape[1]
    capacity = 9 * tokens.shape[0] * top_count // (8 * experts)
    dense = 4 * top_count >= experts and experts % 8 == 0 and capacity % 8 == 0
    body = placed_dense if dense else placed_sparse
    return body(tokens, out_grad, route_ids, route_probs, gate_store, up_store, down_store)


def solution(mesh):
    return jax.shard_map(
        placed,
        mesh=mesh,
        in_specs=(
            P("expert", None),
            P("expert", None),
            P("expert", None),
            P("expert", None),
            P(None, "expert", "dp"),
            P(None, "expert", "dp"),
            P(None, "expert", "dp"),
        ),
        out_specs=(
            P("expert", None, "dp"),
            P("expert", None, "dp"),
            P("expert", None, "dp"),
            P("expert", None),
        ),
        check_vma=False,
    )
```

```python
import functools

import jax
import jax.numpy as jnp
from jax import lax
from jax.experimental import pallas as pl
from jax.experimental.pallas import tpu as pltpu
from jax.sharding import PartitionSpec as P


def joined(own, other):
    first = lax.axis_index("dp") == 0
    return jnp.where(first, jnp.concatenate([own, other], -1), jnp.concatenate([other, own], -1))


def swapped(part):
    return lax.ppermute(part, "dp", [(0, 1), (1, 0)])


def placed_sparse(tokens, out_grad, route_ids, route_probs, gate_store, up_store, down_store):
    tok_rows, model_width = tokens.shape
    top_count = route_ids.shape[1]
    experts = lax.axis_size("expert")
    capacity = max(2, 9 * tok_rows * top_count // (8 * experts))
    slots = experts * capacity
    width = model_width // 2
    here = lax.axis_index("dp") * width
    there = width - here
    f32, bf16 = jnp.float32, jnp.bfloat16

    chosen = route_ids[:, :, None] == jnp.arange(experts, dtype=jnp.int32)[None, None, :]
    weight = jnp.sum(jnp.where(chosen, route_probs[:, :, None], 0.0), axis=1)
    named = jnp.any(chosen, axis=1)
    earlier = jnp.arange(tok_rows)[:, None] > jnp.arange(tok_rows)[None, :]
    rank = jnp.dot(earlier.astype(bf16), named.astype(bf16), preferred_element_type=f32)
    rank = jnp.where(named, rank, -1.0)
    hit = rank.T[:, None, :] == jnp.arange(capacity, dtype=f32)[None, :, None]
    slot_prob = jnp.sum(jnp.where(hit, weight.T[:, None, :], 0.0), axis=2)
    place = hit.astype(bf16).reshape(slots, tok_rows)

    x_part = jnp.dot(
        place, lax.dynamic_slice_in_dim(tokens, here, width, 1), preferred_element_type=f32
    ).astype(bf16)
    dy_part = (
        jnp.dot(place, lax.dynamic_slice_in_dim(out_grad, here, width, 1), preferred_element_type=f32)
        * slot_prob.reshape(slots, 1)
    ).astype(bf16)

    def exchange(a):
        return lax.all_to_all(a, "expert", split_axis=0, concat_axis=0, tiled=True)

    def panel(store):
        return lax.all_to_all(store, "expert", split_axis=0, concat_axis=1, tiled=True)[0]

    x_own = exchange(x_part.reshape(experts, capacity, width)).reshape(slots, width)
    gate_panel = panel(gate_store)
    up_panel = panel(up_store)
    dy_own = exchange(dy_part.reshape(experts, capacity, width)).reshape(slots, width)
    down_panel = panel(down_store)
    rows_in = joined(x_own, swapped(x_own))
    dy_rows = joined(dy_own, swapped(dy_own))
    gate_pre = jnp.dot(rows_in, gate_panel, preferred_element_type=f32)
    up_pre = jnp.dot(rows_in, up_panel, preferred_element_type=f32)
    sig = jax.nn.sigmoid(gate_pre)
    activation = (gate_pre * sig * up_pre).astype(bf16)
    act_grad = jnp.dot(dy_rows, down_panel, preferred_element_type=f32)
    up_grad = (act_grad * gate_pre * sig).astype(bf16)
    gate_grad = (act_grad * up_pre * sig * (1.0 + gate_pre * (1.0 - sig))).astype(bf16)
    back = (((1,), (1,)), ((), ()))

    def slot_part(start):
        rows = [lax.dynamic_slice_in_dim(w, start, width, 0) for w in (gate_panel, up_panel)]
        return lax.dot_general(gate_grad, rows[0], back, preferred_element_type=f32) + lax.dot_general(
            up_grad, rows[1], back, preferred_element_type=f32
        )

    arrived = swapped(slot_part(there).astype(bf16))
    summed = (slot_part(here) + arrived.astype(f32)).astype(bf16)
    returned = exchange(summed.reshape(experts, capacity, width)).reshape(slots, width)
    share = lax.dot_general(place, returned, (((0,), (0,)), ((), ())), preferred_element_type=f32).astype(bf16)
    grad_tokens = joined(share, swapped(share))
    outer = (((0,), (0,)), ((), ()))
    grad_down = lax.dot_general(dy_rows, activation, outer, preferred_element_type=f32).astype(bf16)
    grad_gate = lax.dot_general(rows_in, gate_grad, outer, preferred_element_type=f32).astype(bf16)
    grad_up = lax.dot_general(rows_in, up_grad, outer, preferred_element_type=f32).astype(bf16)
    return (grad_gate[None], grad_up[None], grad_down[None], grad_tokens)


f32, bf16 = jnp.float32, jnp.bfloat16
MESH = pl.DeviceIdType.MESH
CUTS = 2
FIRST, PACE = 4, 5
VMEM_BYTES = 56000 * 1024
Y_LAG, X_LAG, HOP_LAG = 6, 2, 2


def dense_kernel(
    experts, capacity,
    ids_ref, probs_ref, x_ref, dy_ref, gate_ref, up_ref, down_ref,
    grad_gate_ref, grad_up_ref, grad_down_ref, grad_tokens_ref,
    info, info_all, gu, dn, tok, nbr_out, rows, pls, pre, act, activ, gg,
    mine, cs_out, cs_in, comb, s_out, t_own, t_out, xr, z_out, z_in, fin,
    local_sem, info_send, info_recv, w_send, w_recv, w_own,
    ag_up, ag_down, ag_zr, ag_xs, ag_xr, y_send, y_recv, c_send, c_recv,
    cs_send, cs_recv, ys_send, ys_recv, xs_send, xs_recv, zs_send, zs_recv, fin_send, fin_recv, fin_keep,
):
    me, core = lax.axis_index("expert"), lax.axis_index("dp")
    planes = experts // 4
    z, y, x = me // 4, (me // 2) % 2, me % 2
    x_peer, y_peer = me + 1 - 2 * x, me + 2 - 4 * y
    tok_rows, model_width = x_ref.shape
    width = model_width // 2
    hid = gate_ref.shape[2]
    pair = 2 * capacity
    quad = 4 * capacity
    slots = experts * capacity
    slab = model_width // planes
    here = pl.multiple_of(core * width, width)
    batch0 = (((0,), (0,)), ((), ()))

    def remote(src, dst, send, recv, expert=None):
        target = {"dp": 1 - core} if expert is None else {"expert": expert}
        return pltpu.make_async_remote_copy(
            src_ref=src, dst_ref=dst, send_sem=send, recv_sem=recv, device_id=target, device_id_type=MESH
        )

    def at(start, size):
        return pl.ds(pl.multiple_of(start, size), size)

    def peer_of(k):
        return lax.rem(me + k, experts)

    barrier = pltpu.get_barrier_semaphore()

    def greet(k, carry):
        pl.semaphore_signal(barrier, inc=1, device_id={"expert": peer_of(k)}, device_id_type=MESH)
        return carry

    lax.fori_loop(1, experts, greet, 0)
    pl.semaphore_signal(barrier, inc=1, device_id={"dp": 1 - core}, device_id_type=MESH)

    own_copies = []
    for a, ref in enumerate((x_ref, dy_ref)):
        own_copies.append(
            pltpu.make_async_copy(ref.at[:, pl.ds(here, width)], tok.at[a, z, at(x * tok_rows, tok_rows), :], local_sem.at[a])
        )
    own_rows = at((me % 4) * tok_rows, tok_rows)
    own_panels = [
        pltpu.make_async_copy(gate_ref.at[me], gu.at[z, own_rows, pl.ds(0, hid)], w_own.at[0]),
        pltpu.make_async_copy(up_ref.at[me], gu.at[z, own_rows, pl.ds(hid, hid)], w_own.at[1]),
        pltpu.make_async_copy(down_ref.at[me], dn.at[z, own_rows, :], w_own.at[2]),
    ]
    for copy in own_copies:
        copy.start()
    for copy in own_panels:
        copy.start()
    pl.semaphore_wait(barrier, experts)

    def w_copy(w, target, owner):
        spot = at((owner % 4) * tok_rows, tok_rows)
        if w == 0:
            src, dst = gate_ref, gu.at[owner // 4, spot, pl.ds(0, hid)]
        elif w == 1:
            src, dst = up_ref, gu.at[owner // 4, spot, pl.ds(hid, hid)]
        else:
            src, dst = down_ref, dn.at[owner // 4, spot, :]
        return remote(src.at[target], dst, w_send.at[w, target], w_recv.at[w, owner], target)

    others = experts - 1

    def start_weights(first, last):
        for w in range(3):

            def body(n, carry):
                w_copy(w, peer_of(n + 1 - w * others), me).start()
                return carry

            lax.fori_loop(jnp.maximum(first, w * others), jnp.minimum(last, (w + 1) * others), body, 0)

    def wait_panel(w, source):
        w_copy(w, source, source).wait_recv()

    def tok_block(a, zs, xs):
        return tok.at[a, zs, at(xs * tok_rows, tok_rows), :]

    def ag_copy(a, zs, direction):
        block = tok_block(a, zs, x)
        if direction == 0:
            return remote(block, block, ag_up.at[a, zs], ag_zr.at[a, zs], me + 4)
        if direction == 1:
            return remote(block, block, ag_down.at[a, zs], ag_zr.at[a, zs], me - 4)
        return remote(block, block, ag_xs.at[a, zs], ag_xr.at[a, zs], x_peer)

    def walk(t):
        return z + ((t + 1) // 2) * (1 - 2 * (t % 2))

    def inside(zs):
        return jnp.logical_and(zs >= 0, zs < planes)

    def forwards(zs):
        return (
            jnp.logical_and(zs <= z, z < planes - 1),
            jnp.logical_and(zs >= z, z > 0),
        )

    def send_block(a, zs):
        go_up, go_down = forwards(zs)

        @pl.when(go_up)
        def _():
            ag_copy(a, zs, 0).start()

        @pl.when(go_down)
        def _():
            ag_copy(a, zs, 1).start()

        ag_copy(a, zs, 2).start()

    for a in range(2):
        own_copies[a].wait()
        send_block(a, z)

    ids, probs = ids_ref[...], probs_ref[...]
    named_by = lax.broadcasted_iota(jnp.int32, (experts,) + ids.shape, 0) == ids[None, :, :]
    weight = jnp.sum(jnp.where(named_by, probs[None, :, :], 0.0), axis=1)
    named = jnp.sum(jnp.where(named_by, 1.0, 0.0), axis=1)
    before = lax.broadcasted_iota(jnp.int32, (tok_rows, tok_rows), 0) < lax.broadcasted_iota(
        jnp.int32, (tok_rows, tok_rows), 1
    )
    rank = jnp.dot(named.astype(bf16), jnp.where(before, 1.0, 0.0).astype(bf16), preferred_element_type=f32)
    rank = jnp.where(named > 0.5, rank + (x * capacity).astype(f32), -1.0)
    for q in range(4):
        for p in range(planes):
            info[p, pl.ds(2 * q, 1), :] = rank[4 * p + q : 4 * p + q + 1, :]
            info[p, pl.ds(2 * q + 1, 1), :] = weight[4 * p + q : 4 * p + q + 1, :]
    info_all[me] = info[z]

    def info_copy(target, owner):
        return remote(
            info.at[target // 4], info_all.at[owner], info_send.at[target], info_recv.at[owner], target
        )

    def send_info(k, carry):
        info_copy(peer_of(k), me).start()
        return carry

    lax.fori_loop(1, experts, send_info, 0)
    start_weights(0, FIRST * others // 15)

    def wait_info(k, carry):
        source = peer_of(k)
        info_copy(source, source).wait_recv()
        return carry

    lax.fori_loop(1, experts, wait_info, 0)

    def pair_rows(zs, ys):
        return at((2 * zs + ys) * pair, pair)

    def places(zs, expert_index):
        first = 4 * zs + 2 * y
        lines = pl.ds(2 * expert_index, 2)
        both = jnp.concatenate([info_all[first, lines, :], info_all[first + 1, lines, :]], axis=1)
        hit = both[0:1, :] == lax.broadcasted_iota(jnp.int32, (pair, 2 * tok_rows), 0).astype(f32)
        prob = jnp.sum(jnp.where(hit, both[1:2, :], 0.0), axis=1, keepdims=True)
        return jnp.where(hit, 1.0, 0.0).astype(bf16), prob

    def y_copy(a, zs, ys):
        return remote(
            nbr_out.at[a, zs], rows.at[a, core, pair_rows(zs, ys), :], y_send.at[a, zs], y_recv.at[a, zs], y_peer
        )

    def core_copy(a, half, zs, ys):
        block = rows.at[a, half, pair_rows(zs, ys), :]
        return remote(block, block, c_send.at[a, 2 * zs + ys], c_recv.at[a, 2 * zs + ys])

    mine_q = me % 4
    peer_q = y_peer % 4

    def gather(a, zs):
        own_place, own_prob = places(zs, mine_q)
        nbr_place, nbr_prob = places(zs, peer_q)
        if a == 0:
            pls[zs, pl.ds(0, pair), :] = own_place
            pls[zs, pl.ds(pair, pair), :] = nbr_place
        ag_copy(a, zs, 2).wait_recv()
        lent = jnp.dot(nbr_place, tok[a, zs], preferred_element_type=f32)
        if a == 1:
            lent = lent * nbr_prob
        nbr_out[a, zs] = lent.astype(bf16)
        y_copy(a, zs, y).start()
        got = jnp.dot(own_place, tok[a, zs], preferred_element_type=f32)
        if a == 1:
            got = got * own_prob
        rows[a, core, pair_rows(zs, y), :] = got.astype(bf16)
        core_copy(a, core, zs, y).start()

    hops = 2 * planes - 2

    def spread(t, carry):
        zs, ready = walk(t), walk(t - 1)

        @pl.when(jnp.logical_and(t <= hops, inside(zs)))
        def _():
            for a in range(2):
                block = tok_block(a, zs, x)
                remote(block, block, ag_up.at[a, zs], ag_zr.at[a, zs], x_peer).wait_recv()
                send_block(a, zs)

        @pl.when(inside(ready))
        def _():
            for a in range(2):
                gather(a, ready)

        start_weights((FIRST + PACE * (t - 1)) * others // 15, (FIRST + PACE * t) * others // 15)
        return carry

    lax.fori_loop(1, hops + 2, spread, 0)
    start_weights((FIRST + PACE * (hops + 1)) * others // 15, 3 * others)

    def pass_on(a, zs):
        y_copy(a, zs, 1 - y).wait_recv()
        core_copy(a, core, zs, 1 - y).start()

    def take_core(a, zs):
        for ys in range(2):
            core_copy(a, 1 - core, zs, ys).wait_recv()

    for w in range(2):
        own_panels[w].wait()

        def wait_gu(k, carry):
            wait_panel(w, peer_of(k))
            return carry

        lax.fori_loop(1, experts, wait_gu, 0)

    def slab_of(a, g, spot):
        half, off = (g * slab) // width, (g * slab) % width
        return rows[a, half, spot, pl.ds(off, slab)]

    def forward(m):
        spot = at(m * quad, quad)
        total = jnp.dot(slab_of(0, 0, spot), gu[0], preferred_element_type=f32)
        for g in range(1, planes):
            total += jnp.dot(slab_of(0, g, spot), gu[g], preferred_element_type=f32)
        pre[spot, :] = total

    def first_half(t, carry):
        zs, ready = walk(t), walk(t - 1)

        @pl.when(jnp.logical_and(t <= hops, inside(zs)))
        def _():
            for a in range(2):
                pass_on(a, zs)

        @pl.when(jnp.logical_and(t >= 1, inside(ready)))
        def _():
            take_core(0, ready)
            forward(ready)

        return carry

    lax.fori_loop(0, hops + 2, first_half, 0)

    def settle(zs, carry):
        take_core(1, zs)
        return carry

    lax.fori_loop(0, planes, settle, 0)
    own_panels[2].wait()
    for g in range(planes):
        for q in range(4):
            source = 4 * g + q

            @pl.when(source != me)
            def _():
                wait_panel(2, source)

        def backward(m, carry):
            spot = at(m * quad, quad)
            part = jnp.dot(slab_of(1, g, spot), dn[g], preferred_element_type=f32)
            if g == 0:
                act[spot, :] = part
            else:
                act[spot, :] += part
            return carry

        lax.fori_loop(0, planes, backward, 0)

    def pointwise(m, carry):
        spot = at(m * 16, 16)
        gate_pre, up_pre, act_grad = pre[spot, pl.ds(0, hid)], pre[spot, pl.ds(hid, hid)], act[spot, :]
        sig = jax.nn.sigmoid(gate_pre)
        activ[spot, :] = (gate_pre * sig * up_pre).astype(bf16)
        gg[spot, pl.ds(0, hid)] = (act_grad * up_pre * sig * (1.0 + gate_pre * (1.0 - sig))).astype(bf16)
        gg[spot, pl.ds(hid, hid)] = (act_grad * gate_pre * sig).astype(bf16)
        return carry

    back = (((1,), (1,)), ((), ()))
    chunk = width // CUTS
    pieces = planes * CUTS

    upper = (2 * z) // planes
    near = z + upper * (planes - 1 - 2 * z)
    far_count = planes - 1 - 2 * near

    def plane_of(c):
        i = c // CUTS
        j = i - far_count
        close = (j + planes) // planes
        swing = (2 * near - j // 2) * (1 - j % 2) + (j // 2) * (j % 2)
        d = close * swing + (1 - close) * (planes - 1 - i)
        return d + upper * (planes - 1 - 2 * d)

    def cs_copy(d, i):
        return remote(cs_out.at[d, i], cs_in.at[d, i], cs_send.at[d, i], cs_recv.at[d, i])

    def ys_copy(d, i):
        return remote(s_out.at[d, i], comb.at[d, i, pl.ds(pair, pair), :], ys_send.at[d, i], ys_recv.at[d, i], y_peer)

    def xs_copy(d, i):
        return remote(t_out.at[d, i], xr.at[d, i], xs_send.at[d, i], xs_recv.at[d, i], x_peer)

    def weight_rows(half, i):
        start = half * width + i * chunk
        return gu[start // slab, at(start % slab, chunk), :]

    def slot_step(d, i):
        @pl.when(i == 0)
        def _():
            lax.fori_loop(d * (quad // 16), (d + 1) * (quad // 16), pointwise, 0)

        spot = at(d * quad, quad)
        cs_out[d, i] = lax.dot_general(
            gg[spot, :], weight_rows(1 - core, i), back, preferred_element_type=f32
        ).astype(bf16)
        cs_copy(d, i).start()
        mine[d, i] = lax.dot_general(gg[spot, :], weight_rows(core, i), back, preferred_element_type=f32)

    def slot_sum(d, i):
        cs_copy(d, i).wait_recv()
        away, home = at((1 - y) * pair, pair), at(y * pair, pair)
        s_out[d, i] = (mine[d, i, away, :] + cs_in[d, i, away, :].astype(f32)).astype(bf16)
        ys_copy(d, i).start()
        comb[d, i, pl.ds(0, pair), :] = (mine[d, i, home, :] + cs_in[d, i, home, :].astype(f32)).astype(bf16)

    def token_step(d, i):
        ys_copy(d, i).wait_recv()
        t_out[d, i] = lax.dot_general(
            pls[d, :, at((1 - x) * tok_rows, tok_rows)], comb[d, i], batch0, preferred_element_type=f32
        ).astype(bf16)
        xs_copy(d, i).start()
        t_own[d, i] = lax.dot_general(
            pls[d, :, at(x * tok_rows, tok_rows)], comb[d, i], batch0, preferred_element_type=f32
        )

    def z_copy(d, i, up):
        if up:
            return remote(z_out.at[d, i], z_in.at[0, d, i], zs_send.at[d, i], zs_recv.at[0, d, i], me + 4)
        return remote(z_out.at[d, i], z_in.at[1, d, i], zs_send.at[d, i], zs_recv.at[1, d, i], me - 4)

    def z_take(d, i, side):
        remote(
            z_out.at[d, i], z_in.at[side, d, i], zs_send.at[d, i], zs_recv.at[side, d, i], x_peer
        ).wait_recv()
        t_own[d, i] += z_in[side, d, i].astype(f32)

    def fin_copy(i):
        spot = grad_tokens_ref.at[:, pl.ds(pl.multiple_of(here + i * chunk, chunk), chunk)]
        return remote(fin.at[i], spot, fin_send.at[i], fin_recv.at[i]), pltpu.make_async_copy(
            fin.at[i], spot, fin_keep.at[i]
        )

    def z_step(d, i):
        xs_copy(d, i).wait_recv()
        t_own[d, i] += xr[d, i].astype(f32)

        @pl.when(jnp.logical_and(d >= z, z > 0))
        def _():
            z_take(d, i, 0)

        @pl.when(jnp.logical_and(d <= z, z < planes - 1))
        def _():
            z_take(d, i, 1)

        @pl.when(d != z)
        def _():
            z_out[d, i] = t_own[d, i].astype(bf16)

        @pl.when(d > z)
        def _():
            z_copy(d, i, True).start()

        @pl.when(d < z)
        def _():
            z_copy(d, i, False).start()

        @pl.when(d == z)
        def _():
            fin[i] = t_own[d, i].astype(bf16)
            out, keep = fin_copy(i)
            out.start()
            keep.start()

    tile = width // 4

    def weight_grad(i):
        half, off, span = i // 4, at((i % 4) * tile, tile), at(i * tile, tile)
        both = lax.dot_general(rows[0, half, :, off], gg[...], batch0, preferred_element_type=f32)
        grad_gate_ref[span, :] = both[:, :hid].astype(bf16)
        grad_up_ref[span, :] = both[:, hid:].astype(bf16)
        grad_down_ref[span, :] = lax.dot_general(
            rows[1, half, :, off], activ[...], batch0, preferred_element_type=f32
        ).astype(bf16)

    def hop_lag(d):
        waits = jnp.logical_or(jnp.logical_and(d > z, upper == 0), jnp.logical_and(d < z, upper == 1))
        return X_LAG + jnp.where(waits, HOP_LAG * near, 0)

    steps = pieces + max(8, Y_LAG + X_LAG + max(0, HOP_LAG * (planes // 2 - 1) - CUTS))

    def ladder(s, carry):
        @pl.when(s < pieces)
        def _():
            slot_step(plane_of(s), s % CUTS)

        @pl.when(jnp.logical_and(s >= 1, s <= pieces))
        def _():
            slot_sum(plane_of(s - 1), (s - 1) % CUTS)

        @pl.when(jnp.logical_and(s >= Y_LAG, s < pieces + Y_LAG))
        def _():
            token_step(plane_of(s - Y_LAG), (s - Y_LAG) % CUTS)

        lag = Y_LAG + X_LAG

        def z_try(c, inner):
            d = plane_of(c)

            @pl.when(c + Y_LAG + hop_lag(d) == s)
            def _():
                z_step(d, c % CUTS)

            return inner

        @pl.when(s >= lag)
        def _():
            lax.fori_loop(0, pieces, z_try, 0)

        @pl.when(jnp.logical_and(s >= pieces, s < pieces + 8))
        def _():
            weight_grad(s - pieces)

        return carry

    lax.fori_loop(0, steps, ladder, 0)

    def drain_peers(k, carry):
        target = peer_of(k)
        for w in range(3):
            w_copy(w, target, me).wait_send()
        info_copy(target, me).wait_send()
        return carry

    lax.fori_loop(1, experts, drain_peers, 0)

    def drain_tokens(zs, carry):
        go_up, go_down = forwards(zs)
        for a in range(2):

            @pl.when(go_up)
            def _():
                ag_copy(a, zs, 0).wait_send()

            @pl.when(go_down)
            def _():
                ag_copy(a, zs, 1).wait_send()

            ag_copy(a, zs, 2).wait_send()
            y_copy(a, zs, y).wait_send()
            for ys in range(2):
                core_copy(a, core, zs, ys).wait_send()
        for i in range(CUTS):
            cs_copy(zs, i).wait_send()
            ys_copy(zs, i).wait_send()
            xs_copy(zs, i).wait_send()

            @pl.when(zs > z)
            def _():
                z_copy(zs, i, True).wait_send()

            @pl.when(zs < z)
            def _():
                z_copy(zs, i, False).wait_send()

        return carry

    lax.fori_loop(0, planes, drain_tokens, 0)

    for i in range(CUTS):
        out, keep = fin_copy(i)
        keep.wait()
        out.wait()


def placed_dense(tokens, out_grad, route_ids, route_probs, gate_store, up_store, down_store):
    tok_rows, model_width = tokens.shape
    top_count = route_ids.shape[1]
    experts, _, hid = gate_store.shape
    capacity = 9 * tok_rows * top_count // (8 * experts)
    slots, width, planes = experts * capacity, model_width // 2, experts // 4
    pair, quad, slab = 2 * capacity, 4 * capacity, model_width // planes
    chunk = width // CUTS
    vmem, dma = pltpu.VMEM, pltpu.SemaphoreType.DMA
    anywhere, on_chip = pl.BlockSpec(memory_space=pl.ANY), pl.BlockSpec(memory_space=pltpu.VMEM)
    scratch = [
        vmem((planes, 8, tok_rows), f32),
        vmem((experts, 8, tok_rows), f32),
        vmem((planes, slab, 2 * hid), bf16),
        vmem((planes, slab, hid), bf16),
        vmem((2, planes, 2 * tok_rows, width), bf16),
        vmem((2, planes, pair, width), bf16),
        vmem((2, 2, slots, width), bf16),
        vmem((planes, quad, 2 * tok_rows), bf16),
        vmem((slots, 2 * hid), f32),
        vmem((slots, hid), f32),
        vmem((slots, hid), bf16),
        vmem((slots, 2 * hid), bf16),
        vmem((planes, CUTS, quad, chunk), f32),
        vmem((planes, CUTS, quad, chunk), bf16),
        vmem((planes, CUTS, quad, chunk), bf16),
        vmem((planes, CUTS, quad, chunk), bf16),
        vmem((planes, CUTS, pair, chunk), bf16),
        vmem((planes, CUTS, tok_rows, chunk), f32),
        vmem((planes, CUTS, tok_rows, chunk), bf16),
        vmem((planes, CUTS, tok_rows, chunk), bf16),
        vmem((planes, CUTS, tok_rows, chunk), bf16),
        vmem((2, planes, CUTS, tok_rows, chunk), bf16),
        vmem((CUTS, tok_rows, chunk), bf16),
        dma((2,)), dma((experts,)), dma((experts,)), dma((3, experts)), dma((3, experts)), dma((3,)),
        dma((2, planes)), dma((2, planes)), dma((2, planes)), dma((2, planes)), dma((2, planes)),
        dma((2, planes)), dma((2, planes)), dma((2, 2 * planes)), dma((2, 2 * planes)),
        dma((planes, CUTS)), dma((planes, CUTS)), dma((planes, CUTS)), dma((planes, CUTS)),
        dma((planes, CUTS)), dma((planes, CUTS)), dma((planes, CUTS)), dma((2, planes, CUTS)),
        dma((CUTS,)), dma((CUTS,)), dma((CUTS,)),
    ]
    grad = pltpu.VMEM((model_width, hid), bf16)
    outs = pl.pallas_call(
        functools.partial(dense_kernel, experts, capacity),
        out_shape=(grad, grad, grad, pltpu.VMEM((tok_rows, model_width), bf16)),
        in_specs=[on_chip, on_chip] + [anywhere] * 5,
        out_specs=(on_chip,) * 4,
        scratch_shapes=scratch,
        compiler_params=pltpu.CompilerParams(
            collective_id=0, has_side_effects=True, vmem_limit_bytes=VMEM_BYTES
        ),
    )(route_ids.T, route_probs.T, tokens, out_grad, gate_store, up_store, down_store)
    return (outs[0][None], outs[1][None], outs[2][None], outs[3])


def placed(tokens, out_grad, route_ids, route_probs, gate_store, up_store, down_store):
    experts, top_count = lax.axis_size("expert"), route_ids.shape[1]
    capacity = 9 * tokens.shape[0] * top_count // (8 * experts)
    dense = 4 * top_count >= experts and experts % 8 == 0 and capacity % 8 == 0
    body = placed_dense if dense else placed_sparse
    return body(tokens, out_grad, route_ids, route_probs, gate_store, up_store, down_store)


def solution(mesh):
    return jax.shard_map(
        placed,
        mesh=mesh,
        in_specs=(
            P("expert", None),
            P("expert", None),
            P("expert", None),
            P("expert", None),
            P(None, "expert", "dp"),
            P(None, "expert", "dp"),
            P(None, "expert", "dp"),
        ),
        out_specs=(
            P("expert", None, "dp"),
            P("expert", None, "dp"),
            P("expert", None, "dp"),
            P("expert", None),
        ),
        check_vma=False,
    )
```

```python
import functools

import jax
import jax.numpy as jnp
from jax import lax
from jax.experimental import pallas as pl
from jax.experimental.pallas import tpu as pltpu
from jax.sharding import PartitionSpec as P


def joined(own, other):
    first = lax.axis_index("dp") == 0
    return jnp.where(first, jnp.concatenate([own, other], -1), jnp.concatenate([other, own], -1))


def swapped(part):
    return lax.ppermute(part, "dp", [(0, 1), (1, 0)])


def placed_sparse(tokens, out_grad, route_ids, route_probs, gate_store, up_store, down_store):
    tok_rows, model_width = tokens.shape
    top_count = route_ids.shape[1]
    experts = lax.axis_size("expert")
    capacity = max(2, 9 * tok_rows * top_count // (8 * experts))
    slots = experts * capacity
    width = model_width // 2
    here = lax.axis_index("dp") * width
    there = width - here
    f32, bf16 = jnp.float32, jnp.bfloat16

    chosen = route_ids[:, :, None] == jnp.arange(experts, dtype=jnp.int32)[None, None, :]
    weight = jnp.sum(jnp.where(chosen, route_probs[:, :, None], 0.0), axis=1)
    named = jnp.any(chosen, axis=1)
    earlier = jnp.arange(tok_rows)[:, None] > jnp.arange(tok_rows)[None, :]
    rank = jnp.dot(earlier.astype(bf16), named.astype(bf16), preferred_element_type=f32)
    rank = jnp.where(named, rank, -1.0)
    hit = rank.T[:, None, :] == jnp.arange(capacity, dtype=f32)[None, :, None]
    slot_prob = jnp.sum(jnp.where(hit, weight.T[:, None, :], 0.0), axis=2)
    place = hit.astype(bf16).reshape(slots, tok_rows)

    x_part = jnp.dot(
        place, lax.dynamic_slice_in_dim(tokens, here, width, 1), preferred_element_type=f32
    ).astype(bf16)
    dy_part = (
        jnp.dot(place, lax.dynamic_slice_in_dim(out_grad, here, width, 1), preferred_element_type=f32)
        * slot_prob.reshape(slots, 1)
    ).astype(bf16)

    def exchange(a):
        return lax.all_to_all(a, "expert", split_axis=0, concat_axis=0, tiled=True)

    def panel(store):
        return lax.all_to_all(store, "expert", split_axis=0, concat_axis=1, tiled=True)[0]

    x_own = exchange(x_part.reshape(experts, capacity, width)).reshape(slots, width)
    gate_panel = panel(gate_store)
    up_panel = panel(up_store)
    dy_own = exchange(dy_part.reshape(experts, capacity, width)).reshape(slots, width)
    down_panel = panel(down_store)
    rows_in = joined(x_own, swapped(x_own))
    dy_rows = joined(dy_own, swapped(dy_own))
    gate_pre = jnp.dot(rows_in, gate_panel, preferred_element_type=f32)
    up_pre = jnp.dot(rows_in, up_panel, preferred_element_type=f32)
    sig = jax.nn.sigmoid(gate_pre)
    activation = (gate_pre * sig * up_pre).astype(bf16)
    act_grad = jnp.dot(dy_rows, down_panel, preferred_element_type=f32)
    up_grad = (act_grad * gate_pre * sig).astype(bf16)
    gate_grad = (act_grad * up_pre * sig * (1.0 + gate_pre * (1.0 - sig))).astype(bf16)
    back = (((1,), (1,)), ((), ()))

    def slot_part(start):
        rows = [lax.dynamic_slice_in_dim(w, start, width, 0) for w in (gate_panel, up_panel)]
        return lax.dot_general(gate_grad, rows[0], back, preferred_element_type=f32) + lax.dot_general(
            up_grad, rows[1], back, preferred_element_type=f32
        )

    arrived = swapped(slot_part(there).astype(bf16))
    summed = (slot_part(here) + arrived.astype(f32)).astype(bf16)
    returned = exchange(summed.reshape(experts, capacity, width)).reshape(slots, width)
    share = lax.dot_general(place, returned, (((0,), (0,)), ((), ())), preferred_element_type=f32).astype(bf16)
    grad_tokens = joined(share, swapped(share))
    outer = (((0,), (0,)), ((), ()))
    grad_down = lax.dot_general(dy_rows, activation, outer, preferred_element_type=f32).astype(bf16)
    grad_gate = lax.dot_general(rows_in, gate_grad, outer, preferred_element_type=f32).astype(bf16)
    grad_up = lax.dot_general(rows_in, up_grad, outer, preferred_element_type=f32).astype(bf16)
    return (grad_gate[None], grad_up[None], grad_down[None], grad_tokens)


f32, bf16 = jnp.float32, jnp.bfloat16
MESH = pl.DeviceIdType.MESH
CUTS = 2
S_LAG = 3
FIRST, PACE = 4, 5
VMEM_BYTES = 56000 * 1024
Y_LAG, X_LAG, HOP_LAG = 6, 2, 2


def dense_kernel(
    experts, capacity,
    ids_ref, probs_ref, x_ref, dy_ref, gate_ref, up_ref, down_ref,
    grad_gate_ref, grad_up_ref, grad_down_ref, grad_tokens_ref,
    info, info_all, gu, dn, tok, nbr_out, rows, pls, pre, act, activ, gg,
    mine, cs_out, cs_in, comb, s_out, t_own, t_out, xr, z_out, z_in, fin,
    local_sem, info_send, info_recv, w_send, w_recv, w_own,
    ag_up, ag_down, ag_zr, ag_xs, ag_xr, y_send, y_recv, c_send, c_recv,
    cs_send, cs_recv, ys_send, ys_recv, xs_send, xs_recv, zs_send, zs_recv, fin_send, fin_recv, fin_keep,
):
    me, core = lax.axis_index("expert"), lax.axis_index("dp")
    planes = experts // 4
    z, y, x = me // 4, (me // 2) % 2, me % 2
    x_peer, y_peer = me + 1 - 2 * x, me + 2 - 4 * y
    tok_rows, model_width = x_ref.shape
    width = model_width // 2
    hid = gate_ref.shape[2]
    pair = 2 * capacity
    quad = 4 * capacity
    slots = experts * capacity
    slab = model_width // planes
    here = pl.multiple_of(core * width, width)
    batch0 = (((0,), (0,)), ((), ()))

    def remote(src, dst, send, recv, expert=None):
        target = {"dp": 1 - core} if expert is None else {"expert": expert}
        return pltpu.make_async_remote_copy(
            src_ref=src, dst_ref=dst, send_sem=send, recv_sem=recv, device_id=target, device_id_type=MESH
        )

    def at(start, size):
        return pl.ds(pl.multiple_of(start, size), size)

    def peer_of(k):
        return lax.rem(me + k, experts)

    barrier = pltpu.get_barrier_semaphore()

    def greet(k, carry):
        pl.semaphore_signal(barrier, inc=1, device_id={"expert": peer_of(k)}, device_id_type=MESH)
        return carry

    lax.fori_loop(1, experts, greet, 0)
    pl.semaphore_signal(barrier, inc=1, device_id={"dp": 1 - core}, device_id_type=MESH)

    own_copies = []
    for a, ref in enumerate((x_ref, dy_ref)):
        own_copies.append(
            pltpu.make_async_copy(ref.at[:, pl.ds(here, width)], tok.at[a, z, at(x * tok_rows, tok_rows), :], local_sem.at[a])
        )
    own_rows = at((me % 4) * tok_rows, tok_rows)
    own_panels = [
        pltpu.make_async_copy(gate_ref.at[me], gu.at[z, own_rows, pl.ds(0, hid)], w_own.at[0]),
        pltpu.make_async_copy(up_ref.at[me], gu.at[z, own_rows, pl.ds(hid, hid)], w_own.at[1]),
        pltpu.make_async_copy(down_ref.at[me], dn.at[z, own_rows, :], w_own.at[2]),
    ]
    for copy in own_copies:
        copy.start()
    for copy in own_panels:
        copy.start()
    pl.semaphore_wait(barrier, experts)

    def w_copy(w, target, owner):
        spot = at((owner % 4) * tok_rows, tok_rows)
        if w == 0:
            src, dst = gate_ref, gu.at[owner // 4, spot, pl.ds(0, hid)]
        elif w == 1:
            src, dst = up_ref, gu.at[owner // 4, spot, pl.ds(hid, hid)]
        else:
            src, dst = down_ref, dn.at[owner // 4, spot, :]
        return remote(src.at[target], dst, w_send.at[w, target], w_recv.at[w, owner], target)

    others = experts - 1

    def start_weights(first, last):
        for w in range(3):

            def body(n, carry):
                w_copy(w, peer_of(n + 1 - w * others), me).start()
                return carry

            lax.fori_loop(jnp.maximum(first, w * others), jnp.minimum(last, (w + 1) * others), body, 0)

    def wait_panel(w, source):
        w_copy(w, source, source).wait_recv()

    def tok_block(a, zs, xs):
        return tok.at[a, zs, at(xs * tok_rows, tok_rows), :]

    def ag_copy(a, zs, direction):
        block = tok_block(a, zs, x)
        if direction == 0:
            return remote(block, block, ag_up.at[a, zs], ag_zr.at[a, zs], me + 4)
        if direction == 1:
            return remote(block, block, ag_down.at[a, zs], ag_zr.at[a, zs], me - 4)
        return remote(block, block, ag_xs.at[a, zs], ag_xr.at[a, zs], x_peer)

    def walk(t):
        return z + ((t + 1) // 2) * (1 - 2 * (t % 2))

    def inside(zs):
        return jnp.logical_and(zs >= 0, zs < planes)

    def forwards(zs):
        return (
            jnp.logical_and(zs <= z, z < planes - 1),
            jnp.logical_and(zs >= z, z > 0),
        )

    def send_block(a, zs):
        go_up, go_down = forwards(zs)

        @pl.when(go_up)
        def _():
            ag_copy(a, zs, 0).start()

        @pl.when(go_down)
        def _():
            ag_copy(a, zs, 1).start()

        ag_copy(a, zs, 2).start()

    for a in range(2):
        own_copies[a].wait()
        send_block(a, z)

    ids, probs = ids_ref[...], probs_ref[...]
    named_by = lax.broadcasted_iota(jnp.int32, (experts,) + ids.shape, 0) == ids[None, :, :]
    weight = jnp.sum(jnp.where(named_by, probs[None, :, :], 0.0), axis=1)
    named = jnp.sum(jnp.where(named_by, 1.0, 0.0), axis=1)
    before = lax.broadcasted_iota(jnp.int32, (tok_rows, tok_rows), 0) < lax.broadcasted_iota(
        jnp.int32, (tok_rows, tok_rows), 1
    )
    rank = jnp.dot(named.astype(bf16), jnp.where(before, 1.0, 0.0).astype(bf16), preferred_element_type=f32)
    rank = jnp.where(named > 0.5, rank, -4.0 * capacity)
    for q in range(4):
        for p in range(planes):
            info[p, pl.ds(2 * q, 1), :] = rank[4 * p + q : 4 * p + q + 1, :]
            info[p, pl.ds(2 * q + 1, 1), :] = weight[4 * p + q : 4 * p + q + 1, :]
    info_all[me] = info[z]

    def info_copy(target, owner):
        return remote(
            info.at[target // 4], info_all.at[owner], info_send.at[target], info_recv.at[owner], target
        )

    def send_info(k, carry):
        info_copy(peer_of(k), me).start()
        return carry

    lax.fori_loop(1, experts, send_info, 0)
    start_weights(0, FIRST * others // 15)

    def wait_info(k, carry):
        source = peer_of(k)
        info_copy(source, source).wait_recv()
        return carry

    lax.fori_loop(1, experts, wait_info, 0)

    def pair_rows(zs, ys):
        return at((2 * zs + ys) * pair, pair)

    def places(first, second, expert_index):
        lines = pl.ds(2 * expert_index, 2)
        one, two = info_all[first, lines, :], info_all[second, lines, :]
        ranks = jnp.concatenate([one[0:1, :], two[0:1, :] + float(capacity)], axis=1)
        probs = jnp.concatenate([one[1:2, :], two[1:2, :]], axis=1)
        hit = ranks == lax.broadcasted_iota(jnp.int32, (pair, 2 * tok_rows), 0).astype(f32)
        prob = jnp.sum(jnp.where(hit, probs, 0.0), axis=1, keepdims=True)
        return jnp.where(hit, 1.0, 0.0).astype(bf16), prob

    def y_copy(a, zs, ys):
        return remote(
            nbr_out.at[a, zs], rows.at[a, core, pair_rows(zs, ys), :], y_send.at[a, zs], y_recv.at[a, zs], y_peer
        )

    def core_copy(a, half, zs, ys):
        block = rows.at[a, half, pair_rows(zs, ys), :]
        return remote(block, block, c_send.at[a, 2 * zs + ys], c_recv.at[a, 2 * zs + ys])

    mine_q = me % 4
    peer_q = y_peer % 4

    def gather(a, zs):
        first = 4 * zs + 2 * y
        own_place, own_prob = places(first, first + 1, mine_q)
        nbr_place, nbr_prob = places(first, first + 1, peer_q)
        if a == 0:
            pls[0, zs, pl.ds(0, pair), :] = own_place
            pls[0, zs, pl.ds(pair, pair), :] = nbr_place
            for k, q in enumerate((mine_q, x_peer % 4)):
                pls[1, zs, pl.ds(k * pair, pair), :] = places(4 * zs + x, 4 * zs + 2 + x, q)[0]
        ag_copy(a, zs, 2).wait_recv()
        lent = jnp.dot(nbr_place, tok[a, zs], preferred_element_type=f32)
        if a == 1:
            lent = lent * nbr_prob
        nbr_out[a, zs] = lent.astype(bf16)
        y_copy(a, zs, y).start()
        got = jnp.dot(own_place, tok[a, zs], preferred_element_type=f32)
        if a == 1:
            got = got * own_prob
        rows[a, core, pair_rows(zs, y), :] = got.astype(bf16)
        core_copy(a, core, zs, y).start()

    hops = 2 * planes - 2

    def spread(t, carry):
        zs, ready = walk(t), walk(t - 1)

        @pl.when(jnp.logical_and(t <= hops, inside(zs)))
        def _():
            for a in range(2):
                block = tok_block(a, zs, x)
                remote(block, block, ag_up.at[a, zs], ag_zr.at[a, zs], x_peer).wait_recv()
                send_block(a, zs)

        @pl.when(inside(ready))
        def _():
            for a in range(2):
                gather(a, ready)

        start_weights((FIRST + PACE * (t - 1)) * others // 15, (FIRST + PACE * t) * others // 15)
        return carry

    lax.fori_loop(1, hops + 2, spread, 0)
    start_weights((FIRST + PACE * (hops + 1)) * others // 15, 3 * others)

    def pass_on(a, zs):
        y_copy(a, zs, 1 - y).wait_recv()
        core_copy(a, core, zs, 1 - y).start()

    def take_core(a, zs):
        for ys in range(2):
            core_copy(a, 1 - core, zs, ys).wait_recv()

    for w in range(2):
        own_panels[w].wait()

        def wait_gu(k, carry):
            wait_panel(w, peer_of(k))
            return carry

        lax.fori_loop(1, experts, wait_gu, 0)

    def slab_of(a, g, spot):
        half, off = (g * slab) // width, (g * slab) % width
        return rows[a, half, spot, pl.ds(off, slab)]

    def forward(m):
        spot = at(m * quad, quad)
        total = jnp.dot(slab_of(0, 0, spot), gu[0], preferred_element_type=f32)
        for g in range(1, planes):
            total += jnp.dot(slab_of(0, g, spot), gu[g], preferred_element_type=f32)
        pre[spot, :] = total

    def first_half(t, carry):
        zs, ready = walk(t), walk(t - 1)

        @pl.when(jnp.logical_and(t <= hops, inside(zs)))
        def _():
            for a in range(2):
                pass_on(a, zs)

        @pl.when(jnp.logical_and(t >= 1, inside(ready)))
        def _():
            take_core(0, ready)
            forward(ready)

        return carry

    lax.fori_loop(0, hops + 2, first_half, 0)

    def settle(zs, carry):
        take_core(1, zs)
        return carry

    lax.fori_loop(0, planes, settle, 0)
    own_panels[2].wait()
    for g in range(planes):
        for q in range(4):
            source = 4 * g + q

            @pl.when(source != me)
            def _():
                wait_panel(2, source)

        def backward(m, carry):
            spot = at(m * quad, quad)
            part = jnp.dot(slab_of(1, g, spot), dn[g], preferred_element_type=f32)
            if g == 0:
                act[spot, :] = part
            else:
                act[spot, :] += part
            return carry

        lax.fori_loop(0, planes, backward, 0)

    def pointwise(m, carry):
        spot = at(m * 16, 16)
        gate_pre, up_pre, act_grad = pre[spot, pl.ds(0, hid)], pre[spot, pl.ds(hid, hid)], act[spot, :]
        sig = jax.nn.sigmoid(gate_pre)
        activ[spot, :] = (gate_pre * sig * up_pre).astype(bf16)
        gg[spot, pl.ds(0, hid)] = (act_grad * up_pre * sig * (1.0 + gate_pre * (1.0 - sig))).astype(bf16)
        gg[spot, pl.ds(hid, hid)] = (act_grad * gate_pre * sig).astype(bf16)
        return carry

    back = (((1,), (1,)), ((), ()))
    chunk = width // CUTS
    pieces = planes * CUTS

    upper = (2 * z) // planes
    near = z + upper * (planes - 1 - 2 * z)
    far_count = planes - 1 - 2 * near

    def plane_of(c):
        i = c // CUTS
        j = i - far_count
        close = (j + planes) // planes
        swing = (2 * near - j // 2) * (1 - j % 2) + (j // 2) * (j % 2)
        d = close * swing + (1 - close) * (planes - 1 - i)
        return d + upper * (planes - 1 - 2 * d)

    def blend(i, first, second):
        return first + (second - first) * i

    def cs_copy(d, i):
        return remote(cs_out.at[d, i], cs_in.at[d, i], cs_send.at[d, i], cs_recv.at[d, i])

    def ys_copy(d, i):
        return remote(
            s_out.at[d, i], comb.at[d, i, pl.ds(pair, pair), :], ys_send.at[d, i], ys_recv.at[d, i], blend(i, y_peer, x_peer)
        )

    def xs_copy(d, i):
        return remote(t_out.at[d, i], xr.at[d, i], xs_send.at[d, i], xs_recv.at[d, i], blend(i, x_peer, y_peer))

    def weight_rows(half, i):
        start = half * width + i * chunk
        return gu[start // slab, at(start % slab, chunk), :]

    def slot_step(d, i):
        @pl.when(i == 0)
        def _():
            lax.fori_loop(d * (quad // 16), (d + 1) * (quad // 16), pointwise, 0)

        spot = at(d * quad, quad)
        cs_out[d, i] = lax.dot_general(
            gg[spot, :], weight_rows(1 - core, i), back, preferred_element_type=f32
        ).astype(bf16)
        cs_copy(d, i).start()
        mine[d, i] = lax.dot_general(gg[spot, :], weight_rows(core, i), back, preferred_element_type=f32)

    def slot_sum(d, i):
        cs_copy(d, i).wait_recv()
        mine[d, i] += cs_in[d, i].astype(f32)

        def both(q):
            return jnp.concatenate(
                [mine[d, i, at(q * capacity, capacity), :], mine[d, i, at((q + 1 + i) * capacity, capacity), :]], axis=0
            ).astype(bf16)

        s_out[d, i] = both(blend(i, 2 - 2 * y, 1 - x))
        ys_copy(d, i).start()
        comb[d, i, pl.ds(0, pair), :] = both(blend(i, 2 * y, x))

    def token_step(d, i):
        ys_copy(d, i).wait_recv()
        here_first = blend(i, x, y)
        t_out[d, i] = lax.dot_general(
            pls[i, d, :, at((1 - here_first) * tok_rows, tok_rows)], comb[d, i], batch0, preferred_element_type=f32
        ).astype(bf16)
        xs_copy(d, i).start()
        t_own[d, i] = lax.dot_general(
            pls[i, d, :, at(here_first * tok_rows, tok_rows)], comb[d, i], batch0, preferred_element_type=f32
        )

    def z_copy(d, i, up):
        if up:
            return remote(z_out.at[d, i], z_in.at[0, d, i], zs_send.at[d, i], zs_recv.at[0, d, i], me + 4)
        return remote(z_out.at[d, i], z_in.at[1, d, i], zs_send.at[d, i], zs_recv.at[1, d, i], me - 4)

    def z_take(d, i, side):
        remote(
            z_out.at[d, i], z_in.at[side, d, i], zs_send.at[d, i], zs_recv.at[side, d, i], x_peer
        ).wait_recv()
        t_own[d, i] += z_in[side, d, i].astype(f32)

    def fin_copy(i):
        spot = grad_tokens_ref.at[:, pl.ds(pl.multiple_of(here + i * chunk, chunk), chunk)]
        return remote(fin.at[i], spot, fin_send.at[i], fin_recv.at[i]), pltpu.make_async_copy(
            fin.at[i], spot, fin_keep.at[i]
        )

    def z_step(d, i):
        xs_copy(d, i).wait_recv()
        t_own[d, i] += xr[d, i].astype(f32)

        @pl.when(jnp.logical_and(d >= z, z > 0))
        def _():
            z_take(d, i, 0)

        @pl.when(jnp.logical_and(d <= z, z < planes - 1))
        def _():
            z_take(d, i, 1)

        @pl.when(d != z)
        def _():
            z_out[d, i] = t_own[d, i].astype(bf16)

        @pl.when(d > z)
        def _():
            z_copy(d, i, True).start()

        @pl.when(d < z)
        def _():
            z_copy(d, i, False).start()

        @pl.when(d == z)
        def _():
            fin[i] = t_own[d, i].astype(bf16)
            out, keep = fin_copy(i)
            out.start()
            keep.start()

    tile = width // 4

    def weight_grad(i):
        half, off, span = i // 4, at((i % 4) * tile, tile), at(i * tile, tile)
        both = lax.dot_general(rows[0, half, :, off], gg[...], batch0, preferred_element_type=f32)
        grad_gate_ref[span, :] = both[:, :hid].astype(bf16)
        grad_up_ref[span, :] = both[:, hid:].astype(bf16)
        grad_down_ref[span, :] = lax.dot_general(
            rows[1, half, :, off], activ[...], batch0, preferred_element_type=f32
        ).astype(bf16)

    def hop_lag(d):
        waits = jnp.logical_or(jnp.logical_and(d > z, upper == 0), jnp.logical_and(d < z, upper == 1))
        return X_LAG + jnp.where(waits, HOP_LAG * near, 0)

    steps = pieces + max(8, Y_LAG + X_LAG + max(0, HOP_LAG * (planes // 2 - 1) - CUTS))

    def ladder(s, carry):
        @pl.when(s < pieces)
        def _():
            slot_step(plane_of(s), s % CUTS)

        @pl.when(jnp.logical_and(s >= 1, s <= 2 * CUTS))
        def _():
            slot_sum(plane_of(s - 1), (s - 1) % CUTS)

        @pl.when(jnp.logical_and(s >= Y_LAG, s < pieces + Y_LAG))
        def _():
            token_step(plane_of(s - Y_LAG), (s - Y_LAG) % CUTS)

        @pl.when(jnp.logical_and(s > 2 * CUTS + S_LAG, s <= pieces + S_LAG))
        def _():
            slot_sum(plane_of(s - 1 - S_LAG), (s - 1 - S_LAG) % CUTS)

        lag = Y_LAG + X_LAG

        def z_try(c, inner):
            d = plane_of(c)

            @pl.when(c + Y_LAG + hop_lag(d) == s)
            def _():
                z_step(d, c % CUTS)

            return inner

        @pl.when(s >= lag)
        def _():
            lax.fori_loop(0, pieces, z_try, 0)

        @pl.when(jnp.logical_and(s >= pieces, s < pieces + 8))
        def _():
            weight_grad(s - pieces)

        return carry

    lax.fori_loop(0, steps, ladder, 0)

    def drain_peers(k, carry):
        target = peer_of(k)
        for w in range(3):
            w_copy(w, target, me).wait_send()
        info_copy(target, me).wait_send()
        return carry

    lax.fori_loop(1, experts, drain_peers, 0)

    def drain_tokens(zs, carry):
        go_up, go_down = forwards(zs)
        for a in range(2):

            @pl.when(go_up)
            def _():
                ag_copy(a, zs, 0).wait_send()

            @pl.when(go_down)
            def _():
                ag_copy(a, zs, 1).wait_send()

            ag_copy(a, zs, 2).wait_send()
            y_copy(a, zs, y).wait_send()
            for ys in range(2):
                core_copy(a, core, zs, ys).wait_send()
        for i in range(CUTS):
            cs_copy(zs, i).wait_send()
            ys_copy(zs, i).wait_send()
            xs_copy(zs, i).wait_send()

            @pl.when(zs > z)
            def _():
                z_copy(zs, i, True).wait_send()

            @pl.when(zs < z)
            def _():
                z_copy(zs, i, False).wait_send()

        return carry

    lax.fori_loop(0, planes, drain_tokens, 0)

    for i in range(CUTS):
        out, keep = fin_copy(i)
        keep.wait()
        out.wait()


def placed_dense(tokens, out_grad, route_ids, route_probs, gate_store, up_store, down_store):
    tok_rows, model_width = tokens.shape
    top_count = route_ids.shape[1]
    experts, _, hid = gate_store.shape
    capacity = 9 * tok_rows * top_count // (8 * experts)
    slots, width, planes = experts * capacity, model_width // 2, experts // 4
    pair, quad, slab = 2 * capacity, 4 * capacity, model_width // planes
    chunk = width // CUTS
    vmem, dma = pltpu.VMEM, pltpu.SemaphoreType.DMA
    anywhere, on_chip = pl.BlockSpec(memory_space=pl.ANY), pl.BlockSpec(memory_space=pltpu.VMEM)
    scratch = [
        vmem((planes, 8, tok_rows), f32),
        vmem((experts, 8, tok_rows), f32),
        vmem((planes, slab, 2 * hid), bf16),
        vmem((planes, slab, hid), bf16),
        vmem((2, planes, 2 * tok_rows, width), bf16),
        vmem((2, planes, pair, width), bf16),
        vmem((2, 2, slots, width), bf16),
        vmem((2, planes, quad, 2 * tok_rows), bf16),
        vmem((slots, 2 * hid), f32),
        vmem((slots, hid), f32),
        vmem((slots, hid), bf16),
        vmem((slots, 2 * hid), bf16),
        vmem((planes, CUTS, quad, chunk), f32),
        vmem((planes, CUTS, quad, chunk), bf16),
        vmem((planes, CUTS, quad, chunk), bf16),
        vmem((planes, CUTS, quad, chunk), bf16),
        vmem((planes, CUTS, pair, chunk), bf16),
        vmem((planes, CUTS, tok_rows, chunk), f32),
        vmem((planes, CUTS, tok_rows, chunk), bf16),
        vmem((planes, CUTS, tok_rows, chunk), bf16),
        vmem((planes, CUTS, tok_rows, chunk), bf16),
        vmem((2, planes, CUTS, tok_rows, chunk), bf16),
        vmem((CUTS, tok_rows, chunk), bf16),
        dma((2,)), dma((experts,)), dma((experts,)), dma((3, experts)), dma((3, experts)), dma((3,)),
        dma((2, planes)), dma((2, planes)), dma((2, planes)), dma((2, planes)), dma((2, planes)),
        dma((2, planes)), dma((2, planes)), dma((2, 2 * planes)), dma((2, 2 * planes)),
        dma((planes, CUTS)), dma((planes, CUTS)), dma((planes, CUTS)), dma((planes, CUTS)),
        dma((planes, CUTS)), dma((planes, CUTS)), dma((planes, CUTS)), dma((2, planes, CUTS)),
        dma((CUTS,)), dma((CUTS,)), dma((CUTS,)),
    ]
    grad = pltpu.VMEM((model_width, hid), bf16)
    outs = pl.pallas_call(
        functools.partial(dense_kernel, experts, capacity),
        out_shape=(grad, grad, grad, pltpu.VMEM((tok_rows, model_width), bf16)),
        in_specs=[on_chip, on_chip] + [anywhere] * 5,
        out_specs=(on_chip,) * 4,
        scratch_shapes=scratch,
        compiler_params=pltpu.CompilerParams(
            collective_id=0, has_side_effects=True, vmem_limit_bytes=VMEM_BYTES
        ),
    )(route_ids.T, route_probs.T, tokens, out_grad, gate_store, up_store, down_store)
    return (outs[0][None], outs[1][None], outs[2][None], outs[3])


def placed(tokens, out_grad, route_ids, route_probs, gate_store, up_store, down_store):
    experts, top_count = lax.axis_size("expert"), route_ids.shape[1]
    capacity = 9 * tokens.shape[0] * top_count // (8 * experts)
    dense = 4 * top_count >= experts and experts % 8 == 0 and capacity % 8 == 0
    body = placed_dense if dense else placed_sparse
    return body(tokens, out_grad, route_ids, route_probs, gate_store, up_store, down_store)


def solution(mesh):
    return jax.shard_map(
        placed,
        mesh=mesh,
        in_specs=(
            P("expert", None),
            P("expert", None),
            P("expert", None),
            P("expert", None),
            P(None, "expert", "dp"),
            P(None, "expert", "dp"),
            P(None, "expert", "dp"),
        ),
        out_specs=(
            P("expert", None, "dp"),
            P("expert", None, "dp"),
            P("expert", None, "dp"),
            P("expert", None),
        ),
        check_vma=False,
    )
```

```python
import functools

import jax
import jax.numpy as jnp
from jax import lax
from jax.experimental import pallas as pl
from jax.experimental.pallas import tpu as pltpu
from jax.sharding import PartitionSpec as P


def joined(own, other):
    first = lax.axis_index("dp") == 0
    return jnp.where(first, jnp.concatenate([own, other], -1), jnp.concatenate([other, own], -1))


def swapped(part):
    return lax.ppermute(part, "dp", [(0, 1), (1, 0)])


def placed_sparse(tokens, out_grad, route_ids, route_probs, gate_store, up_store, down_store):
    tok_rows, model_width = tokens.shape
    top_count = route_ids.shape[1]
    experts = lax.axis_size("expert")
    capacity = max(2, 9 * tok_rows * top_count // (8 * experts))
    slots = experts * capacity
    width = model_width // 2
    here = lax.axis_index("dp") * width
    there = width - here
    f32, bf16 = jnp.float32, jnp.bfloat16

    chosen = route_ids[:, :, None] == jnp.arange(experts, dtype=jnp.int32)[None, None, :]
    weight = jnp.sum(jnp.where(chosen, route_probs[:, :, None], 0.0), axis=1)
    named = jnp.any(chosen, axis=1)
    earlier = jnp.arange(tok_rows)[:, None] > jnp.arange(tok_rows)[None, :]
    rank = jnp.dot(earlier.astype(bf16), named.astype(bf16), preferred_element_type=f32)
    rank = jnp.where(named, rank, -1.0)
    hit = rank.T[:, None, :] == jnp.arange(capacity, dtype=f32)[None, :, None]
    slot_prob = jnp.sum(jnp.where(hit, weight.T[:, None, :], 0.0), axis=2)
    place = hit.astype(bf16).reshape(slots, tok_rows)

    x_part = jnp.dot(
        place, lax.dynamic_slice_in_dim(tokens, here, width, 1), preferred_element_type=f32
    ).astype(bf16)
    dy_part = (
        jnp.dot(place, lax.dynamic_slice_in_dim(out_grad, here, width, 1), preferred_element_type=f32)
        * slot_prob.reshape(slots, 1)
    ).astype(bf16)

    def exchange(a):
        return lax.all_to_all(a, "expert", split_axis=0, concat_axis=0, tiled=True)

    def panel(store):
        return lax.all_to_all(store, "expert", split_axis=0, concat_axis=1, tiled=True)[0]

    x_own = exchange(x_part.reshape(experts, capacity, width)).reshape(slots, width)
    gate_panel = panel(gate_store)
    up_panel = panel(up_store)
    dy_own = exchange(dy_part.reshape(experts, capacity, width)).reshape(slots, width)
    down_panel = panel(down_store)
    rows_in = joined(x_own, swapped(x_own))
    dy_rows = joined(dy_own, swapped(dy_own))
    gate_pre = jnp.dot(rows_in, gate_panel, preferred_element_type=f32)
    up_pre = jnp.dot(rows_in, up_panel, preferred_element_type=f32)
    sig = jax.nn.sigmoid(gate_pre)
    activation = (gate_pre * sig * up_pre).astype(bf16)
    act_grad = jnp.dot(dy_rows, down_panel, preferred_element_type=f32)
    up_grad = (act_grad * gate_pre * sig).astype(bf16)
    gate_grad = (act_grad * up_pre * sig * (1.0 + gate_pre * (1.0 - sig))).astype(bf16)
    back = (((1,), (1,)), ((), ()))

    def slot_part(start):
        rows = [lax.dynamic_slice_in_dim(w, start, width, 0) for w in (gate_panel, up_panel)]
        return lax.dot_general(gate_grad, rows[0], back, preferred_element_type=f32) + lax.dot_general(
            up_grad, rows[1], back, preferred_element_type=f32
        )

    arrived = swapped(slot_part(there).astype(bf16))
    summed = (slot_part(here) + arrived.astype(f32)).astype(bf16)
    returned = exchange(summed.reshape(experts, capacity, width)).reshape(slots, width)
    share = lax.dot_general(place, returned, (((0,), (0,)), ((), ())), preferred_element_type=f32).astype(bf16)
    grad_tokens = joined(share, swapped(share))
    outer = (((0,), (0,)), ((), ()))
    grad_down = lax.dot_general(dy_rows, activation, outer, preferred_element_type=f32).astype(bf16)
    grad_gate = lax.dot_general(rows_in, gate_grad, outer, preferred_element_type=f32).astype(bf16)
    grad_up = lax.dot_general(rows_in, up_grad, outer, preferred_element_type=f32).astype(bf16)
    return (grad_gate[None], grad_up[None], grad_down[None], grad_tokens)


f32, bf16 = jnp.float32, jnp.bfloat16
MESH = pl.DeviceIdType.MESH
CUTS = 2
S_LAG = 3
FIRST, PACE = 4, 5
VMEM_BYTES = 56000 * 1024
Y_LAG, X_LAG, HOP_LAG = 6, 2, 2


def dense_kernel(
    experts, capacity,
    ids_ref, probs_ref, x_ref, dy_ref, gate_ref, up_ref, down_ref,
    grad_gate_ref, grad_up_ref, grad_down_ref, grad_tokens_ref,
    info, info_all, gu, dn, tok, nbr_out, rows, pls, pre, act, activ, gg,
    mine, cs_out, cs_in, comb, s_out, t_own, t_out, xr, z_out, z_in, fin,
    local_sem, info_send, info_recv, w_send, w_recv, w_own,
    ag_up, ag_down, ag_zr, ag_xs, ag_xr, y_send, y_recv, c_send, c_recv,
    cs_send, cs_recv, ys_send, ys_recv, xs_send, xs_recv, zs_send, zs_recv, fin_send, fin_recv, fin_keep,
):
    me, core = lax.axis_index("expert"), lax.axis_index("dp")
    planes = experts // 4
    z, y, x = me // 4, (me // 2) % 2, me % 2
    x_peer, y_peer = me + 1 - 2 * x, me + 2 - 4 * y
    tok_rows, model_width = x_ref.shape
    width = model_width // 2
    hid = gate_ref.shape[2]
    pair = 2 * capacity
    quad = 4 * capacity
    slots = experts * capacity
    slab = model_width // planes
    here = pl.multiple_of(core * width, width)
    batch0 = (((0,), (0,)), ((), ()))

    def remote(src, dst, send, recv, expert=None):
        target = {"dp": 1 - core} if expert is None else {"expert": expert}
        return pltpu.make_async_remote_copy(
            src_ref=src, dst_ref=dst, send_sem=send, recv_sem=recv, device_id=target, device_id_type=MESH
        )

    def at(start, size):
        return pl.ds(pl.multiple_of(start, size), size)

    def peer_of(k):
        return lax.rem(me + k, experts)

    barrier = pltpu.get_barrier_semaphore()

    def greet(k, carry):
        pl.semaphore_signal(barrier, inc=1, device_id={"expert": peer_of(k)}, device_id_type=MESH)
        return carry

    lax.fori_loop(1, experts, greet, 0)
    pl.semaphore_signal(barrier, inc=1, device_id={"dp": 1 - core}, device_id_type=MESH)

    own_copies = []
    for a, ref in enumerate((x_ref, dy_ref)):
        own_copies.append(
            pltpu.make_async_copy(ref.at[:, pl.ds(here, width)], tok.at[a, z, at(x * tok_rows, tok_rows), :], local_sem.at[a])
        )
    own_rows = at((me % 4) * tok_rows, tok_rows)
    own_panels = [
        pltpu.make_async_copy(gate_ref.at[me], gu.at[z, own_rows, pl.ds(0, hid)], w_own.at[0]),
        pltpu.make_async_copy(up_ref.at[me], gu.at[z, own_rows, pl.ds(hid, hid)], w_own.at[1]),
        pltpu.make_async_copy(down_ref.at[me], dn.at[z, own_rows, :], w_own.at[2]),
    ]
    for copy in own_copies:
        copy.start()
    for copy in own_panels:
        copy.start()
    pl.semaphore_wait(barrier, experts)

    def w_copy(w, target, owner):
        spot = at((owner % 4) * tok_rows, tok_rows)
        if w == 0:
            src, dst = gate_ref, gu.at[owner // 4, spot, pl.ds(0, hid)]
        elif w == 1:
            src, dst = up_ref, gu.at[owner // 4, spot, pl.ds(hid, hid)]
        else:
            src, dst = down_ref, dn.at[owner // 4, spot, :]
        return remote(src.at[target], dst, w_send.at[w, target], w_recv.at[w, owner], target)

    others = experts - 1

    def start_weights(first, last):
        for w in range(3):

            def body(n, carry):
                w_copy(w, peer_of(n + 1 - w * others), me).start()
                return carry

            lax.fori_loop(jnp.maximum(first, w * others), jnp.minimum(last, (w + 1) * others), body, 0)

    def wait_panel(w, source):
        w_copy(w, source, source).wait_recv()

    def tok_block(a, zs, xs):
        return tok.at[a, zs, at(xs * tok_rows, tok_rows), :]

    def ag_copy(a, zs, direction):
        block = tok_block(a, zs, x)
        if direction == 0:
            return remote(block, block, ag_up.at[a, zs], ag_zr.at[a, zs], me + 4)
        if direction == 1:
            return remote(block, block, ag_down.at[a, zs], ag_zr.at[a, zs], me - 4)
        return remote(block, block, ag_xs.at[a, zs], ag_xr.at[a, zs], x_peer)

    def walk(t):
        return z + ((t + 1) // 2) * (1 - 2 * (t % 2))

    def inside(zs):
        return jnp.logical_and(zs >= 0, zs < planes)

    def forwards(zs):
        return (
            jnp.logical_and(zs <= z, z < planes - 1),
            jnp.logical_and(zs >= z, z > 0),
        )

    def send_block(a, zs):
        go_up, go_down = forwards(zs)

        @pl.when(go_up)
        def _():
            ag_copy(a, zs, 0).start()

        @pl.when(go_down)
        def _():
            ag_copy(a, zs, 1).start()

        ag_copy(a, zs, 2).start()

    for a in range(2):
        own_copies[a].wait()
        send_block(a, z)

    ids, probs = ids_ref[...], probs_ref[...]
    named_by = lax.broadcasted_iota(jnp.int32, (experts,) + ids.shape, 0) == ids[None, :, :]
    weight = jnp.sum(jnp.where(named_by, probs[None, :, :], 0.0), axis=1)
    named = jnp.sum(jnp.where(named_by, 1.0, 0.0), axis=1)
    before = lax.broadcasted_iota(jnp.int32, (tok_rows, tok_rows), 0) < lax.broadcasted_iota(
        jnp.int32, (tok_rows, tok_rows), 1
    )
    rank = jnp.dot(named.astype(bf16), jnp.where(before, 1.0, 0.0).astype(bf16), preferred_element_type=f32)
    rank = jnp.where(named > 0.5, rank, -4.0 * capacity)
    for q in range(4):
        for p in range(planes):
            info[p, pl.ds(2 * q, 1), :] = rank[4 * p + q : 4 * p + q + 1, :]
            info[p, pl.ds(2 * q + 1, 1), :] = weight[4 * p + q : 4 * p + q + 1, :]
    info_all[me] = info[z]

    def info_copy(target, owner):
        return remote(
            info.at[target // 4], info_all.at[owner], info_send.at[target], info_recv.at[owner], target
        )

    def send_info(k, carry):
        info_copy(peer_of(k), me).start()
        return carry

    lax.fori_loop(1, experts, send_info, 0)
    start_weights(0, FIRST * others // 15)

    def wait_info(k, carry):
        source = peer_of(k)
        info_copy(source, source).wait_recv()
        return carry

    lax.fori_loop(1, experts, wait_info, 0)

    def pair_rows(zs, ys):
        return at((2 * zs + ys) * pair, pair)

    def places(first, second, expert_index):
        lines = pl.ds(2 * expert_index, 2)
        one, two = info_all[first, lines, :], info_all[second, lines, :]
        ranks = jnp.concatenate([one[0:1, :], two[0:1, :] + float(capacity)], axis=1)
        probs = jnp.concatenate([one[1:2, :], two[1:2, :]], axis=1)
        hit = ranks == lax.broadcasted_iota(jnp.int32, (pair, 2 * tok_rows), 0).astype(f32)
        prob = jnp.sum(jnp.where(hit, probs, 0.0), axis=1, keepdims=True)
        return jnp.where(hit, 1.0, 0.0).astype(bf16), prob

    def y_copy(a, zs, ys):
        return remote(
            nbr_out.at[a, zs], rows.at[a, core, pair_rows(zs, ys), :], y_send.at[a, zs], y_recv.at[a, zs], y_peer
        )

    def core_copy(a, half, zs, ys):
        block = rows.at[a, half, pair_rows(zs, ys), :]
        return remote(block, block, c_send.at[a, 2 * zs + ys], c_recv.at[a, 2 * zs + ys])

    mine_q = me % 4
    peer_q = y_peer % 4

    def gather(a, zs):
        first = 4 * zs + 2 * y
        own_place, own_prob = places(first, first + 1, mine_q)
        nbr_place, nbr_prob = places(first, first + 1, peer_q)
        if a == 0:
            pls[0, zs, pl.ds(0, pair), :] = own_place
            pls[0, zs, pl.ds(pair, pair), :] = nbr_place
            for k, q in enumerate((mine_q, x_peer % 4)):
                pls[1, zs, pl.ds(k * pair, pair), :] = places(4 * zs + x, 4 * zs + 2 + x, q)[0]
        ag_copy(a, zs, 2).wait_recv()
        lent = jnp.dot(nbr_place, tok[a, zs], preferred_element_type=f32)
        if a == 1:
            lent = lent * nbr_prob
        nbr_out[a, zs] = lent.astype(bf16)
        y_copy(a, zs, y).start()
        got = jnp.dot(own_place, tok[a, zs], preferred_element_type=f32)
        if a == 1:
            got = got * own_prob
        rows[a, core, pair_rows(zs, y), :] = got.astype(bf16)
        core_copy(a, core, zs, y).start()

    hops = 2 * planes - 2

    def spread(t, carry):
        zs, ready = walk(t), walk(t - 1)

        @pl.when(jnp.logical_and(t <= hops, inside(zs)))
        def _():
            for a in range(2):
                block = tok_block(a, zs, x)
                remote(block, block, ag_up.at[a, zs], ag_zr.at[a, zs], x_peer).wait_recv()
                send_block(a, zs)

        @pl.when(inside(ready))
        def _():
            for a in range(2):
                gather(a, ready)

        start_weights((FIRST + PACE * (t - 1)) * others // 15, (FIRST + PACE * t) * others // 15)
        return carry

    lax.fori_loop(1, hops + 2, spread, 0)
    start_weights((FIRST + PACE * (hops + 1)) * others // 15, 3 * others)

    def pass_on(a, zs):
        y_copy(a, zs, 1 - y).wait_recv()
        core_copy(a, core, zs, 1 - y).start()

    def take_core(a, zs):
        for ys in range(2):
            core_copy(a, 1 - core, zs, ys).wait_recv()

    for w in range(2):
        own_panels[w].wait()

        def wait_gu(k, carry):
            wait_panel(w, peer_of(k))
            return carry

        lax.fori_loop(1, experts, wait_gu, 0)

    def slab_of(a, g, spot):
        half, off = (g * slab) // width, (g * slab) % width
        return rows[a, half, spot, pl.ds(off, slab)]

    def forward(m):
        spot = at(m * quad, quad)
        total = jnp.dot(slab_of(0, 0, spot), gu[0], preferred_element_type=f32)
        for g in range(1, planes):
            total += jnp.dot(slab_of(0, g, spot), gu[g], preferred_element_type=f32)
        pre[spot, :] = total

    def first_half(t, carry):
        zs, ready = walk(t), walk(t - 1)

        @pl.when(jnp.logical_and(t <= hops, inside(zs)))
        def _():
            for a in range(2):
                pass_on(a, zs)

        @pl.when(jnp.logical_and(t >= 1, inside(ready)))
        def _():
            take_core(0, ready)
            forward(ready)

        return carry

    lax.fori_loop(0, hops + 2, first_half, 0)

    def settle(zs, carry):
        take_core(1, zs)
        return carry

    lax.fori_loop(0, planes, settle, 0)
    own_panels[2].wait()
    upper = (2 * z) // planes
    for turn in range(planes):
        g = turn + upper * (planes - 1 - 2 * turn)
        for q in range(4):
            source = 4 * g + q

            @pl.when(source != me)
            def _():
                wait_panel(2, source)

        def backward(m, carry):
            spot = at(m * quad, quad)
            part = jnp.dot(rows[1, (g * slab) // width, spot, at((g * slab) % width, slab)], dn[g], preferred_element_type=f32)
            if turn == 0:
                act[spot, :] = part
            else:
                act[spot, :] += part
            return carry

        lax.fori_loop(0, planes, backward, 0)

    def pointwise(m, carry):
        spot = at(m * 16, 16)
        gate_pre, up_pre, act_grad = pre[spot, pl.ds(0, hid)], pre[spot, pl.ds(hid, hid)], act[spot, :]
        sig = jax.nn.sigmoid(gate_pre)
        activ[spot, :] = (gate_pre * sig * up_pre).astype(bf16)
        gg[spot, pl.ds(0, hid)] = (act_grad * up_pre * sig * (1.0 + gate_pre * (1.0 - sig))).astype(bf16)
        gg[spot, pl.ds(hid, hid)] = (act_grad * gate_pre * sig).astype(bf16)
        return carry

    back = (((1,), (1,)), ((), ()))
    chunk = width // CUTS
    pieces = planes * CUTS

    near = z + upper * (planes - 1 - 2 * z)
    far_count = planes - 1 - 2 * near

    def plane_of(c):
        i = c // CUTS
        j = i - far_count
        close = (j + planes) // planes
        swing = (2 * near - j // 2) * (1 - j % 2) + (j // 2) * (j % 2)
        d = close * swing + (1 - close) * (planes - 1 - i)
        return d + upper * (planes - 1 - 2 * d)

    def blend(i, first, second):
        return first + (second - first) * i

    def cs_copy(d, i):
        return remote(cs_out.at[d, i], cs_in.at[d, i], cs_send.at[d, i], cs_recv.at[d, i])

    def ys_copy(d, i):
        return remote(
            s_out.at[d, i], comb.at[d, i, pl.ds(pair, pair), :], ys_send.at[d, i], ys_recv.at[d, i], blend(i, y_peer, x_peer)
        )

    def xs_copy(d, i):
        return remote(t_out.at[d, i], xr.at[d, i], xs_send.at[d, i], xs_recv.at[d, i], blend(i, x_peer, y_peer))

    def weight_rows(half, i):
        start = half * width + i * chunk
        return gu[start // slab, at(start % slab, chunk), :]

    def slot_step(d, i):
        @pl.when(i == 0)
        def _():
            lax.fori_loop(d * (quad // 16), (d + 1) * (quad // 16), pointwise, 0)

        spot = at(d * quad, quad)
        cs_out[d, i] = lax.dot_general(
            gg[spot, :], weight_rows(1 - core, i), back, preferred_element_type=f32
        ).astype(bf16)
        cs_copy(d, i).start()
        mine[d, i] = lax.dot_general(gg[spot, :], weight_rows(core, i), back, preferred_element_type=f32)

    def slot_sum(d, i):
        cs_copy(d, i).wait_recv()
        mine[d, i] += cs_in[d, i].astype(f32)

        def both(q):
            return jnp.concatenate(
                [mine[d, i, at(q * capacity, capacity), :], mine[d, i, at((q + 1 + i) * capacity, capacity), :]], axis=0
            ).astype(bf16)

        s_out[d, i] = both(blend(i, 2 - 2 * y, 1 - x))
        ys_copy(d, i).start()
        comb[d, i, pl.ds(0, pair), :] = both(blend(i, 2 * y, x))

    def token_step(d, i):
        ys_copy(d, i).wait_recv()
        here_first = blend(i, x, y)
        t_out[d, i] = lax.dot_general(
            pls[i, d, :, at((1 - here_first) * tok_rows, tok_rows)], comb[d, i], batch0, preferred_element_type=f32
        ).astype(bf16)
        xs_copy(d, i).start()
        t_own[d, i] = lax.dot_general(
            pls[i, d, :, at(here_first * tok_rows, tok_rows)], comb[d, i], batch0, preferred_element_type=f32
        )

    def z_copy(d, i, up):
        if up:
            return remote(z_out.at[d, i], z_in.at[0, d, i], zs_send.at[d, i], zs_recv.at[0, d, i], me + 4)
        return remote(z_out.at[d, i], z_in.at[1, d, i], zs_send.at[d, i], zs_recv.at[1, d, i], me - 4)

    def z_take(d, i, side):
        remote(
            z_out.at[d, i], z_in.at[side, d, i], zs_send.at[d, i], zs_recv.at[side, d, i], x_peer
        ).wait_recv()
        t_own[d, i] += z_in[side, d, i].astype(f32)

    def fin_copy(i):
        spot = grad_tokens_ref.at[:, pl.ds(pl.multiple_of(here + i * chunk, chunk), chunk)]
        return remote(fin.at[i], spot, fin_send.at[i], fin_recv.at[i]), pltpu.make_async_copy(
            fin.at[i], spot, fin_keep.at[i]
        )

    def z_step(d, i):
        xs_copy(d, i).wait_recv()
        t_own[d, i] += xr[d, i].astype(f32)

        @pl.when(jnp.logical_and(d >= z, z > 0))
        def _():
            z_take(d, i, 0)

        @pl.when(jnp.logical_and(d <= z, z < planes - 1))
        def _():
            z_take(d, i, 1)

        @pl.when(d != z)
        def _():
            z_out[d, i] = t_own[d, i].astype(bf16)

        @pl.when(d > z)
        def _():
            z_copy(d, i, True).start()

        @pl.when(d < z)
        def _():
            z_copy(d, i, False).start()

        @pl.when(d == z)
        def _():
            fin[i] = t_own[d, i].astype(bf16)
            out, keep = fin_copy(i)
            out.start()
            keep.start()

    tile = width // 4

    def weight_grad(i):
        half, off, span = i // 4, at((i % 4) * tile, tile), at(i * tile, tile)
        both = lax.dot_general(rows[0, half, :, off], gg[...], batch0, preferred_element_type=f32)
        grad_gate_ref[span, :] = both[:, :hid].astype(bf16)
        grad_up_ref[span, :] = both[:, hid:].astype(bf16)
        grad_down_ref[span, :] = lax.dot_general(
            rows[1, half, :, off], activ[...], batch0, preferred_element_type=f32
        ).astype(bf16)

    def hop_lag(d):
        waits = jnp.logical_or(jnp.logical_and(d > z, upper == 0), jnp.logical_and(d < z, upper == 1))
        return X_LAG + jnp.where(waits, HOP_LAG * near, 0)

    steps = pieces + max(8, Y_LAG + X_LAG + max(0, HOP_LAG * (planes // 2 - 1) - CUTS))

    def ladder(s, carry):
        @pl.when(s < pieces)
        def _():
            slot_step(plane_of(s), s % CUTS)

        @pl.when(jnp.logical_and(s >= 1, s <= 2 * CUTS))
        def _():
            slot_sum(plane_of(s - 1), (s - 1) % CUTS)

        @pl.when(jnp.logical_and(s >= Y_LAG, s < pieces + Y_LAG))
        def _():
            token_step(plane_of(s - Y_LAG), (s - Y_LAG) % CUTS)

        @pl.when(jnp.logical_and(s > 2 * CUTS + S_LAG, s <= pieces + S_LAG))
        def _():
            slot_sum(plane_of(s - 1 - S_LAG), (s - 1 - S_LAG) % CUTS)

        lag = Y_LAG + X_LAG

        def z_try(c, inner):
            d = plane_of(c)

            @pl.when(c + Y_LAG + hop_lag(d) == s)
            def _():
                z_step(d, c % CUTS)

            return inner

        @pl.when(s >= lag)
        def _():
            lax.fori_loop(0, pieces, z_try, 0)

        @pl.when(jnp.logical_and(s >= pieces, s < pieces + 8))
        def _():
            weight_grad(s - pieces)

        return carry

    lax.fori_loop(0, steps, ladder, 0)

    def drain_peers(k, carry):
        target = peer_of(k)
        for w in range(3):
            w_copy(w, target, me).wait_send()
        info_copy(target, me).wait_send()
        return carry

    lax.fori_loop(1, experts, drain_peers, 0)

    def drain_tokens(zs, carry):
        go_up, go_down = forwards(zs)
        for a in range(2):

            @pl.when(go_up)
            def _():
                ag_copy(a, zs, 0).wait_send()

            @pl.when(go_down)
            def _():
                ag_copy(a, zs, 1).wait_send()

            ag_copy(a, zs, 2).wait_send()
            y_copy(a, zs, y).wait_send()
            for ys in range(2):
                core_copy(a, core, zs, ys).wait_send()
        for i in range(CUTS):
            cs_copy(zs, i).wait_send()
            ys_copy(zs, i).wait_send()
            xs_copy(zs, i).wait_send()

            @pl.when(zs > z)
            def _():
                z_copy(zs, i, True).wait_send()

            @pl.when(zs < z)
            def _():
                z_copy(zs, i, False).wait_send()

        return carry

    lax.fori_loop(0, planes, drain_tokens, 0)

    for i in range(CUTS):
        out, keep = fin_copy(i)
        keep.wait()
        out.wait()


def placed_dense(tokens, out_grad, route_ids, route_probs, gate_store, up_store, down_store):
    tok_rows, model_width = tokens.shape
    top_count = route_ids.shape[1]
    experts, _, hid = gate_store.shape
    capacity = 9 * tok_rows * top_count // (8 * experts)
    slots, width, planes = experts * capacity, model_width // 2, experts // 4
    pair, quad, slab = 2 * capacity, 4 * capacity, model_width // planes
    chunk = width // CUTS
    vmem, dma = pltpu.VMEM, pltpu.SemaphoreType.DMA
    anywhere, on_chip = pl.BlockSpec(memory_space=pl.ANY), pl.BlockSpec(memory_space=pltpu.VMEM)
    scratch = [
        vmem((planes, 8, tok_rows), f32),
        vmem((experts, 8, tok_rows), f32),
        vmem((planes, slab, 2 * hid), bf16),
        vmem((planes, slab, hid), bf16),
        vmem((2, planes, 2 * tok_rows, width), bf16),
        vmem((2, planes, pair, width), bf16),
        vmem((2, 2, slots, width), bf16),
        vmem((2, planes, quad, 2 * tok_rows), bf16),
        vmem((slots, 2 * hid), f32),
        vmem((slots, hid), f32),
        vmem((slots, hid), bf16),
        vmem((slots, 2 * hid), bf16),
        vmem((planes, CUTS, quad, chunk), f32),
        vmem((planes, CUTS, quad, chunk), bf16),
        vmem((planes, CUTS, quad, chunk), bf16),
        vmem((planes, CUTS, quad, chunk), bf16),
        vmem((planes, CUTS, pair, chunk), bf16),
        vmem((planes, CUTS, tok_rows, chunk), f32),
        vmem((planes, CUTS, tok_rows, chunk), bf16),
        vmem((planes, CUTS, tok_rows, chunk), bf16),
        vmem((planes, CUTS, tok_rows, chunk), bf16),
        vmem((2, planes, CUTS, tok_rows, chunk), bf16),
        vmem((CUTS, tok_rows, chunk), bf16),
        dma((2,)), dma((experts,)), dma((experts,)), dma((3, experts)), dma((3, experts)), dma((3,)),
        dma((2, planes)), dma((2, planes)), dma((2, planes)), dma((2, planes)), dma((2, planes)),
        dma((2, planes)), dma((2, planes)), dma((2, 2 * planes)), dma((2, 2 * planes)),
        dma((planes, CUTS)), dma((planes, CUTS)), dma((planes, CUTS)), dma((planes, CUTS)),
        dma((planes, CUTS)), dma((planes, CUTS)), dma((planes, CUTS)), dma((2, planes, CUTS)),
        dma((CUTS,)), dma((CUTS,)), dma((CUTS,)),
    ]
    grad = pltpu.VMEM((model_width, hid), bf16)
    outs = pl.pallas_call(
        functools.partial(dense_kernel, experts, capacity),
        out_shape=(grad, grad, grad, pltpu.VMEM((tok_rows, model_width), bf16)),
        in_specs=[on_chip, on_chip] + [anywhere] * 5,
        out_specs=(on_chip,) * 4,
        scratch_shapes=scratch,
        compiler_params=pltpu.CompilerParams(
            collective_id=0, has_side_effects=True, vmem_limit_bytes=VMEM_BYTES
        ),
    )(route_ids.T, route_probs.T, tokens, out_grad, gate_store, up_store, down_store)
    return (outs[0][None], outs[1][None], outs[2][None], outs[3])


def placed(tokens, out_grad, route_ids, route_probs, gate_store, up_store, down_store):
    experts, top_count = lax.axis_size("expert"), route_ids.shape[1]
    capacity = 9 * tokens.shape[0] * top_count // (8 * experts)
    dense = 4 * top_count >= experts and experts % 8 == 0 and capacity % 8 == 0
    body = placed_dense if dense else placed_sparse
    return body(tokens, out_grad, route_ids, route_probs, gate_store, up_store, down_store)


def solution(mesh):
    return jax.shard_map(
        placed,
        mesh=mesh,
        in_specs=(
            P("expert", None),
            P("expert", None),
            P("expert", None),
            P("expert", None),
            P(None, "expert", "dp"),
            P(None, "expert", "dp"),
            P(None, "expert", "dp"),
        ),
        out_specs=(
            P("expert", None, "dp"),
            P("expert", None, "dp"),
            P("expert", None, "dp"),
            P("expert", None),
        ),
        check_vma=False,
    )
```

```python
import functools

import jax
import jax.numpy as jnp
from jax import lax
from jax.experimental import pallas as pl
from jax.experimental.pallas import tpu as pltpu
from jax.sharding import PartitionSpec as P


def joined(own, other):
    first = lax.axis_index("dp") == 0
    return jnp.where(first, jnp.concatenate([own, other], -1), jnp.concatenate([other, own], -1))


def swapped(part):
    return lax.ppermute(part, "dp", [(0, 1), (1, 0)])


def placed_sparse(tokens, out_grad, route_ids, route_probs, gate_store, up_store, down_store):
    tok_rows, model_width = tokens.shape
    top_count = route_ids.shape[1]
    experts = lax.axis_size("expert")
    capacity = max(2, 9 * tok_rows * top_count // (8 * experts))
    slots = experts * capacity
    width = model_width // 2
    here = lax.axis_index("dp") * width
    there = width - here
    f32, bf16 = jnp.float32, jnp.bfloat16

    chosen = route_ids[:, :, None] == jnp.arange(experts, dtype=jnp.int32)[None, None, :]
    weight = jnp.sum(jnp.where(chosen, route_probs[:, :, None], 0.0), axis=1)
    named = jnp.any(chosen, axis=1)
    earlier = jnp.arange(tok_rows)[:, None] > jnp.arange(tok_rows)[None, :]
    rank = jnp.dot(earlier.astype(bf16), named.astype(bf16), preferred_element_type=f32)
    rank = jnp.where(named, rank, -1.0)
    hit = rank.T[:, None, :] == jnp.arange(capacity, dtype=f32)[None, :, None]
    slot_prob = jnp.sum(jnp.where(hit, weight.T[:, None, :], 0.0), axis=2)
    place = hit.astype(bf16).reshape(slots, tok_rows)

    x_part = jnp.dot(
        place, lax.dynamic_slice_in_dim(tokens, here, width, 1), preferred_element_type=f32
    ).astype(bf16)
    dy_part = (
        jnp.dot(place, lax.dynamic_slice_in_dim(out_grad, here, width, 1), preferred_element_type=f32)
        * slot_prob.reshape(slots, 1)
    ).astype(bf16)

    def exchange(a):
        return lax.all_to_all(a, "expert", split_axis=0, concat_axis=0, tiled=True)

    def panel(store):
        return lax.all_to_all(store, "expert", split_axis=0, concat_axis=1, tiled=True)[0]

    x_own = exchange(x_part.reshape(experts, capacity, width)).reshape(slots, width)
    gate_panel = panel(gate_store)
    up_panel = panel(up_store)
    dy_own = exchange(dy_part.reshape(experts, capacity, width)).reshape(slots, width)
    down_panel = panel(down_store)
    rows_in = joined(x_own, swapped(x_own))
    dy_rows = joined(dy_own, swapped(dy_own))
    gate_pre = jnp.dot(rows_in, gate_panel, preferred_element_type=f32)
    up_pre = jnp.dot(rows_in, up_panel, preferred_element_type=f32)
    sig = jax.nn.sigmoid(gate_pre)
    activation = (gate_pre * sig * up_pre).astype(bf16)
    act_grad = jnp.dot(dy_rows, down_panel, preferred_element_type=f32)
    up_grad = (act_grad * gate_pre * sig).astype(bf16)
    gate_grad = (act_grad * up_pre * sig * (1.0 + gate_pre * (1.0 - sig))).astype(bf16)
    back = (((1,), (1,)), ((), ()))

    def slot_part(start):
        rows = [lax.dynamic_slice_in_dim(w, start, width, 0) for w in (gate_panel, up_panel)]
        return lax.dot_general(gate_grad, rows[0], back, preferred_element_type=f32) + lax.dot_general(
            up_grad, rows[1], back, preferred_element_type=f32
        )

    arrived = swapped(slot_part(there).astype(bf16))
    summed = (slot_part(here) + arrived.astype(f32)).astype(bf16)
    returned = exchange(summed.reshape(experts, capacity, width)).reshape(slots, width)
    share = lax.dot_general(place, returned, (((0,), (0,)), ((), ())), preferred_element_type=f32).astype(bf16)
    grad_tokens = joined(share, swapped(share))
    outer = (((0,), (0,)), ((), ()))
    grad_down = lax.dot_general(dy_rows, activation, outer, preferred_element_type=f32).astype(bf16)
    grad_gate = lax.dot_general(rows_in, gate_grad, outer, preferred_element_type=f32).astype(bf16)
    grad_up = lax.dot_general(rows_in, up_grad, outer, preferred_element_type=f32).astype(bf16)
    return (grad_gate[None], grad_up[None], grad_down[None], grad_tokens)


f32, bf16 = jnp.float32, jnp.bfloat16
MESH = pl.DeviceIdType.MESH
CUTS = 2
S_LAG = 3
FIRST, PACE = 4, 5
VMEM_BYTES = 56000 * 1024
Y_LAG, X_LAG, HOP_LAG = 6, 2, 2


def dense_kernel(
    experts, capacity,
    ids_ref, probs_ref, x_ref, dy_ref, gate_ref, up_ref, down_ref,
    grad_gate_ref, grad_up_ref, grad_down_ref, grad_tokens_ref,
    info, info_all, gu, dn, tok, nbr_out, rows, pls, pre, act, activ, gg,
    mine, cs_out, cs_in, comb, s_out, t_own, t_out, xr, z_out, z_in, fin,
    local_sem, info_send, info_recv, w_send, w_recv, w_own,
    ag_up, ag_down, ag_zr, ag_xs, ag_xr, y_send, y_recv, c_send, c_recv,
    cs_send, cs_recv, ys_send, ys_recv, xs_send, xs_recv, zs_send, zs_recv, fin_send, fin_recv, fin_keep,
):
    me, core = lax.axis_index("expert"), lax.axis_index("dp")
    planes = experts // 4
    z, y, x = me // 4, (me // 2) % 2, me % 2
    x_peer, y_peer = me + 1 - 2 * x, me + 2 - 4 * y
    tok_rows, model_width = x_ref.shape
    width = model_width // 2
    hid = gate_ref.shape[2]
    pair = 2 * capacity
    quad = 4 * capacity
    slots = experts * capacity
    slab = model_width // planes
    here = pl.multiple_of(core * width, width)
    batch0 = (((0,), (0,)), ((), ()))

    def remote(src, dst, send, recv, expert=None):
        target = {"dp": 1 - core} if expert is None else {"expert": expert}
        return pltpu.make_async_remote_copy(
            src_ref=src, dst_ref=dst, send_sem=send, recv_sem=recv, device_id=target, device_id_type=MESH
        )

    def at(start, size):
        return pl.ds(pl.multiple_of(start, size), size)

    def peer_of(k):
        return lax.rem(me + k, experts)

    barrier = pltpu.get_barrier_semaphore()

    def greet(k, carry):
        pl.semaphore_signal(barrier, inc=1, device_id={"expert": peer_of(k)}, device_id_type=MESH)
        return carry

    lax.fori_loop(1, experts, greet, 0)
    pl.semaphore_signal(barrier, inc=1, device_id={"dp": 1 - core}, device_id_type=MESH)

    own_copies = []
    for a, ref in enumerate((x_ref, dy_ref)):
        own_copies.append(
            pltpu.make_async_copy(ref.at[:, pl.ds(here, width)], tok.at[a, z, at(x * tok_rows, tok_rows), :], local_sem.at[a])
        )
    own_rows = at((me % 4) * tok_rows, tok_rows)
    own_panels = [
        pltpu.make_async_copy(gate_ref.at[me], gu.at[z, own_rows, pl.ds(0, hid)], w_own.at[0]),
        pltpu.make_async_copy(up_ref.at[me], gu.at[z, own_rows, pl.ds(hid, hid)], w_own.at[1]),
        pltpu.make_async_copy(down_ref.at[me], dn.at[z, own_rows, :], w_own.at[2]),
    ]
    for copy in own_copies:
        copy.start()
    for copy in own_panels:
        copy.start()
    ids, probs = ids_ref[...], probs_ref[...]
    named_by = lax.broadcasted_iota(jnp.int32, (experts,) + ids.shape, 0) == ids[None, :, :]
    weight = jnp.sum(jnp.where(named_by, probs[None, :, :], 0.0), axis=1)
    named = jnp.sum(jnp.where(named_by, 1.0, 0.0), axis=1)
    before = lax.broadcasted_iota(jnp.int32, (tok_rows, tok_rows), 0) < lax.broadcasted_iota(
        jnp.int32, (tok_rows, tok_rows), 1
    )
    rank = jnp.dot(named.astype(bf16), jnp.where(before, 1.0, 0.0).astype(bf16), preferred_element_type=f32)
    rank = jnp.where(named > 0.5, rank, -4.0 * capacity)
    for q in range(4):
        for p in range(planes):
            info[p, pl.ds(2 * q, 1), :] = rank[4 * p + q : 4 * p + q + 1, :]
            info[p, pl.ds(2 * q + 1, 1), :] = weight[4 * p + q : 4 * p + q + 1, :]
    info_all[me] = info[z]

    pl.semaphore_wait(barrier, experts)

    def w_copy(w, target, owner):
        spot = at((owner % 4) * tok_rows, tok_rows)
        if w == 0:
            src, dst = gate_ref, gu.at[owner // 4, spot, pl.ds(0, hid)]
        elif w == 1:
            src, dst = up_ref, gu.at[owner // 4, spot, pl.ds(hid, hid)]
        else:
            src, dst = down_ref, dn.at[owner // 4, spot, :]
        return remote(src.at[target], dst, w_send.at[w, target], w_recv.at[w, owner], target)

    others = experts - 1

    def start_weights(first, last):
        for w in range(3):

            def body(n, carry):
                w_copy(w, peer_of(n + 1 - w * others), me).start()
                return carry

            lax.fori_loop(jnp.maximum(first, w * others), jnp.minimum(last, (w + 1) * others), body, 0)

    def wait_panel(w, source):
        w_copy(w, source, source).wait_recv()

    def tok_block(a, zs, xs):
        return tok.at[a, zs, at(xs * tok_rows, tok_rows), :]

    def ag_copy(a, zs, direction):
        block = tok_block(a, zs, x)
        if direction == 0:
            return remote(block, block, ag_up.at[a, zs], ag_zr.at[a, zs], me + 4)
        if direction == 1:
            return remote(block, block, ag_down.at[a, zs], ag_zr.at[a, zs], me - 4)
        return remote(block, block, ag_xs.at[a, zs], ag_xr.at[a, zs], x_peer)

    def walk(t):
        return z + ((t + 1) // 2) * (1 - 2 * (t % 2))

    def inside(zs):
        return jnp.logical_and(zs >= 0, zs < planes)

    def forwards(zs):
        return (
            jnp.logical_and(zs <= z, z < planes - 1),
            jnp.logical_and(zs >= z, z > 0),
        )

    def send_block(a, zs):
        go_up, go_down = forwards(zs)

        @pl.when(go_up)
        def _():
            ag_copy(a, zs, 0).start()

        @pl.when(go_down)
        def _():
            ag_copy(a, zs, 1).start()

        ag_copy(a, zs, 2).start()

    for a in range(2):
        own_copies[a].wait()
        send_block(a, z)

    def info_copy(target, owner):
        return remote(
            info.at[target // 4], info_all.at[owner], info_send.at[target], info_recv.at[owner], target
        )

    def send_info(k, carry):
        info_copy(peer_of(k), me).start()
        return carry

    lax.fori_loop(1, experts, send_info, 0)
    start_weights(0, FIRST * others // 15)

    def wait_info(k, carry):
        source = peer_of(k)
        info_copy(source, source).wait_recv()
        return carry

    lax.fori_loop(1, experts, wait_info, 0)

    def pair_rows(zs, ys):
        return at((2 * zs + ys) * pair, pair)

    def places(first, second, expert_index):
        lines = pl.ds(2 * expert_index, 2)
        one, two = info_all[first, lines, :], info_all[second, lines, :]
        ranks = jnp.concatenate([one[0:1, :], two[0:1, :] + float(capacity)], axis=1)
        probs = jnp.concatenate([one[1:2, :], two[1:2, :]], axis=1)
        hit = ranks == lax.broadcasted_iota(jnp.int32, (pair, 2 * tok_rows), 0).astype(f32)
        prob = jnp.sum(jnp.where(hit, probs, 0.0), axis=1, keepdims=True)
        return jnp.where(hit, 1.0, 0.0).astype(bf16), prob

    def y_copy(a, zs, ys):
        return remote(
            nbr_out.at[a, zs], rows.at[a, core, pair_rows(zs, ys), :], y_send.at[a, zs], y_recv.at[a, zs], y_peer
        )

    def core_copy(a, half, zs, ys):
        block = rows.at[a, half, pair_rows(zs, ys), :]
        return remote(block, block, c_send.at[a, 2 * zs + ys], c_recv.at[a, 2 * zs + ys])

    mine_q = me % 4
    peer_q = y_peer % 4

    def gather(a, zs):
        first = 4 * zs + 2 * y
        own_place, own_prob = places(first, first + 1, mine_q)
        nbr_place, nbr_prob = places(first, first + 1, peer_q)
        if a == 0:
            pls[0, zs, pl.ds(0, pair), :] = own_place
            pls[0, zs, pl.ds(pair, pair), :] = nbr_place
            for k, q in enumerate((mine_q, x_peer % 4)):
                pls[1, zs, pl.ds(k * pair, pair), :] = places(4 * zs + x, 4 * zs + 2 + x, q)[0]
        ag_copy(a, zs, 2).wait_recv()
        lent = jnp.dot(nbr_place, tok[a, zs], preferred_element_type=f32)
        if a == 1:
            lent = lent * nbr_prob
        nbr_out[a, zs] = lent.astype(bf16)
        y_copy(a, zs, y).start()
        got = jnp.dot(own_place, tok[a, zs], preferred_element_type=f32)
        if a == 1:
            got = got * own_prob
        rows[a, core, pair_rows(zs, y), :] = got.astype(bf16)
        core_copy(a, core, zs, y).start()

    hops = 2 * planes - 2

    def spread(t, carry):
        zs, ready = walk(t), walk(t - 1)

        @pl.when(jnp.logical_and(t <= hops, inside(zs)))
        def _():
            for a in range(2):
                block = tok_block(a, zs, x)
                remote(block, block, ag_up.at[a, zs], ag_zr.at[a, zs], x_peer).wait_recv()
                send_block(a, zs)

        @pl.when(inside(ready))
        def _():
            for a in range(2):
                gather(a, ready)

        start_weights((FIRST + PACE * (t - 1)) * others // 15, (FIRST + PACE * t) * others // 15)
        return carry

    lax.fori_loop(1, hops + 2, spread, 0)
    start_weights((FIRST + PACE * (hops + 1)) * others // 15, 3 * others)

    def pass_on(a, zs):
        y_copy(a, zs, 1 - y).wait_recv()
        core_copy(a, core, zs, 1 - y).start()

    def take_core(a, zs):
        for ys in range(2):
            core_copy(a, 1 - core, zs, ys).wait_recv()

    for w in range(2):
        own_panels[w].wait()

        def wait_gu(k, carry):
            wait_panel(w, peer_of(k))
            return carry

        lax.fori_loop(1, experts, wait_gu, 0)

    def slab_of(a, g, spot):
        half, off = (g * slab) // width, (g * slab) % width
        return rows[a, half, spot, pl.ds(off, slab)]

    def forward(m):
        spot = at(m * quad, quad)
        total = jnp.dot(slab_of(0, 0, spot), gu[0], preferred_element_type=f32)
        for g in range(1, planes):
            total += jnp.dot(slab_of(0, g, spot), gu[g], preferred_element_type=f32)
        pre[spot, :] = total

    def first_half(t, carry):
        zs, ready = walk(t), walk(t - 1)

        @pl.when(jnp.logical_and(t <= hops, inside(zs)))
        def _():
            for a in range(2):
                pass_on(a, zs)

        @pl.when(jnp.logical_and(t >= 1, inside(ready)))
        def _():
            take_core(0, ready)
            forward(ready)

        return carry

    lax.fori_loop(0, hops + 2, first_half, 0)

    def settle(zs, carry):
        take_core(1, zs)
        return carry

    lax.fori_loop(0, planes, settle, 0)
    own_panels[2].wait()
    upper = (2 * z) // planes
    for turn in range(planes):
        g = turn + upper * (planes - 1 - 2 * turn)
        for q in range(4):
            source = 4 * g + q

            @pl.when(source != me)
            def _():
                wait_panel(2, source)

        def backward(m, carry):
            spot = at(m * quad, quad)
            part = jnp.dot(rows[1, (g * slab) // width, spot, at((g * slab) % width, slab)], dn[g], preferred_element_type=f32)
            if turn == 0:
                act[spot, :] = part
            else:
                act[spot, :] += part
            return carry

        lax.fori_loop(0, planes, backward, 0)

    def pointwise(m, carry):
        spot = at(m * 16, 16)
        gate_pre, up_pre, act_grad = pre[spot, pl.ds(0, hid)], pre[spot, pl.ds(hid, hid)], act[spot, :]
        sig = jax.nn.sigmoid(gate_pre)
        activ[spot, :] = (gate_pre * sig * up_pre).astype(bf16)
        gg[spot, pl.ds(0, hid)] = (act_grad * up_pre * sig * (1.0 + gate_pre * (1.0 - sig))).astype(bf16)
        gg[spot, pl.ds(hid, hid)] = (act_grad * gate_pre * sig).astype(bf16)
        return carry

    back = (((1,), (1,)), ((), ()))
    chunk = width // CUTS
    pieces = planes * CUTS

    near = z + upper * (planes - 1 - 2 * z)
    far_count = planes - 1 - 2 * near

    def plane_of(c):
        i = c // CUTS
        j = i - far_count
        close = (j + planes) // planes
        swing = (2 * near - j // 2) * (1 - j % 2) + (j // 2) * (j % 2)
        d = close * swing + (1 - close) * (planes - 1 - i)
        return d + upper * (planes - 1 - 2 * d)

    def blend(i, first, second):
        return first + (second - first) * i

    def cs_copy(d, i):
        return remote(cs_out.at[d, i], cs_in.at[d, i], cs_send.at[d, i], cs_recv.at[d, i])

    def ys_copy(d, i):
        return remote(
            s_out.at[d, i], comb.at[d, i, pl.ds(pair, pair), :], ys_send.at[d, i], ys_recv.at[d, i], blend(i, y_peer, x_peer)
        )

    def xs_copy(d, i):
        return remote(t_out.at[d, i], xr.at[d, i], xs_send.at[d, i], xs_recv.at[d, i], blend(i, x_peer, y_peer))

    def weight_rows(half, i):
        start = half * width + i * chunk
        return gu[start // slab, at(start % slab, chunk), :]

    def slot_step(d, i):
        @pl.when(i == 0)
        def _():
            lax.fori_loop(d * (quad // 16), (d + 1) * (quad // 16), pointwise, 0)

        spot = at(d * quad, quad)
        cs_out[d, i] = lax.dot_general(
            gg[spot, :], weight_rows(1 - core, i), back, preferred_element_type=f32
        ).astype(bf16)
        cs_copy(d, i).start()
        mine[d, i] = lax.dot_general(gg[spot, :], weight_rows(core, i), back, preferred_element_type=f32)

    def slot_sum(d, i):
        cs_copy(d, i).wait_recv()
        mine[d, i] += cs_in[d, i].astype(f32)

        def both(q):
            return jnp.concatenate(
                [mine[d, i, at(q * capacity, capacity), :], mine[d, i, at((q + 1 + i) * capacity, capacity), :]], axis=0
            ).astype(bf16)

        s_out[d, i] = both(blend(i, 2 - 2 * y, 1 - x))
        ys_copy(d, i).start()
        comb[d, i, pl.ds(0, pair), :] = both(blend(i, 2 * y, x))

    def token_step(d, i):
        ys_copy(d, i).wait_recv()
        here_first = blend(i, x, y)
        t_out[d, i] = lax.dot_general(
            pls[i, d, :, at((1 - here_first) * tok_rows, tok_rows)], comb[d, i], batch0, preferred_element_type=f32
        ).astype(bf16)
        xs_copy(d, i).start()
        t_own[d, i] = lax.dot_general(
            pls[i, d, :, at(here_first * tok_rows, tok_rows)], comb[d, i], batch0, preferred_element_type=f32
        )

    def z_copy(d, i, up):
        if up:
            return remote(z_out.at[d, i], z_in.at[0, d, i], zs_send.at[d, i], zs_recv.at[0, d, i], me + 4)
        return remote(z_out.at[d, i], z_in.at[1, d, i], zs_send.at[d, i], zs_recv.at[1, d, i], me - 4)

    def z_take(d, i, side):
        remote(
            z_out.at[d, i], z_in.at[side, d, i], zs_send.at[d, i], zs_recv.at[side, d, i], x_peer
        ).wait_recv()
        t_own[d, i] += z_in[side, d, i].astype(f32)

    def fin_copy(i):
        spot = grad_tokens_ref.at[:, pl.ds(pl.multiple_of(here + i * chunk, chunk), chunk)]
        return remote(fin.at[i], spot, fin_send.at[i], fin_recv.at[i]), pltpu.make_async_copy(
            fin.at[i], spot, fin_keep.at[i]
        )

    def z_step(d, i):
        xs_copy(d, i).wait_recv()
        t_own[d, i] += xr[d, i].astype(f32)

        @pl.when(jnp.logical_and(d >= z, z > 0))
        def _():
            z_take(d, i, 0)

        @pl.when(jnp.logical_and(d <= z, z < planes - 1))
        def _():
            z_take(d, i, 1)

        @pl.when(d != z)
        def _():
            z_out[d, i] = t_own[d, i].astype(bf16)

        @pl.when(d > z)
        def _():
            z_copy(d, i, True).start()

        @pl.when(d < z)
        def _():
            z_copy(d, i, False).start()

        @pl.when(d == z)
        def _():
            fin[i] = t_own[d, i].astype(bf16)
            out, keep = fin_copy(i)
            out.start()
            keep.start()

    tile = width // 4

    def weight_grad(i):
        half, off, span = i // 4, at((i % 4) * tile, tile), at(i * tile, tile)
        both = lax.dot_general(rows[0, half, :, off], gg[...], batch0, preferred_element_type=f32)
        grad_gate_ref[span, :] = both[:, :hid].astype(bf16)
        grad_up_ref[span, :] = both[:, hid:].astype(bf16)
        grad_down_ref[span, :] = lax.dot_general(
            rows[1, half, :, off], activ[...], batch0, preferred_element_type=f32
        ).astype(bf16)

    def hop_lag(d):
        waits = jnp.logical_or(jnp.logical_and(d > z, upper == 0), jnp.logical_and(d < z, upper == 1))
        return X_LAG + jnp.where(waits, HOP_LAG * near, 0)

    steps = pieces + max(8, Y_LAG + X_LAG + max(0, HOP_LAG * (planes // 2 - 1) - CUTS))

    def ladder(s, carry):
        @pl.when(s < pieces)
        def _():
            slot_step(plane_of(s), s % CUTS)

        @pl.when(jnp.logical_and(s >= 1, s <= 2 * CUTS))
        def _():
            slot_sum(plane_of(s - 1), (s - 1) % CUTS)

        @pl.when(jnp.logical_and(s >= Y_LAG, s < pieces + Y_LAG))
        def _():
            token_step(plane_of(s - Y_LAG), (s - Y_LAG) % CUTS)

        @pl.when(jnp.logical_and(s > 2 * CUTS + S_LAG, s <= pieces + S_LAG))
        def _():
            slot_sum(plane_of(s - 1 - S_LAG), (s - 1 - S_LAG) % CUTS)

        lag = Y_LAG + X_LAG

        def z_try(c, inner):
            d = plane_of(c)

            @pl.when(c + Y_LAG + hop_lag(d) == s)
            def _():
                z_step(d, c % CUTS)

            return inner

        @pl.when(s >= lag)
        def _():
            lax.fori_loop(0, pieces, z_try, 0)

        @pl.when(jnp.logical_and(s >= pieces, s < pieces + 8))
        def _():
            weight_grad(s - pieces)

        return carry

    lax.fori_loop(0, steps, ladder, 0)

    def drain_peers(k, carry):
        target = peer_of(k)
        for w in range(3):
            w_copy(w, target, me).wait_send()
        info_copy(target, me).wait_send()
        return carry

    lax.fori_loop(1, experts, drain_peers, 0)

    def drain_tokens(zs, carry):
        go_up, go_down = forwards(zs)
        for a in range(2):

            @pl.when(go_up)
            def _():
                ag_copy(a, zs, 0).wait_send()

            @pl.when(go_down)
            def _():
                ag_copy(a, zs, 1).wait_send()

            ag_copy(a, zs, 2).wait_send()
            y_copy(a, zs, y).wait_send()
            for ys in range(2):
                core_copy(a, core, zs, ys).wait_send()
        for i in range(CUTS):
            cs_copy(zs, i).wait_send()
            ys_copy(zs, i).wait_send()
            xs_copy(zs, i).wait_send()

            @pl.when(zs > z)
            def _():
                z_copy(zs, i, True).wait_send()

            @pl.when(zs < z)
            def _():
                z_copy(zs, i, False).wait_send()

        return carry

    lax.fori_loop(0, planes, drain_tokens, 0)

    for i in range(CUTS):
        out, keep = fin_copy(i)
        keep.wait()
        out.wait()


def placed_dense(tokens, out_grad, route_ids, route_probs, gate_store, up_store, down_store):
    tok_rows, model_width = tokens.shape
    top_count = route_ids.shape[1]
    experts, _, hid = gate_store.shape
    capacity = 9 * tok_rows * top_count // (8 * experts)
    slots, width, planes = experts * capacity, model_width // 2, experts // 4
    pair, quad, slab = 2 * capacity, 4 * capacity, model_width // planes
    chunk = width // CUTS
    vmem, dma = pltpu.VMEM, pltpu.SemaphoreType.DMA
    anywhere, on_chip = pl.BlockSpec(memory_space=pl.ANY), pl.BlockSpec(memory_space=pltpu.VMEM)
    scratch = [
        vmem((planes, 8, tok_rows), f32),
        vmem((experts, 8, tok_rows), f32),
        vmem((planes, slab, 2 * hid), bf16),
        vmem((planes, slab, hid), bf16),
        vmem((2, planes, 2 * tok_rows, width), bf16),
        vmem((2, planes, pair, width), bf16),
        vmem((2, 2, slots, width), bf16),
        vmem((2, planes, quad, 2 * tok_rows), bf16),
        vmem((slots, 2 * hid), f32),
        vmem((slots, hid), f32),
        vmem((slots, hid), bf16),
        vmem((slots, 2 * hid), bf16),
        vmem((planes, CUTS, quad, chunk), f32),
        vmem((planes, CUTS, quad, chunk), bf16),
        vmem((planes, CUTS, quad, chunk), bf16),
        vmem((planes, CUTS, quad, chunk), bf16),
        vmem((planes, CUTS, pair, chunk), bf16),
        vmem((planes, CUTS, tok_rows, chunk), f32),
        vmem((planes, CUTS, tok_rows, chunk), bf16),
        vmem((planes, CUTS, tok_rows, chunk), bf16),
        vmem((planes, CUTS, tok_rows, chunk), bf16),
        vmem((2, planes, CUTS, tok_rows, chunk), bf16),
        vmem((CUTS, tok_rows, chunk), bf16),
        dma((2,)), dma((experts,)), dma((experts,)), dma((3, experts)), dma((3, experts)), dma((3,)),
        dma((2, planes)), dma((2, planes)), dma((2, planes)), dma((2, planes)), dma((2, planes)),
        dma((2, planes)), dma((2, planes)), dma((2, 2 * planes)), dma((2, 2 * planes)),
        dma((planes, CUTS)), dma((planes, CUTS)), dma((planes, CUTS)), dma((planes, CUTS)),
        dma((planes, CUTS)), dma((planes, CUTS)), dma((planes, CUTS)), dma((2, planes, CUTS)),
        dma((CUTS,)), dma((CUTS,)), dma((CUTS,)),
    ]
    grad = pltpu.VMEM((model_width, hid), bf16)
    outs = pl.pallas_call(
        functools.partial(dense_kernel, experts, capacity),
        out_shape=(grad, grad, grad, pltpu.VMEM((tok_rows, model_width), bf16)),
        in_specs=[on_chip, on_chip] + [anywhere] * 5,
        out_specs=(on_chip,) * 4,
        scratch_shapes=scratch,
        compiler_params=pltpu.CompilerParams(
            collective_id=0, has_side_effects=True, vmem_limit_bytes=VMEM_BYTES
        ),
    )(route_ids.T, route_probs.T, tokens, out_grad, gate_store, up_store, down_store)
    return (outs[0][None], outs[1][None], outs[2][None], outs[3])


def placed(tokens, out_grad, route_ids, route_probs, gate_store, up_store, down_store):
    experts, top_count = lax.axis_size("expert"), route_ids.shape[1]
    capacity = 9 * tokens.shape[0] * top_count // (8 * experts)
    dense = 4 * top_count >= experts and experts % 8 == 0 and capacity % 8 == 0
    body = placed_dense if dense else placed_sparse
    return body(tokens, out_grad, route_ids, route_probs, gate_store, up_store, down_store)


def solution(mesh):
    return jax.shard_map(
        placed,
        mesh=mesh,
        in_specs=(
            P("expert", None),
            P("expert", None),
            P("expert", None),
            P("expert", None),
            P(None, "expert", "dp"),
            P(None, "expert", "dp"),
            P(None, "expert", "dp"),
        ),
        out_specs=(
            P("expert", None, "dp"),
            P("expert", None, "dp"),
            P("expert", None, "dp"),
            P("expert", None),
        ),
        check_vma=False,
    )
```
